256 devices in a mesh: blk: 2 (over y_hi), theta: 32 (over x, z), radial: 4 (over y_lo, core).
Axes of the slice: x: 4, y: 4 (y_hi: 2, y_lo: 2; y = y_hi * 2 + y_lo), z: 8, core: 2. Of those that a mesh axis runs over, the one named last changes fastest.
Arguments:
- base_state: float32 [5, 12, 32, 32768], P(None, 'blk', 'radial', 'theta'), may hold values from -4 to 12, as said below
- section_state: float32 [5, 12, 32, 32768], P(None, 'blk', 'radial', 'theta'), may hold values from -4 to 12, as said below
- rotor_step: int32 [1], replicated, may hold values from 4096 to 131071
Outputs:
- next_state: float32 [5, 12, 32, 32768], P(None, 'blk', 'radial', 'theta')
The draws below stay inside these ranges and needn't reach their ends.
Inputs may be any that keep to these rules, and one draw needn't show every extreme that they name: `base_state`: density between 0.5 and 2, pressure between 0.5 and 2, every velocity component under 2 in magnitude. `section_state`: density between 0.5 and 2, pressure between 0.5 and 2, every velocity component under 2 in magnitude.
All inputs are finite; a program needn't handle non-finite values.
Results may differ from the reference program's by a relative error of at most 0.0003.
Values sent between devices are 32-bit elements; how exact they have to be, the bound alone decides.
A program may use at most 64 MiB of HBM per device.

```python
import math
import jax
import jax.numpy as jnp
from jax import lax

ZD = 6
TD = 1024
NZ = 12
NR = 32
NT = 32768


gamma_ratio = 1.4


def physical_state(key):
    density_key, velocity_key, pressure_key = jax.random.split(key, 3)
    shape = (NZ, NR, NT)
    density = jnp.exp(jax.random.uniform(density_key, shape, jnp.float32, math.log(0.5), math.log(2.0)))
    velocity = jnp.clip(0.5 * jax.random.normal(velocity_key, (3, NZ, NR, NT), jnp.float32), -1.5, 1.5)
    pressure = jnp.exp(jax.random.uniform(pressure_key, shape, jnp.float32, math.log(0.5), math.log(2.0)))
    energy = pressure / (gamma_ratio - 1.0) + 0.5 * density * jnp.sum(jnp.square(velocity), axis=0)
    return jnp.concatenate([density[None], density[None] * velocity, energy[None]], axis=0)


def draw_base_state(key, part):
    return physical_state(jax.random.fold_in(key, 11))


def draw_section_state(key, part):
    return physical_state(jax.random.fold_in(key, 23))


def setup_inputs(seed: int = 0) -> dict:
    key_list = jax.random.split(jax.random.key(seed), 4)
    base_state = draw_base_state(jax.random.fold_in(key_list[3], 71), 0)
    section_state = draw_section_state(jax.random.fold_in(key_list[3], 71), 0)
    rotor_step = jax.random.randint(key_list[2], (1,), 4 * TD, 4 * NT).astype(jnp.int32)
    return {"base_state": base_state, "section_state": section_state, "rotor_step": rotor_step}


gamma_ratio = 1.4
weno_epsilon = 1e-06
step_ratio = 0.12

def pressure_of(state):
    kinetic = 0.5 * (jnp.square(state[1]) + jnp.square(state[2]) + jnp.square(state[3])) / state[0]
    return (gamma_ratio - 1.0) * (state[4] - kinetic)

def euler_flux(state, normal):
    pressure = pressure_of(state)
    velocity = state[normal] / state[0]
    flux = state * velocity[None]
    flux = flux.at[normal].add(pressure)
    flux = flux.at[4].add(pressure * velocity)
    return flux

def wave_speed(state, normal):
    pressure = pressure_of(state)
    return jnp.abs(state[normal] / state[0]) + jnp.sqrt(gamma_ratio * pressure / state[0])

def weno_side(far_left, left_cell, centre, right_cell, far_right):
    smooth_low = 13.0 / 12.0 * jnp.square(far_left - 2.0 * left_cell + centre) + 0.25 * jnp.square(far_left - 4.0 * left_cell + 3.0 * centre)
    smooth_mid = 13.0 / 12.0 * jnp.square(left_cell - 2.0 * centre + right_cell) + 0.25 * jnp.square(left_cell - right_cell)
    smooth_high = 13.0 / 12.0 * jnp.square(centre - 2.0 * right_cell + far_right) + 0.25 * jnp.square(3.0 * centre - 4.0 * right_cell + far_right)
    weight_low = 0.1 / jnp.square(weno_epsilon + smooth_low)
    weight_mid = 0.6 / jnp.square(weno_epsilon + smooth_mid)
    weight_high = 0.3 / jnp.square(weno_epsilon + smooth_high)
    guess_low = (2.0 * far_left - 7.0 * left_cell + 11.0 * centre) / 6.0
    guess_mid = (-left_cell + 5.0 * centre + 2.0 * right_cell) / 6.0
    guess_high = (2.0 * centre + 5.0 * right_cell - far_right) / 6.0
    return (weight_low * guess_low + weight_mid * guess_mid + weight_high * guess_high) / (weight_low + weight_mid + weight_high)

def face_flux(padded, fluxes, axis, count, normal, first, second):
    states = [lax.slice_in_dim(padded, shift_index, shift_index + count + 1, axis=axis) for shift_index in range(6)]
    physical = [lax.slice_in_dim(fluxes, shift_index, shift_index + count + 1, axis=axis) for shift_index in range(6)]
    mean = 0.5 * (states[2] + states[3])
    density = mean[0]
    normal_speed = mean[normal] / density
    speed_first = mean[first] / density
    speed_second = mean[second] / density
    kinetic = 0.5 * (jnp.square(normal_speed) + jnp.square(speed_first) + jnp.square(speed_second))
    pressure = pressure_of(mean)
    sound = jnp.sqrt(gamma_ratio * pressure / density)
    enthalpy = (mean[4] + pressure) / density
    inv_sound = 1.0 / sound
    factor_one = (gamma_ratio - 1.0) * jnp.square(inv_sound)
    factor_two = factor_one * kinetic
    dissipation = jnp.maximum(wave_speed(states[2], normal), wave_speed(states[3], normal))

    def project(vector):
        dens_part = vector[0]
        norm_part = vector[normal]
        first_part = vector[first]
        second_part = vector[second]
        energy_part = vector[4]
        tangent_sum = factor_one * (speed_first * first_part + speed_second * second_part - energy_part)
        wave_minus = 0.5 * ((factor_two + normal_speed * inv_sound) * dens_part - (factor_one * normal_speed + inv_sound) * norm_part - tangent_sum)
        entropy = (1.0 - factor_two) * dens_part + factor_one * normal_speed * norm_part + tangent_sum
        shear_first = first_part - speed_first * dens_part
        shear_second = second_part - speed_second * dens_part
        wave_plus = 0.5 * ((factor_two - normal_speed * inv_sound) * dens_part - (factor_one * normal_speed - inv_sound) * norm_part - tangent_sum)
        return (wave_minus, entropy, shear_first, shear_second, wave_plus)
    state_chars = [project(cell_state) for cell_state in states]
    flux_chars = [project(cell_flux) for cell_flux in physical]
    recon = []
    for field_index in range(5):
        plus_vals = [0.5 * (flux_chars[cell][field_index] + dissipation * state_chars[cell][field_index]) for cell in range(6)]
        minus_vals = [0.5 * (flux_chars[cell][field_index] - dissipation * state_chars[cell][field_index]) for cell in range(6)]
        recon.append(weno_side(plus_vals[0], plus_vals[1], plus_vals[2], plus_vals[3], plus_vals[4]) + weno_side(minus_vals[5], minus_vals[4], minus_vals[3], minus_vals[2], minus_vals[1]))
    wave_minus, entropy, shear_first, shear_second, wave_plus = recon
    acoustic = wave_minus + entropy + wave_plus
    parts = {}
    parts[0] = acoustic
    parts[normal] = (normal_speed - sound) * wave_minus + normal_speed * entropy + (normal_speed + sound) * wave_plus
    parts[first] = speed_first * acoustic + shear_first
    parts[second] = speed_second * acoustic + shear_second
    parts[4] = (enthalpy - normal_speed * sound) * wave_minus + kinetic * entropy + speed_first * shear_first + speed_second * shear_second + (enthalpy + normal_speed * sound) * wave_plus
    return jnp.stack([parts[index_part] for index_part in range(5)])

def divergence(padded, axis, count, normal, first, second):
    faces = face_flux(padded, euler_flux(padded, normal), axis, count, normal, first, second)
    return lax.slice_in_dim(faces, 1, count + 1, axis=axis) - lax.slice_in_dim(faces, 0, count, axis=axis)

def flip_radial(cells):
    turned = cells[:, :, ::-1]
    return jnp.concatenate([turned[:3], -turned[3:4], turned[4:]], axis=0)

def flip_theta(cells):
    return jnp.concatenate([cells[:2], -cells[2:3], cells[3:]], axis=0)

def mortar(planes, offset, fraction):
    count = planes.shape[3]
    cells = jnp.arange(count, dtype=jnp.int32)
    lower_index = ((offset - cells - 1) % count).astype(jnp.int32)
    upper_index = ((offset - cells) % count).astype(jnp.int32)
    blended = (1.0 - fraction) * jnp.take(planes, lower_index, axis=3) + fraction * jnp.take(planes, upper_index, axis=3)
    return flip_theta(blended)

def reference(base_state, section_state, rotor_step):
    state = section_state
    offset = rotor_step[0] // 4
    fraction = (rotor_step[0] % 4).astype(jnp.float32) / 4.0
    theta_padded = jnp.concatenate([state[..., -3:], state, state[..., :3]], axis=3)
    radial_padded = jnp.concatenate([flip_radial(state[:, :, :3]), state, flip_radial(state[:, :, -3:])], axis=2)
    front = state[:, :ZD]
    aft = state[:, ZD:]
    front_padded = jnp.concatenate([front[:, :1], front[:, :1], front[:, :1], front, mortar(aft[:, :3], offset, fraction)], axis=1)
    aft_padded = jnp.concatenate([mortar(front[:, -3:], offset, fraction), aft, aft[:, -1:], aft[:, -1:], aft[:, -1:]], axis=1)
    axial = jnp.concatenate([divergence(front_padded, 1, ZD, 1, 2, 3), divergence(aft_padded, 1, ZD, 1, 2, 3)], axis=1)
    radial = divergence(radial_padded, 2, NR, 3, 1, 2)
    azimuthal = divergence(theta_padded, 3, NT, 2, 1, 3)
    change = -step_ratio * (axial + radial + azimuthal)
    return 0.75 * base_state + 0.25 * (state + change)
```

```python
import jax
import jax.numpy as jnp
from jax import lax
from jax.sharding import PartitionSpec as P

gamma_ratio = 1.4
weno_epsilon = 1e-06
step_ratio = 0.12


def padded_2(cells, sides, width, closed):
    for axis, dim in sides:
        count = lax.axis_size(axis)
        ends = count if closed else count - 1
        head = lax.slice_in_dim(cells, 0, width, axis=dim)
        tail = lax.slice_in_dim(cells, cells.shape[dim] - width, cells.shape[dim], axis=dim)
        cells = jnp.concatenate(
            [
                lax.ppermute(tail, axis, [(i, (i + 1) % count) for i in range(ends)]),
                cells,
                lax.ppermute(head, axis, [((i + 1) % count, i) for i in range(ends)]),
            ],
            axis=dim,
        )
    return cells


def partner(block, axis, distance):
    count = lax.axis_size(axis)
    route = []
    for low in range(count):
        high = low | 1 << distance
        if high != low and high < count:
            route += [(low, high), (high, low)]
    return lax.ppermute(block, axis, route)


def pressure_of(state):
    kinetic = 0.5 * (jnp.square(state[1]) + jnp.square(state[2]) + jnp.square(state[3])) / state[0]
    return (gamma_ratio - 1.0) * (state[4] - kinetic)


def euler_flux(state, normal):
    pressure = pressure_of(state)
    velocity = state[normal] / state[0]
    flux = state * velocity[None]
    flux = flux.at[normal].add(pressure)
    flux = flux.at[4].add(pressure * velocity)
    return flux


def wave_speed(state, normal):
    pressure = pressure_of(state)
    return jnp.abs(state[normal] / state[0]) + jnp.sqrt(gamma_ratio * pressure / state[0])


def weno_side(far_left, left_cell, centre, right_cell, far_right):
    smooth_low = 13.0 / 12.0 * jnp.square(far_left - 2.0 * left_cell + centre) + 0.25 * jnp.square(
        far_left - 4.0 * left_cell + 3.0 * centre
    )
    smooth_mid = 13.0 / 12.0 * jnp.square(
        left_cell - 2.0 * centre + right_cell
    ) + 0.25 * jnp.square(left_cell - right_cell)
    smooth_high = 13.0 / 12.0 * jnp.square(
        centre - 2.0 * right_cell + far_right
    ) + 0.25 * jnp.square(3.0 * centre - 4.0 * right_cell + far_right)
    weight_low = 0.1 / jnp.square(weno_epsilon + smooth_low)
    weight_mid = 0.6 / jnp.square(weno_epsilon + smooth_mid)
    weight_high = 0.3 / jnp.square(weno_epsilon + smooth_high)
    guess_low = (2.0 * far_left - 7.0 * left_cell + 11.0 * centre) / 6.0
    guess_mid = (-left_cell + 5.0 * centre + 2.0 * right_cell) / 6.0
    guess_high = (2.0 * centre + 5.0 * right_cell - far_right) / 6.0
    return (weight_low * guess_low + weight_mid * guess_mid + weight_high * guess_high) / (
        weight_low + weight_mid + weight_high
    )


def face_flux(padded, fluxes, axis, count, normal, first, second):
    states = [
        lax.slice_in_dim(padded, shift_index, shift_index + count + 1, axis=axis)
        for shift_index in range(6)
    ]
    physical = [
        lax.slice_in_dim(fluxes, shift_index, shift_index + count + 1, axis=axis)
        for shift_index in range(6)
    ]
    mean = 0.5 * (states[2] + states[3])
    density = mean[0]
    normal_speed = mean[normal] / density
    speed_first = mean[first] / density
    speed_second = mean[second] / density
    kinetic = 0.5 * (jnp.square(normal_speed) + jnp.square(speed_first) + jnp.square(speed_second))
    pressure = pressure_of(mean)
    sound = jnp.sqrt(gamma_ratio * pressure / density)
    enthalpy = (mean[4] + pressure) / density
    inv_sound = 1.0 / sound
    factor_one = (gamma_ratio - 1.0) * jnp.square(inv_sound)
    factor_two = factor_one * kinetic
    dissipation = jnp.maximum(wave_speed(states[2], normal), wave_speed(states[3], normal))

    def project(vector):
        dens_part = vector[0]
        norm_part = vector[normal]
        first_part = vector[first]
        second_part = vector[second]
        energy_part = vector[4]
        tangent_sum = factor_one * (
            speed_first * first_part + speed_second * second_part - energy_part
        )
        wave_minus = 0.5 * (
            (factor_two + normal_speed * inv_sound) * dens_part
            - (factor_one * normal_speed + inv_sound) * norm_part
            - tangent_sum
        )
        entropy = (
            (1.0 - factor_two) * dens_part + factor_one * normal_speed * norm_part + tangent_sum
        )
        shear_first = first_part - speed_first * dens_part
        shear_second = second_part - speed_second * dens_part
        wave_plus = 0.5 * (
            (factor_two - normal_speed * inv_sound) * dens_part
            - (factor_one * normal_speed - inv_sound) * norm_part
            - tangent_sum
        )
        return (wave_minus, entropy, shear_first, shear_second, wave_plus)

    state_chars = [project(cell_state) for cell_state in states]
    flux_chars = [project(cell_flux) for cell_flux in physical]
    recon = []
    for field_index in range(5):
        plus_vals = [
            0.5 * (flux_chars[cell][field_index] + dissipation * state_chars[cell][field_index])
            for cell in range(6)
        ]
        minus_vals = [
            0.5 * (flux_chars[cell][field_index] - dissipation * state_chars[cell][field_index])
            for cell in range(6)
        ]
        recon.append(
            weno_side(plus_vals[0], plus_vals[1], plus_vals[2], plus_vals[3], plus_vals[4])
            + weno_side(minus_vals[5], minus_vals[4], minus_vals[3], minus_vals[2], minus_vals[1])
        )
    wave_minus, entropy, shear_first, shear_second, wave_plus = recon
    acoustic = wave_minus + entropy + wave_plus
    parts = {}
    parts[0] = acoustic
    parts[normal] = (
        (normal_speed - sound) * wave_minus
        + normal_speed * entropy
        + (normal_speed + sound) * wave_plus
    )
    parts[first] = speed_first * acoustic + shear_first
    parts[second] = speed_second * acoustic + shear_second
    parts[4] = (
        (enthalpy - normal_speed * sound) * wave_minus
        + kinetic * entropy
        + speed_first * shear_first
        + speed_second * shear_second
        + (enthalpy + normal_speed * sound) * wave_plus
    )
    return jnp.stack([parts[index_part] for index_part in range(5)])


def divergence(padded, axis, count, normal, first, second):
    faces = face_flux(padded, euler_flux(padded, normal), axis, count, normal, first, second)
    return lax.slice_in_dim(faces, 1, count + 1, axis=axis) - lax.slice_in_dim(
        faces, 0, count, axis=axis
    )


def flip_radial(cells):
    turned = cells[:, :, ::-1]
    return jnp.concatenate([turned[:3], -turned[3:4], turned[4:]], axis=0)


def flip_theta(cells):
    return jnp.concatenate([cells[:2], -cells[2:3], cells[3:]], axis=0)


def shift_ring(cells, axis, distance):
    count = lax.axis_size(axis)
    return lax.ppermute(cells, axis, [(i, (i + distance) % count) for i in range(count)])


def facing_window(section_state, rotor_step):
    width = section_state.shape[3]
    offset = rotor_step[0] // 4
    turns = offset // width
    remainder = offset % width
    block_index = lax.axis_index("blk")
    slab_count = lax.axis_size("theta")
    block_count = lax.axis_size("blk")
    outgoing = jnp.where(block_index == 0, section_state[:, -3:], section_state[:, :3])
    outgoing = outgoing[..., ::-1]
    route = []
    for blk_from in range(block_count):
        for slab_from in range(slab_count):
            blk_to = (blk_from + 1) % block_count
            slab_to = (-1 - slab_from) % slab_count
            route.append((blk_from * slab_count + slab_from, blk_to * slab_count + slab_to))
    held = lax.ppermute(outgoing, ("blk", "theta"), route)
    bit = 1
    while bit < slab_count:
        moved = shift_ring(held, "theta", bit)
        held = jnp.where((turns // bit) % 2 == 1, moved, held)
        bit *= 2
    following = shift_ring(held, "theta", 1)
    doubled = jnp.concatenate([following, held], axis=3)
    return lax.dynamic_slice_in_dim(doubled, width - 1 - remainder, width + 1, 3)


def shards(base_state, section_state, rotor_step):
    planes = section_state.shape[1]
    bands = section_state.shape[2]
    width = section_state.shape[3]
    fraction = (rotor_step[0] % 4).astype(jnp.float32) / 4.0
    theta_padded = padded_2(section_state, (("theta", 3),), 3, True)
    radial_raw = padded_2(section_state, (("radial", 2),), 3, False)
    band_index = lax.axis_index("radial")
    band_count = lax.axis_size("radial")
    lower_wall = jnp.where(
        band_index == 0, flip_radial(section_state[:, :, :3]), radial_raw[:, :, :3]
    )
    upper_wall = jnp.where(
        band_index == band_count - 1, flip_radial(section_state[:, :, -3:]), radial_raw[:, :, -3:]
    )
    radial_padded = jnp.concatenate([lower_wall, section_state, upper_wall], axis=2)
    block_index = lax.axis_index("blk")
    front = block_index == 0
    window = facing_window(section_state, rotor_step)
    ghost = flip_theta(
        (1.0 - fraction) * window[..., 1 : width + 1] + fraction * window[..., :width]
    )
    edge_low = jnp.concatenate(
        [section_state[:, :1], section_state[:, :1], section_state[:, :1]], axis=1
    )
    edge_high = jnp.concatenate(
        [section_state[:, -1:], section_state[:, -1:], section_state[:, -1:]], axis=1
    )
    local_window = jnp.where(
        front,
        jnp.concatenate([edge_low, section_state], axis=1),
        jnp.concatenate([section_state, edge_high], axis=1),
    )
    local_faces = face_flux(
        local_window, euler_flux(local_window, 1), 1, local_window.shape[1] - 6, 1, 2, 3
    )
    mortar_window = jnp.where(
        front,
        jnp.concatenate([section_state[:, 1:], ghost], axis=1),
        jnp.concatenate([ghost, section_state[:, :-1]], axis=1),
    )
    mortar_faces = face_flux(
        mortar_window, euler_flux(mortar_window, 1), 1, mortar_window.shape[1] - 6, 1, 2, 3
    )
    faces = jnp.where(
        front,
        jnp.concatenate([local_faces, mortar_faces], axis=1),
        jnp.concatenate([mortar_faces, local_faces], axis=1),
    )
    axial = lax.slice_in_dim(faces, 1, planes + 1, axis=1) - lax.slice_in_dim(
        faces, 0, planes, axis=1
    )
    radial = divergence(radial_padded, 2, bands, 3, 1, 2)
    azimuthal = divergence(theta_padded, 3, width, 2, 1, 3)
    change = -step_ratio * (axial + radial + azimuthal)
    return 0.75 * base_state + 0.25 * (section_state + change)


def solution(mesh):
    in_specs = (P(None, "blk", "radial", "theta"), P(None, "blk", "radial", "theta"), P())
    out_specs = P(None, "blk", "radial", "theta")
    return jax.shard_map(shards, mesh=mesh, in_specs=in_specs, out_specs=out_specs, check_vma=False)
```

```python
import jax
import jax.numpy as jnp
from jax import lax
from jax.sharding import PartitionSpec as P

gamma_ratio = 1.4
weno_epsilon = 1e-06
step_ratio = 0.12


def padded_2(cells, sides, width, closed):
    for axis, dim in sides:
        count = lax.axis_size(axis)
        ends = count if closed else count - 1
        head = lax.slice_in_dim(cells, 0, width, axis=dim)
        tail = lax.slice_in_dim(cells, cells.shape[dim] - width, cells.shape[dim], axis=dim)
        cells = jnp.concatenate(
            [
                lax.ppermute(tail, axis, [(i, (i + 1) % count) for i in range(ends)]),
                cells,
                lax.ppermute(head, axis, [((i + 1) % count, i) for i in range(ends)]),
            ],
            axis=dim,
        )
    return cells


def partner(block, axis, distance):
    count = lax.axis_size(axis)
    route = []
    for low in range(count):
        high = low | 1 << distance
        if high != low and high < count:
            route += [(low, high), (high, low)]
    return lax.ppermute(block, axis, route)


def pressure_of(state):
    kinetic = 0.5 * (jnp.square(state[1]) + jnp.square(state[2]) + jnp.square(state[3])) / state[0]
    return (gamma_ratio - 1.0) * (state[4] - kinetic)


def euler_flux(state, normal):
    pressure = pressure_of(state)
    velocity = state[normal] / state[0]
    flux = state * velocity[None]
    flux = flux.at[normal].add(pressure)
    flux = flux.at[4].add(pressure * velocity)
    return flux


def wave_speed(state, normal):
    pressure = pressure_of(state)
    return jnp.abs(state[normal] / state[0]) + jnp.sqrt(gamma_ratio * pressure / state[0])


def weno_side(far_left, left_cell, centre, right_cell, far_right):
    smooth_low = 13.0 / 12.0 * jnp.square(far_left - 2.0 * left_cell + centre) + 0.25 * jnp.square(
        far_left - 4.0 * left_cell + 3.0 * centre
    )
    smooth_mid = 13.0 / 12.0 * jnp.square(
        left_cell - 2.0 * centre + right_cell
    ) + 0.25 * jnp.square(left_cell - right_cell)
    smooth_high = 13.0 / 12.0 * jnp.square(
        centre - 2.0 * right_cell + far_right
    ) + 0.25 * jnp.square(3.0 * centre - 4.0 * right_cell + far_right)
    weight_low = 0.1 / jnp.square(weno_epsilon + smooth_low)
    weight_mid = 0.6 / jnp.square(weno_epsilon + smooth_mid)
    weight_high = 0.3 / jnp.square(weno_epsilon + smooth_high)
    guess_low = (2.0 * far_left - 7.0 * left_cell + 11.0 * centre) / 6.0
    guess_mid = (-left_cell + 5.0 * centre + 2.0 * right_cell) / 6.0
    guess_high = (2.0 * centre + 5.0 * right_cell - far_right) / 6.0
    return (weight_low * guess_low + weight_mid * guess_mid + weight_high * guess_high) / (
        weight_low + weight_mid + weight_high
    )


def face_flux(padded, fluxes, axis, count, normal, first, second):
    states = [
        lax.slice_in_dim(padded, shift_index, shift_index + count + 1, axis=axis)
        for shift_index in range(6)
    ]
    physical = [
        lax.slice_in_dim(fluxes, shift_index, shift_index + count + 1, axis=axis)
        for shift_index in range(6)
    ]
    mean = 0.5 * (states[2] + states[3])
    density = mean[0]
    normal_speed = mean[normal] / density
    speed_first = mean[first] / density
    speed_second = mean[second] / density
    kinetic = 0.5 * (jnp.square(normal_speed) + jnp.square(speed_first) + jnp.square(speed_second))
    pressure = pressure_of(mean)
    sound = jnp.sqrt(gamma_ratio * pressure / density)
    enthalpy = (mean[4] + pressure) / density
    inv_sound = 1.0 / sound
    factor_one = (gamma_ratio - 1.0) * jnp.square(inv_sound)
    factor_two = factor_one * kinetic
    dissipation = jnp.maximum(wave_speed(states[2], normal), wave_speed(states[3], normal))

    def project(vector):
        dens_part = vector[0]
        norm_part = vector[normal]
        first_part = vector[first]
        second_part = vector[second]
        energy_part = vector[4]
        tangent_sum = factor_one * (
            speed_first * first_part + speed_second * second_part - energy_part
        )
        wave_minus = 0.5 * (
            (factor_two + normal_speed * inv_sound) * dens_part
            - (factor_one * normal_speed + inv_sound) * norm_part
            - tangent_sum
        )
        entropy = (
            (1.0 - factor_two) * dens_part + factor_one * normal_speed * norm_part + tangent_sum
        )
        shear_first = first_part - speed_first * dens_part
        shear_second = second_part - speed_second * dens_part
        wave_plus = 0.5 * (
            (factor_two - normal_speed * inv_sound) * dens_part
            - (factor_one * normal_speed - inv_sound) * norm_part
            - tangent_sum
        )
        return (wave_minus, entropy, shear_first, shear_second, wave_plus)

    state_chars = [project(cell_state) for cell_state in states]
    flux_chars = [project(cell_flux) for cell_flux in physical]
    recon = []
    for field_index in range(5):
        plus_vals = [
            0.5 * (flux_chars[cell][field_index] + dissipation * state_chars[cell][field_index])
            for cell in range(6)
        ]
        minus_vals = [
            0.5 * (flux_chars[cell][field_index] - dissipation * state_chars[cell][field_index])
            for cell in range(6)
        ]
        recon.append(
            weno_side(plus_vals[0], plus_vals[1], plus_vals[2], plus_vals[3], plus_vals[4])
            + weno_side(minus_vals[5], minus_vals[4], minus_vals[3], minus_vals[2], minus_vals[1])
        )
    wave_minus, entropy, shear_first, shear_second, wave_plus = recon
    acoustic = wave_minus + entropy + wave_plus
    parts = {}
    parts[0] = acoustic
    parts[normal] = (
        (normal_speed - sound) * wave_minus
        + normal_speed * entropy
        + (normal_speed + sound) * wave_plus
    )
    parts[first] = speed_first * acoustic + shear_first
    parts[second] = speed_second * acoustic + shear_second
    parts[4] = (
        (enthalpy - normal_speed * sound) * wave_minus
        + kinetic * entropy
        + speed_first * shear_first
        + speed_second * shear_second
        + (enthalpy + normal_speed * sound) * wave_plus
    )
    return jnp.stack([parts[index_part] for index_part in range(5)])


def divergence(padded, axis, count, normal, first, second):
    faces = face_flux(padded, euler_flux(padded, normal), axis, count, normal, first, second)
    return lax.slice_in_dim(faces, 1, count + 1, axis=axis) - lax.slice_in_dim(
        faces, 0, count, axis=axis
    )


def flip_radial(cells):
    turned = cells[:, :, ::-1]
    return jnp.concatenate([turned[:3], -turned[3:4], turned[4:]], axis=0)


def flip_theta(cells):
    return jnp.concatenate([cells[:2], -cells[2:3], cells[3:]], axis=0)


def facing_window(section_state, rotor_step):
    width = section_state.shape[3]
    offset = rotor_step[0] // 4
    rows = lax.axis_size("tx")
    columns = lax.axis_size("tz")
    slab_count = rows * columns
    turns = offset // width % slab_count
    remainder = offset % width
    block_index = lax.axis_index("blk")
    block_count = lax.axis_size("blk")
    outgoing = jnp.where(block_index == 0, section_state[:, -3:], section_state[:, :3])
    outgoing = outgoing[..., ::-1]
    this_route = []
    next_route = []
    for blk_from in range(block_count):
        blk_to = (blk_from + 1) % block_count
        for slab_from in range(slab_count):
            source = blk_from * slab_count + slab_from
            this_route.append((source, blk_to * slab_count + (-1 - slab_from) % slab_count))
            next_route.append((source, blk_to * slab_count + (-slab_from) % slab_count))
    axes = ("blk", "tx", "tz")
    this_slab = lax.ppermute(outgoing, axes, this_route)
    next_slab = lax.ppermute(outgoing, axes, next_route)
    doubled = jnp.concatenate([next_slab, this_slab], axis=3)
    window = lax.dynamic_slice_in_dim(doubled, width - 1 - remainder, width + 1, 3)
    row = lax.axis_index("tx")
    column = lax.axis_index("tz")
    step = turns % columns
    carry = (column + step >= columns).astype(jnp.int32)
    source_row = (row - turns // columns - carry) % rows
    gathered = lax.all_gather(window, "tx")
    chosen = lax.dynamic_index_in_dim(gathered, source_row, 0, keepdims=False)
    gathered = lax.all_gather(chosen, "tz")
    source_column = (column - step) % columns
    return lax.dynamic_index_in_dim(gathered, source_column, 0, keepdims=False)


def shards(base_state, section_state, rotor_step):
    planes = section_state.shape[1]
    bands = section_state.shape[2]
    width = section_state.shape[3]
    fraction = (rotor_step[0] % 4).astype(jnp.float32) / 4.0
    theta_padded = padded_2(section_state, ((("tx", "tz"), 3),), 3, True)
    radial_raw = padded_2(section_state, (("radial", 2),), 3, False)
    band_index = lax.axis_index("radial")
    band_count = lax.axis_size("radial")
    lower_wall = jnp.where(
        band_index == 0, flip_radial(section_state[:, :, :3]), radial_raw[:, :, :3]
    )
    upper_wall = jnp.where(
        band_index == band_count - 1, flip_radial(section_state[:, :, -3:]), radial_raw[:, :, -3:]
    )
    radial_padded = jnp.concatenate([lower_wall, section_state, upper_wall], axis=2)
    block_index = lax.axis_index("blk")
    front = block_index == 0
    window = facing_window(section_state, rotor_step)
    ghost = flip_theta(
        (1.0 - fraction) * window[..., 1 : width + 1] + fraction * window[..., :width]
    )
    edge_low = jnp.concatenate(
        [section_state[:, :1], section_state[:, :1], section_state[:, :1]], axis=1
    )
    edge_high = jnp.concatenate(
        [section_state[:, -1:], section_state[:, -1:], section_state[:, -1:]], axis=1
    )
    local_window = jnp.where(
        front,
        jnp.concatenate([edge_low, section_state], axis=1),
        jnp.concatenate([section_state, edge_high], axis=1),
    )
    local_faces = face_flux(
        local_window, euler_flux(local_window, 1), 1, local_window.shape[1] - 6, 1, 2, 3
    )
    mortar_window = jnp.where(
        front,
        jnp.concatenate([section_state[:, 1:], ghost], axis=1),
        jnp.concatenate([ghost, section_state[:, :-1]], axis=1),
    )
    mortar_faces = face_flux(
        mortar_window, euler_flux(mortar_window, 1), 1, mortar_window.shape[1] - 6, 1, 2, 3
    )
    faces = jnp.where(
        front,
        jnp.concatenate([local_faces, mortar_faces], axis=1),
        jnp.concatenate([mortar_faces, local_faces], axis=1),
    )
    axial = lax.slice_in_dim(faces, 1, planes + 1, axis=1) - lax.slice_in_dim(
        faces, 0, planes, axis=1
    )
    radial = divergence(radial_padded, 2, bands, 3, 1, 2)
    azimuthal = divergence(theta_padded, 3, width, 2, 1, 3)
    change = -step_ratio * (axial + radial + azimuthal)
    return 0.75 * base_state + 0.25 * (section_state + change)


def solution(mesh):
    blocks, slabs, bands = (mesh.shape[name] for name in ("blk", "theta", "radial"))
    rows = 4 if slabs % 4 == 0 else 1
    grid = jax.sharding.Mesh(
        mesh.devices.reshape(blocks, rows, slabs // rows, bands), ("blk", "tx", "tz", "radial")
    )
    in_specs = (P(None, "blk", "radial", ("tx", "tz")), P(None, "blk", "radial", ("tx", "tz")), P())
    out_specs = P(None, "blk", "radial", ("tx", "tz"))
    inner = jax.shard_map(shards, mesh=grid, in_specs=in_specs, out_specs=out_specs, check_vma=False)
    sharded = jax.sharding.NamedSharding(mesh, P(None, "blk", "radial", "theta"))

    def run(base_state, section_state, rotor_step):
        return jax.lax.with_sharding_constraint(
            inner(base_state, section_state, rotor_step), sharded
        )

    return run
```

```python
import jax
import jax.numpy as jnp
from jax import lax
from jax.sharding import PartitionSpec as P

gamma_ratio = 1.4
weno_epsilon = 1e-06
step_ratio = 0.12


def padded_2(cells, sides, width, closed):
    for axis, dim in sides:
        count = lax.axis_size(axis)
        ends = count if closed else count - 1
        head = lax.slice_in_dim(cells, 0, width, axis=dim)
        tail = lax.slice_in_dim(cells, cells.shape[dim] - width, cells.shape[dim], axis=dim)
        cells = jnp.concatenate(
            [
                lax.ppermute(tail, axis, [(i, (i + 1) % count) for i in range(ends)]),
                cells,
                lax.ppermute(head, axis, [((i + 1) % count, i) for i in range(ends)]),
            ],
            axis=dim,
        )
    return cells


def partner(block, axis, distance):
    count = lax.axis_size(axis)
    route = []
    for low in range(count):
        high = low | 1 << distance
        if high != low and high < count:
            route += [(low, high), (high, low)]
    return lax.ppermute(block, axis, route)


def pressure_of(state):
    kinetic = 0.5 * (jnp.square(state[1]) + jnp.square(state[2]) + jnp.square(state[3])) / state[0]
    return (gamma_ratio - 1.0) * (state[4] - kinetic)


def euler_flux(state, normal):
    pressure = pressure_of(state)
    velocity = state[normal] / state[0]
    flux = state * velocity[None]
    flux = flux.at[normal].add(pressure)
    flux = flux.at[4].add(pressure * velocity)
    return flux


def wave_speed(state, normal):
    pressure = pressure_of(state)
    return jnp.abs(state[normal] / state[0]) + jnp.sqrt(gamma_ratio * pressure / state[0])


def weno_side(far_left, left_cell, centre, right_cell, far_right):
    smooth_low = 13.0 / 12.0 * jnp.square(far_left - 2.0 * left_cell + centre) + 0.25 * jnp.square(
        far_left - 4.0 * left_cell + 3.0 * centre
    )
    smooth_mid = 13.0 / 12.0 * jnp.square(
        left_cell - 2.0 * centre + right_cell
    ) + 0.25 * jnp.square(left_cell - right_cell)
    smooth_high = 13.0 / 12.0 * jnp.square(
        centre - 2.0 * right_cell + far_right
    ) + 0.25 * jnp.square(3.0 * centre - 4.0 * right_cell + far_right)
    weight_low = 0.1 / jnp.square(weno_epsilon + smooth_low)
    weight_mid = 0.6 / jnp.square(weno_epsilon + smooth_mid)
    weight_high = 0.3 / jnp.square(weno_epsilon + smooth_high)
    guess_low = (2.0 * far_left - 7.0 * left_cell + 11.0 * centre) / 6.0
    guess_mid = (-left_cell + 5.0 * centre + 2.0 * right_cell) / 6.0
    guess_high = (2.0 * centre + 5.0 * right_cell - far_right) / 6.0
    return (weight_low * guess_low + weight_mid * guess_mid + weight_high * guess_high) / (
        weight_low + weight_mid + weight_high
    )


def face_flux(padded, fluxes, axis, count, normal, first, second):
    states = [
        lax.slice_in_dim(padded, shift_index, shift_index + count + 1, axis=axis)
        for shift_index in range(6)
    ]
    physical = [
        lax.slice_in_dim(fluxes, shift_index, shift_index + count + 1, axis=axis)
        for shift_index in range(6)
    ]
    mean = 0.5 * (states[2] + states[3])
    density = mean[0]
    normal_speed = mean[normal] / density
    speed_first = mean[first] / density
    speed_second = mean[second] / density
    kinetic = 0.5 * (jnp.square(normal_speed) + jnp.square(speed_first) + jnp.square(speed_second))
    pressure = pressure_of(mean)
    sound = jnp.sqrt(gamma_ratio * pressure / density)
    enthalpy = (mean[4] + pressure) / density
    inv_sound = 1.0 / sound
    factor_one = (gamma_ratio - 1.0) * jnp.square(inv_sound)
    factor_two = factor_one * kinetic
    dissipation = jnp.maximum(wave_speed(states[2], normal), wave_speed(states[3], normal))

    def project(vector):
        dens_part = vector[0]
        norm_part = vector[normal]
        first_part = vector[first]
        second_part = vector[second]
        energy_part = vector[4]
        tangent_sum = factor_one * (
            speed_first * first_part + speed_second * second_part - energy_part
        )
        wave_minus = 0.5 * (
            (factor_two + normal_speed * inv_sound) * dens_part
            - (factor_one * normal_speed + inv_sound) * norm_part
            - tangent_sum
        )
        entropy = (
            (1.0 - factor_two) * dens_part + factor_one * normal_speed * norm_part + tangent_sum
        )
        shear_first = first_part - speed_first * dens_part
        shear_second = second_part - speed_second * dens_part
        wave_plus = 0.5 * (
            (factor_two - normal_speed * inv_sound) * dens_part
            - (factor_one * normal_speed - inv_sound) * norm_part
            - tangent_sum
        )
        return (wave_minus, entropy, shear_first, shear_second, wave_plus)

    state_chars = [project(cell_state) for cell_state in states]
    flux_chars = [project(cell_flux) for cell_flux in physical]
    recon = []
    for field_index in range(5):
        plus_vals = [
            0.5 * (flux_chars[cell][field_index] + dissipation * state_chars[cell][field_index])
            for cell in range(6)
        ]
        minus_vals = [
            0.5 * (flux_chars[cell][field_index] - dissipation * state_chars[cell][field_index])
            for cell in range(6)
        ]
        recon.append(
            weno_side(plus_vals[0], plus_vals[1], plus_vals[2], plus_vals[3], plus_vals[4])
            + weno_side(minus_vals[5], minus_vals[4], minus_vals[3], minus_vals[2], minus_vals[1])
        )
    wave_minus, entropy, shear_first, shear_second, wave_plus = recon
    acoustic = wave_minus + entropy + wave_plus
    parts = {}
    parts[0] = acoustic
    parts[normal] = (
        (normal_speed - sound) * wave_minus
        + normal_speed * entropy
        + (normal_speed + sound) * wave_plus
    )
    parts[first] = speed_first * acoustic + shear_first
    parts[second] = speed_second * acoustic + shear_second
    parts[4] = (
        (enthalpy - normal_speed * sound) * wave_minus
        + kinetic * entropy
        + speed_first * shear_first
        + speed_second * shear_second
        + (enthalpy + normal_speed * sound) * wave_plus
    )
    return jnp.stack([parts[index_part] for index_part in range(5)])


def divergence(padded, axis, count, normal, first, second):
    faces = face_flux(padded, euler_flux(padded, normal), axis, count, normal, first, second)
    return lax.slice_in_dim(faces, 1, count + 1, axis=axis) - lax.slice_in_dim(
        faces, 0, count, axis=axis
    )


def flip_radial(cells):
    turned = cells[:, :, ::-1]
    return jnp.concatenate([turned[:3], -turned[3:4], turned[4:]], axis=0)


def flip_theta(cells):
    return jnp.concatenate([cells[:2], -cells[2:3], cells[3:]], axis=0)


def facing_slabs(section_state):
    block_index = lax.axis_index("blk")
    block_count = lax.axis_size("blk")
    slab_count = lax.axis_size("tx") * lax.axis_size("tz")
    outgoing = jnp.where(block_index == 0, section_state[:, -3:], section_state[:, :3])
    outgoing = outgoing[..., ::-1]
    this_route = []
    next_route = []
    for blk_from in range(block_count):
        blk_to = (blk_from + 1) % block_count
        for slab_from in range(slab_count):
            source = blk_from * slab_count + slab_from
            this_route.append((source, blk_to * slab_count + slab_from))
            next_route.append((source, blk_to * slab_count + (slab_from - 1) % slab_count))
    axes = ("blk", "tx", "tz")
    return lax.ppermute(outgoing, axes, this_route), lax.ppermute(outgoing, axes, next_route)


def after(value, index):
    return index + jnp.isnan(value.reshape(-1)[0]).astype(index.dtype)


def window_of(this_slab, next_slab, rotor_step, before):
    width = this_slab.shape[3]
    remainder = after(before, rotor_step[0] // 4 % width)
    doubled = jnp.concatenate([next_slab, this_slab], axis=3)
    return lax.dynamic_slice_in_dim(doubled, width - 1 - remainder, width + 1, 3)


def route_parts(rotor_step, width):
    rows = lax.axis_size("tx")
    columns = lax.axis_size("tz")
    turns = rotor_step[0] // 4 // width
    centre = (turns - 1) % (rows * columns)
    return rows, columns, centre // columns, centre % columns


def pick_row(window, rotor_step, before):
    rows, columns, centre_row, centre_column = route_parts(rotor_step, window.shape[3] - 1)
    reader = (centre_column - lax.axis_index("tz")) % columns
    borrow = (reader > centre_column).astype(jnp.int32)
    source_row = (centre_row - lax.axis_index("tx") - borrow) % rows
    gathered = lax.all_gather(window, "tx")
    return lax.dynamic_index_in_dim(gathered, after(before, source_row), 0, keepdims=False)


def pick_column(chosen, rotor_step, before):
    rows, columns, centre_row, centre_column = route_parts(rotor_step, chosen.shape[3] - 1)
    source_column = (centre_column - lax.axis_index("tz")) % columns
    gathered = lax.all_gather(chosen, "tz")
    return lax.dynamic_index_in_dim(gathered, after(before, source_column), 0, keepdims=False)


def shards(base_state, section_state, rotor_step):
    planes = section_state.shape[1]
    bands = section_state.shape[2]
    width = section_state.shape[3]
    fraction = (rotor_step[0] % 4).astype(jnp.float32) / 4.0
    theta_padded = padded_2(section_state, ((("tx", "tz"), 3),), 3, True)
    radial_raw = padded_2(section_state, (("radial", 2),), 3, False)
    band_index = lax.axis_index("radial")
    band_count = lax.axis_size("radial")
    lower_wall = jnp.where(
        band_index == 0, flip_radial(section_state[:, :, :3]), radial_raw[:, :, :3]
    )
    upper_wall = jnp.where(
        band_index == band_count - 1, flip_radial(section_state[:, :, -3:]), radial_raw[:, :, -3:]
    )
    radial_padded = jnp.concatenate([lower_wall, section_state, upper_wall], axis=2)
    block_index = lax.axis_index("blk")
    front = block_index == 0
    this_slab, next_slab = facing_slabs(section_state)
    edge_low = jnp.concatenate(
        [section_state[:, :1], section_state[:, :1], section_state[:, :1]], axis=1
    )
    edge_high = jnp.concatenate(
        [section_state[:, -1:], section_state[:, -1:], section_state[:, -1:]], axis=1
    )
    local_window = jnp.where(
        front,
        jnp.concatenate([edge_low, section_state], axis=1),
        jnp.concatenate([section_state, edge_high], axis=1),
    )
    local_faces = face_flux(
        local_window, euler_flux(local_window, 1), 1, local_window.shape[1] - 6, 1, 2, 3
    )
    window = window_of(this_slab, next_slab, rotor_step, local_faces)
    radial = divergence(radial_padded, 2, bands, 3, 1, 2)
    chosen = pick_row(window, rotor_step, radial)
    azimuthal = divergence(theta_padded, 3, width, 2, 1, 3)
    window = pick_column(chosen, rotor_step, azimuthal)
    ghost = flip_theta(
        (1.0 - fraction) * window[..., 1 : width + 1] + fraction * window[..., :width]
    )
    mortar_window = jnp.where(
        front,
        jnp.concatenate([section_state[:, 1:], ghost], axis=1),
        jnp.concatenate([ghost, section_state[:, :-1]], axis=1),
    )
    mortar_faces = face_flux(
        mortar_window, euler_flux(mortar_window, 1), 1, mortar_window.shape[1] - 6, 1, 2, 3
    )
    faces = jnp.where(
        front,
        jnp.concatenate([local_faces, mortar_faces], axis=1),
        jnp.concatenate([mortar_faces, local_faces], axis=1),
    )
    axial = lax.slice_in_dim(faces, 1, planes + 1, axis=1) - lax.slice_in_dim(
        faces, 0, planes, axis=1
    )
    change = -step_ratio * (axial + radial + azimuthal)
    return 0.75 * base_state + 0.25 * (section_state + change)


def solution(mesh):
    blocks, slabs, bands = (mesh.shape[name] for name in ("blk", "theta", "radial"))
    rows = 4 if slabs % 4 == 0 else 1
    grid = jax.sharding.Mesh(
        mesh.devices.reshape(blocks, rows, slabs // rows, bands), ("blk", "tx", "tz", "radial")
    )
    in_specs = (P(None, "blk", "radial", ("tx", "tz")), P(None, "blk", "radial", ("tx", "tz")), P())
    out_specs = P(None, "blk", "radial", ("tx", "tz"))
    inner = jax.shard_map(shards, mesh=grid, in_specs=in_specs, out_specs=out_specs, check_vma=False)
    sharded = jax.sharding.NamedSharding(mesh, P(None, "blk", "radial", "theta"))

    def run(base_state, section_state, rotor_step):
        return jax.lax.with_sharding_constraint(
            inner(base_state, section_state, rotor_step), sharded
        )

    return run
```

```python
import jax
import jax.numpy as jnp
from jax import lax
from jax.sharding import PartitionSpec as P

gamma_ratio = 1.4
weno_epsilon = 1e-06
step_ratio = 0.12


def padded_2(cells, sides, width, closed):
    for axis, dim in sides:
        count = lax.axis_size(axis)
        ends = count if closed else count - 1
        head = lax.slice_in_dim(cells, 0, width, axis=dim)
        tail = lax.slice_in_dim(cells, cells.shape[dim] - width, cells.shape[dim], axis=dim)
        cells = jnp.concatenate(
            [
                lax.ppermute(tail, axis, [(i, (i + 1) % count) for i in range(ends)]),
                cells,
                lax.ppermute(head, axis, [((i + 1) % count, i) for i in range(ends)]),
            ],
            axis=dim,
        )
    return cells


def partner(block, axis, distance):
    count = lax.axis_size(axis)
    route = []
    for low in range(count):
        high = low | 1 << distance
        if high != low and high < count:
            route += [(low, high), (high, low)]
    return lax.ppermute(block, axis, route)


def pressure_of(state):
    kinetic = 0.5 * (jnp.square(state[1]) + jnp.square(state[2]) + jnp.square(state[3])) / state[0]
    return (gamma_ratio - 1.0) * (state[4] - kinetic)


def euler_flux(state, normal):
    pressure = pressure_of(state)
    velocity = state[normal] / state[0]
    flux = state * velocity[None]
    flux = flux.at[normal].add(pressure)
    flux = flux.at[4].add(pressure * velocity)
    return flux


def wave_speed(state, normal):
    pressure = pressure_of(state)
    return jnp.abs(state[normal] / state[0]) + jnp.sqrt(gamma_ratio * pressure / state[0])


def weno_side(far_left, left_cell, centre, right_cell, far_right):
    smooth_low = 13.0 / 12.0 * jnp.square(far_left - 2.0 * left_cell + centre) + 0.25 * jnp.square(
        far_left - 4.0 * left_cell + 3.0 * centre
    )
    smooth_mid = 13.0 / 12.0 * jnp.square(
        left_cell - 2.0 * centre + right_cell
    ) + 0.25 * jnp.square(left_cell - right_cell)
    smooth_high = 13.0 / 12.0 * jnp.square(
        centre - 2.0 * right_cell + far_right
    ) + 0.25 * jnp.square(3.0 * centre - 4.0 * right_cell + far_right)
    weight_low = 0.1 / jnp.square(weno_epsilon + smooth_low)
    weight_mid = 0.6 / jnp.square(weno_epsilon + smooth_mid)
    weight_high = 0.3 / jnp.square(weno_epsilon + smooth_high)
    guess_low = (2.0 * far_left - 7.0 * left_cell + 11.0 * centre) / 6.0
    guess_mid = (-left_cell + 5.0 * centre + 2.0 * right_cell) / 6.0
    guess_high = (2.0 * centre + 5.0 * right_cell - far_right) / 6.0
    return (weight_low * guess_low + weight_mid * guess_mid + weight_high * guess_high) / (
        weight_low + weight_mid + weight_high
    )


def face_flux(padded, fluxes, axis, count, normal, first, second):
    states = [
        lax.slice_in_dim(padded, shift_index, shift_index + count + 1, axis=axis)
        for shift_index in range(6)
    ]
    physical = [
        lax.slice_in_dim(fluxes, shift_index, shift_index + count + 1, axis=axis)
        for shift_index in range(6)
    ]
    mean = 0.5 * (states[2] + states[3])
    density = mean[0]
    normal_speed = mean[normal] / density
    speed_first = mean[first] / density
    speed_second = mean[second] / density
    kinetic = 0.5 * (jnp.square(normal_speed) + jnp.square(speed_first) + jnp.square(speed_second))
    pressure = pressure_of(mean)
    sound = jnp.sqrt(gamma_ratio * pressure / density)
    enthalpy = (mean[4] + pressure) / density
    inv_sound = 1.0 / sound
    factor_one = (gamma_ratio - 1.0) * jnp.square(inv_sound)
    factor_two = factor_one * kinetic
    dissipation = jnp.maximum(wave_speed(states[2], normal), wave_speed(states[3], normal))

    def project(vector):
        dens_part = vector[0]
        norm_part = vector[normal]
        first_part = vector[first]
        second_part = vector[second]
        energy_part = vector[4]
        tangent_sum = factor_one * (
            speed_first * first_part + speed_second * second_part - energy_part
        )
        wave_minus = 0.5 * (
            (factor_two + normal_speed * inv_sound) * dens_part
            - (factor_one * normal_speed + inv_sound) * norm_part
            - tangent_sum
        )
        entropy = (
            (1.0 - factor_two) * dens_part + factor_one * normal_speed * norm_part + tangent_sum
        )
        shear_first = first_part - speed_first * dens_part
        shear_second = second_part - speed_second * dens_part
        wave_plus = 0.5 * (
            (factor_two - normal_speed * inv_sound) * dens_part
            - (factor_one * normal_speed - inv_sound) * norm_part
            - tangent_sum
        )
        return (wave_minus, entropy, shear_first, shear_second, wave_plus)

    state_chars = [project(cell_state) for cell_state in states]
    flux_chars = [project(cell_flux) for cell_flux in physical]
    recon = []
    for field_index in range(5):
        plus_vals = [
            0.5 * (flux_chars[cell][field_index] + dissipation * state_chars[cell][field_index])
            for cell in range(6)
        ]
        minus_vals = [
            0.5 * (flux_chars[cell][field_index] - dissipation * state_chars[cell][field_index])
            for cell in range(6)
        ]
        recon.append(
            weno_side(plus_vals[0], plus_vals[1], plus_vals[2], plus_vals[3], plus_vals[4])
            + weno_side(minus_vals[5], minus_vals[4], minus_vals[3], minus_vals[2], minus_vals[1])
        )
    wave_minus, entropy, shear_first, shear_second, wave_plus = recon
    acoustic = wave_minus + entropy + wave_plus
    parts = {}
    parts[0] = acoustic
    parts[normal] = (
        (normal_speed - sound) * wave_minus
        + normal_speed * entropy
        + (normal_speed + sound) * wave_plus
    )
    parts[first] = speed_first * acoustic + shear_first
    parts[second] = speed_second * acoustic + shear_second
    parts[4] = (
        (enthalpy - normal_speed * sound) * wave_minus
        + kinetic * entropy
        + speed_first * shear_first
        + speed_second * shear_second
        + (enthalpy + normal_speed * sound) * wave_plus
    )
    return jnp.stack([parts[index_part] for index_part in range(5)])


def divergence(padded, axis, count, normal, first, second):
    faces = face_flux(padded, euler_flux(padded, normal), axis, count, normal, first, second)
    return lax.slice_in_dim(faces, 1, count + 1, axis=axis) - lax.slice_in_dim(
        faces, 0, count, axis=axis
    )


def flip_radial(cells):
    turned = cells[:, :, ::-1]
    return jnp.concatenate([turned[:3], -turned[3:4], turned[4:]], axis=0)


def flip_theta(cells):
    return jnp.concatenate([cells[:2], -cells[2:3], cells[3:]], axis=0)


def facing_slabs(section_state):
    block_index = lax.axis_index("blk")
    block_count = lax.axis_size("blk")
    slab_count = lax.axis_size("tx") * lax.axis_size("tz")
    outgoing = jnp.where(block_index == 0, section_state[:, -3:], section_state[:, :3])
    outgoing = outgoing[..., ::-1]
    this_route = []
    next_route = []
    for blk_from in range(block_count):
        blk_to = (blk_from + 1) % block_count
        for slab_from in range(slab_count):
            source = blk_from * slab_count + slab_from
            this_route.append((source, blk_to * slab_count + slab_from))
            next_route.append((source, blk_to * slab_count + (slab_from - 1) % slab_count))
    axes = ("blk", "tx", "tz")
    return lax.ppermute(outgoing, axes, this_route), lax.ppermute(outgoing, axes, next_route)


def after(value, index):
    return index + jnp.isnan(value.reshape(-1)[0]).astype(jnp.int32)


def window_of(this_slab, next_slab, rotor_step, before):
    width = this_slab.shape[3]
    remainder = rotor_step[0] // 4 % width
    doubled = jnp.concatenate([next_slab, this_slab], axis=3)
    return lax.dynamic_slice_in_dim(doubled, width - 1 - remainder, width + 1, 3)


def route_parts(rotor_step, width):
    rows = lax.axis_size("tx")
    columns = lax.axis_size("tz")
    turns = rotor_step[0] // 4 // width
    centre = (turns - 1) % (rows * columns)
    return rows, columns, centre // columns, centre % columns


def pick_row(window, rotor_step, before):
    rows, columns, centre_row, centre_column = route_parts(rotor_step, window.shape[3] - 1)
    reader = (centre_column - lax.axis_index("tz")) % columns
    borrow = (reader > centre_column).astype(jnp.int32)
    source_row = (centre_row - lax.axis_index("tx") - borrow) % rows
    gathered = lax.all_gather(window, "tx")
    return lax.dynamic_index_in_dim(gathered, after(before, source_row), 0, keepdims=False)


def pick_column(chosen, rotor_step, before):
    rows, columns, centre_row, centre_column = route_parts(rotor_step, chosen.shape[3] - 1)
    source_column = (centre_column - lax.axis_index("tz")) % columns
    gathered = lax.all_gather(chosen, "tz")
    return lax.dynamic_index_in_dim(gathered, after(before, source_column), 0, keepdims=False)


def shards(base_state, section_state, rotor_step):
    planes = section_state.shape[1]
    bands = section_state.shape[2]
    width = section_state.shape[3]
    fraction = (rotor_step[0] % 4).astype(jnp.float32) / 4.0
    theta_padded = padded_2(section_state, ((("tx", "tz"), 3),), 3, True)
    radial_raw = padded_2(section_state, (("radial", 2),), 3, False)
    band_index = lax.axis_index("radial")
    band_count = lax.axis_size("radial")
    lower_wall = jnp.where(
        band_index == 0, flip_radial(section_state[:, :, :3]), radial_raw[:, :, :3]
    )
    upper_wall = jnp.where(
        band_index == band_count - 1, flip_radial(section_state[:, :, -3:]), radial_raw[:, :, -3:]
    )
    radial_padded = jnp.concatenate([lower_wall, section_state, upper_wall], axis=2)
    block_index = lax.axis_index("blk")
    front = block_index == 0
    this_slab, next_slab = facing_slabs(section_state)
    window = window_of(this_slab, next_slab, rotor_step, rotor_step)
    radial_padded = lax.dynamic_slice_in_dim(radial_padded, after(window, 0), 5, 0)
    radial = divergence(radial_padded, 2, bands, 3, 1, 2)
    chosen = pick_row(window, rotor_step, radial)
    azimuthal = divergence(theta_padded, 3, width, 2, 1, 3)
    edge_low = jnp.concatenate(
        [section_state[:, :1], section_state[:, :1], section_state[:, :1]], axis=1
    )
    edge_high = jnp.concatenate(
        [section_state[:, -1:], section_state[:, -1:], section_state[:, -1:]], axis=1
    )
    local_window = jnp.where(
        front,
        jnp.concatenate([edge_low, section_state], axis=1),
        jnp.concatenate([section_state, edge_high], axis=1),
    )
    local_window = lax.dynamic_slice_in_dim(local_window, after(chosen, 0), 5, 0)
    local_faces = face_flux(
        local_window, euler_flux(local_window, 1), 1, local_window.shape[1] - 6, 1, 2, 3
    )
    window = pick_column(chosen, rotor_step, local_faces)
    ghost = flip_theta(
        (1.0 - fraction) * window[..., 1 : width + 1] + fraction * window[..., :width]
    )
    mortar_window = jnp.where(
        front,
        jnp.concatenate([section_state[:, 1:], ghost], axis=1),
        jnp.concatenate([ghost, section_state[:, :-1]], axis=1),
    )
    mortar_faces = face_flux(
        mortar_window, euler_flux(mortar_window, 1), 1, mortar_window.shape[1] - 6, 1, 2, 3
    )
    faces = jnp.where(
        front,
        jnp.concatenate([local_faces, mortar_faces], axis=1),
        jnp.concatenate([mortar_faces, local_faces], axis=1),
    )
    axial = lax.slice_in_dim(faces, 1, planes + 1, axis=1) - lax.slice_in_dim(
        faces, 0, planes, axis=1
    )
    change = -step_ratio * (axial + radial + azimuthal)
    return 0.75 * base_state + 0.25 * (section_state + change)


def solution(mesh):
    blocks, slabs, bands = (mesh.shape[name] for name in ("blk", "theta", "radial"))
    rows = 4 if slabs % 4 == 0 else 1
    grid = jax.sharding.Mesh(
        mesh.devices.reshape(blocks, rows, slabs // rows, bands), ("blk", "tx", "tz", "radial")
    )
    in_specs = (P(None, "blk", "radial", ("tx", "tz")), P(None, "blk", "radial", ("tx", "tz")), P())
    out_specs = P(None, "blk", "radial", ("tx", "tz"))
    inner = jax.shard_map(shards, mesh=grid, in_specs=in_specs, out_specs=out_specs, check_vma=False)
    sharded = jax.sharding.NamedSharding(mesh, P(None, "blk", "radial", "theta"))

    def run(base_state, section_state, rotor_step):
        return jax.lax.with_sharding_constraint(
            inner(base_state, section_state, rotor_step), sharded
        )

    return run
```

```python
import jax
import jax.numpy as jnp
from jax import lax
from jax.sharding import PartitionSpec as P

gamma_ratio = 1.4
weno_epsilon = 1e-06
step_ratio = 0.12


def padded_2(cells, sides, width, closed):
    for axis, dim in sides:
        count = lax.axis_size(axis)
        ends = count if closed else count - 1
        head = lax.slice_in_dim(cells, 0, width, axis=dim)
        tail = lax.slice_in_dim(cells, cells.shape[dim] - width, cells.shape[dim], axis=dim)
        cells = jnp.concatenate(
            [
                lax.ppermute(tail, axis, [(i, (i + 1) % count) for i in range(ends)]),
                cells,
                lax.ppermute(head, axis, [((i + 1) % count, i) for i in range(ends)]),
            ],
            axis=dim,
        )
    return cells


def partner(block, axis, distance):
    count = lax.axis_size(axis)
    route = []
    for low in range(count):
        high = low | 1 << distance
        if high != low and high < count:
            route += [(low, high), (high, low)]
    return lax.ppermute(block, axis, route)


def pressure_of(state):
    kinetic = 0.5 * (jnp.square(state[1]) + jnp.square(state[2]) + jnp.square(state[3])) / state[0]
    return (gamma_ratio - 1.0) * (state[4] - kinetic)


def euler_flux(state, normal):
    pressure = pressure_of(state)
    velocity = state[normal] / state[0]
    flux = state * velocity[None]
    flux = flux.at[normal].add(pressure)
    flux = flux.at[4].add(pressure * velocity)
    return flux


def wave_speed(state, normal):
    pressure = pressure_of(state)
    return jnp.abs(state[normal] / state[0]) + jnp.sqrt(gamma_ratio * pressure / state[0])


def weno_side(far_left, left_cell, centre, right_cell, far_right):
    smooth_low = 13.0 / 12.0 * jnp.square(far_left - 2.0 * left_cell + centre) + 0.25 * jnp.square(
        far_left - 4.0 * left_cell + 3.0 * centre
    )
    smooth_mid = 13.0 / 12.0 * jnp.square(
        left_cell - 2.0 * centre + right_cell
    ) + 0.25 * jnp.square(left_cell - right_cell)
    smooth_high = 13.0 / 12.0 * jnp.square(
        centre - 2.0 * right_cell + far_right
    ) + 0.25 * jnp.square(3.0 * centre - 4.0 * right_cell + far_right)
    weight_low = 0.1 / jnp.square(weno_epsilon + smooth_low)
    weight_mid = 0.6 / jnp.square(weno_epsilon + smooth_mid)
    weight_high = 0.3 / jnp.square(weno_epsilon + smooth_high)
    guess_low = (2.0 * far_left - 7.0 * left_cell + 11.0 * centre) / 6.0
    guess_mid = (-left_cell + 5.0 * centre + 2.0 * right_cell) / 6.0
    guess_high = (2.0 * centre + 5.0 * right_cell - far_right) / 6.0
    return (weight_low * guess_low + weight_mid * guess_mid + weight_high * guess_high) / (
        weight_low + weight_mid + weight_high
    )


def face_flux(padded, fluxes, axis, count, normal, first, second):
    states = [
        lax.slice_in_dim(padded, shift_index, shift_index + count + 1, axis=axis)
        for shift_index in range(6)
    ]
    physical = [
        lax.slice_in_dim(fluxes, shift_index, shift_index + count + 1, axis=axis)
        for shift_index in range(6)
    ]
    mean = 0.5 * (states[2] + states[3])
    density = mean[0]
    normal_speed = mean[normal] / density
    speed_first = mean[first] / density
    speed_second = mean[second] / density
    kinetic = 0.5 * (jnp.square(normal_speed) + jnp.square(speed_first) + jnp.square(speed_second))
    pressure = pressure_of(mean)
    sound = jnp.sqrt(gamma_ratio * pressure / density)
    enthalpy = (mean[4] + pressure) / density
    inv_sound = 1.0 / sound
    factor_one = (gamma_ratio - 1.0) * jnp.square(inv_sound)
    factor_two = factor_one * kinetic
    dissipation = jnp.maximum(wave_speed(states[2], normal), wave_speed(states[3], normal))

    def project(vector):
        dens_part = vector[0]
        norm_part = vector[normal]
        first_part = vector[first]
        second_part = vector[second]
        energy_part = vector[4]
        tangent_sum = factor_one * (
            speed_first * first_part + speed_second * second_part - energy_part
        )
        wave_minus = 0.5 * (
            (factor_two + normal_speed * inv_sound) * dens_part
            - (factor_one * normal_speed + inv_sound) * norm_part
            - tangent_sum
        )
        entropy = (
            (1.0 - factor_two) * dens_part + factor_one * normal_speed * norm_part + tangent_sum
        )
        shear_first = first_part - speed_first * dens_part
        shear_second = second_part - speed_second * dens_part
        wave_plus = 0.5 * (
            (factor_two - normal_speed * inv_sound) * dens_part
            - (factor_one * normal_speed - inv_sound) * norm_part
            - tangent_sum
        )
        return (wave_minus, entropy, shear_first, shear_second, wave_plus)

    state_chars = [project(cell_state) for cell_state in states]
    flux_chars = [project(cell_flux) for cell_flux in physical]
    recon = []
    for field_index in range(5):
        plus_vals = [
            0.5 * (flux_chars[cell][field_index] + dissipation * state_chars[cell][field_index])
            for cell in range(6)
        ]
        minus_vals = [
            0.5 * (flux_chars[cell][field_index] - dissipation * state_chars[cell][field_index])
            for cell in range(6)
        ]
        recon.append(
            weno_side(plus_vals[0], plus_vals[1], plus_vals[2], plus_vals[3], plus_vals[4])
            + weno_side(minus_vals[5], minus_vals[4], minus_vals[3], minus_vals[2], minus_vals[1])
        )
    wave_minus, entropy, shear_first, shear_second, wave_plus = recon
    acoustic = wave_minus + entropy + wave_plus
    parts = {}
    parts[0] = acoustic
    parts[normal] = (
        (normal_speed - sound) * wave_minus
        + normal_speed * entropy
        + (normal_speed + sound) * wave_plus
    )
    parts[first] = speed_first * acoustic + shear_first
    parts[second] = speed_second * acoustic + shear_second
    parts[4] = (
        (enthalpy - normal_speed * sound) * wave_minus
        + kinetic * entropy
        + speed_first * shear_first
        + speed_second * shear_second
        + (enthalpy + normal_speed * sound) * wave_plus
    )
    return jnp.stack([parts[index_part] for index_part in range(5)])


def divergence(padded, axis, count, normal, first, second):
    faces = face_flux(padded, euler_flux(padded, normal), axis, count, normal, first, second)
    return lax.slice_in_dim(faces, 1, count + 1, axis=axis) - lax.slice_in_dim(
        faces, 0, count, axis=axis
    )


def flip_radial(cells):
    turned = cells[:, :, ::-1]
    return jnp.concatenate([turned[:3], -turned[3:4], turned[4:]], axis=0)


def flip_theta(cells):
    return jnp.concatenate([cells[:2], -cells[2:3], cells[3:]], axis=0)


def facing_slabs(section_state):
    block_index = lax.axis_index("blk")
    block_count = lax.axis_size("blk")
    slab_count = lax.axis_size("tx") * lax.axis_size("tz")
    outgoing = jnp.where(block_index == 0, section_state[:, -3:], section_state[:, :3])
    outgoing = outgoing[..., ::-1]
    this_route = []
    next_route = []
    for blk_from in range(block_count):
        blk_to = (blk_from + 1) % block_count
        for slab_from in range(slab_count):
            source = blk_from * slab_count + slab_from
            this_route.append((source, blk_to * slab_count + slab_from))
            next_route.append((source, blk_to * slab_count + (slab_from - 1) % slab_count))
    axes = ("blk", "tx", "tz")
    return lax.ppermute(outgoing, axes, this_route), lax.ppermute(outgoing, axes, next_route)


def after(value, index):
    return index + jnp.isnan(value.reshape(-1)[0]).astype(jnp.int32)


def window_of(this_slab, next_slab, rotor_step, before):
    width = this_slab.shape[3]
    remainder = rotor_step[0] // 4 % width
    doubled = jnp.concatenate([next_slab, this_slab], axis=3)
    return lax.dynamic_slice_in_dim(doubled, width - 1 - remainder, width + 1, 3)


def route_parts(rotor_step, width):
    rows = lax.axis_size("tx")
    columns = lax.axis_size("tz")
    turns = rotor_step[0] // 4 // width
    centre = (turns - 1) % (rows * columns)
    return rows, columns, centre // columns, centre % columns


def pick_row(window, rotor_step, before):
    rows, columns, centre_row, centre_column = route_parts(rotor_step, window.shape[3] - 1)
    reader = (centre_column - lax.axis_index("tz")) % columns
    borrow = (reader > centre_column).astype(jnp.int32)
    source_row = (centre_row - lax.axis_index("tx") - borrow) % rows
    gathered = lax.all_gather(window, "tx")
    return lax.dynamic_index_in_dim(gathered, after(before, source_row), 0, keepdims=False)


def pick_column(chosen, rotor_step, before):
    rows, columns, centre_row, centre_column = route_parts(rotor_step, chosen.shape[3] - 1)
    source_column = (centre_column - lax.axis_index("tz")) % columns
    gathered = lax.all_gather(chosen, "tz")
    return lax.dynamic_index_in_dim(gathered, after(before, source_column), 0, keepdims=False)


def shards(base_state, section_state, rotor_step):
    planes = section_state.shape[1]
    bands = section_state.shape[2]
    width = section_state.shape[3]
    fraction = (rotor_step[0] % 4).astype(jnp.float32) / 4.0
    theta_padded = padded_2(section_state, ((("tx", "tz"), 3),), 3, True)
    radial_raw = padded_2(section_state, (("radial", 2),), 3, False)
    band_index = lax.axis_index("radial")
    band_count = lax.axis_size("radial")
    lower_wall = jnp.where(
        band_index == 0, flip_radial(section_state[:, :, :3]), radial_raw[:, :, :3]
    )
    upper_wall = jnp.where(
        band_index == band_count - 1, flip_radial(section_state[:, :, -3:]), radial_raw[:, :, -3:]
    )
    radial_padded = jnp.concatenate([lower_wall, section_state, upper_wall], axis=2)
    block_index = lax.axis_index("blk")
    front = block_index == 0
    this_slab, next_slab = facing_slabs(section_state)
    window = window_of(this_slab, next_slab, rotor_step, rotor_step)
    radial_padded = lax.dynamic_slice_in_dim(radial_padded, after(window, 0), 5, 0)
    radial = divergence(radial_padded, 2, bands, 3, 1, 2)
    chosen = pick_row(window, rotor_step, radial)
    theta_padded = lax.dynamic_slice_in_dim(theta_padded, after(chosen, 0), 5, 0)
    azimuthal = divergence(theta_padded, 3, width, 2, 1, 3)
    edge_low = jnp.concatenate(
        [section_state[:, :1], section_state[:, :1], section_state[:, :1]], axis=1
    )
    edge_high = jnp.concatenate(
        [section_state[:, -1:], section_state[:, -1:], section_state[:, -1:]], axis=1
    )
    local_window = jnp.where(
        front,
        jnp.concatenate([edge_low, section_state], axis=1),
        jnp.concatenate([section_state, edge_high], axis=1),
    )
    local_window = lax.dynamic_slice_in_dim(local_window, after(chosen, 0), 5, 0)
    local_faces = face_flux(
        local_window, euler_flux(local_window, 1), 1, local_window.shape[1] - 6, 1, 2, 3
    )
    window = pick_column(chosen, rotor_step, local_faces + azimuthal[:, :1, :, :1])
    ghost = flip_theta(
        (1.0 - fraction) * window[..., 1 : width + 1] + fraction * window[..., :width]
    )
    mortar_window = jnp.where(
        front,
        jnp.concatenate([section_state[:, 1:], ghost], axis=1),
        jnp.concatenate([ghost, section_state[:, :-1]], axis=1),
    )
    mortar_faces = face_flux(
        mortar_window, euler_flux(mortar_window, 1), 1, mortar_window.shape[1] - 6, 1, 2, 3
    )
    faces = jnp.where(
        front,
        jnp.concatenate([local_faces, mortar_faces], axis=1),
        jnp.concatenate([mortar_faces, local_faces], axis=1),
    )
    axial = lax.slice_in_dim(faces, 1, planes + 1, axis=1) - lax.slice_in_dim(
        faces, 0, planes, axis=1
    )
    change = -step_ratio * (axial + radial + azimuthal)
    return 0.75 * base_state + 0.25 * (section_state + change)


def solution(mesh):
    blocks, slabs, bands = (mesh.shape[name] for name in ("blk", "theta", "radial"))
    rows = 4 if slabs % 4 == 0 else 1
    grid = jax.sharding.Mesh(
        mesh.devices.reshape(blocks, rows, slabs // rows, bands), ("blk", "tx", "tz", "radial")
    )
    in_specs = (P(None, "blk", "radial", ("tx", "tz")), P(None, "blk", "radial", ("tx", "tz")), P())
    out_specs = P(None, "blk", "radial", ("tx", "tz"))
    inner = jax.shard_map(shards, mesh=grid, in_specs=in_specs, out_specs=out_specs, check_vma=False)
    sharded = jax.sharding.NamedSharding(mesh, P(None, "blk", "radial", "theta"))

    def run(base_state, section_state, rotor_step):
        return jax.lax.with_sharding_constraint(
            inner(base_state, section_state, rotor_step), sharded
        )

    return run
```

```python
import jax
import jax.numpy as jnp
from jax import lax
from jax.sharding import PartitionSpec as P

gamma_ratio = 1.4
weno_epsilon = 1e-06
step_ratio = 0.12


def padded_2(cells, sides, width, closed):
    for axis, dim in sides:
        count = lax.axis_size(axis)
        ends = count if closed else count - 1
        head = lax.slice_in_dim(cells, 0, width, axis=dim)
        tail = lax.slice_in_dim(cells, cells.shape[dim] - width, cells.shape[dim], axis=dim)
        cells = jnp.concatenate(
            [
                lax.ppermute(tail, axis, [(i, (i + 1) % count) for i in range(ends)]),
                cells,
                lax.ppermute(head, axis, [((i + 1) % count, i) for i in range(ends)]),
            ],
            axis=dim,
        )
    return cells


def partner(block, axis, distance):
    count = lax.axis_size(axis)
    route = []
    for low in range(count):
        high = low | 1 << distance
        if high != low and high < count:
            route += [(low, high), (high, low)]
    return lax.ppermute(block, axis, route)


def pressure_of(state):
    kinetic = 0.5 * (jnp.square(state[1]) + jnp.square(state[2]) + jnp.square(state[3])) / state[0]
    return (gamma_ratio - 1.0) * (state[4] - kinetic)


def euler_flux(state, normal):
    pressure = pressure_of(state)
    velocity = state[normal] / state[0]
    flux = state * velocity[None]
    flux = flux.at[normal].add(pressure)
    flux = flux.at[4].add(pressure * velocity)
    return flux


def wave_speed(state, normal):
    pressure = pressure_of(state)
    return jnp.abs(state[normal] / state[0]) + jnp.sqrt(gamma_ratio * pressure / state[0])


def weno_side(far_left, left_cell, centre, right_cell, far_right):
    smooth_low = 13.0 / 12.0 * jnp.square(far_left - 2.0 * left_cell + centre) + 0.25 * jnp.square(
        far_left - 4.0 * left_cell + 3.0 * centre
    )
    smooth_mid = 13.0 / 12.0 * jnp.square(
        left_cell - 2.0 * centre + right_cell
    ) + 0.25 * jnp.square(left_cell - right_cell)
    smooth_high = 13.0 / 12.0 * jnp.square(
        centre - 2.0 * right_cell + far_right
    ) + 0.25 * jnp.square(3.0 * centre - 4.0 * right_cell + far_right)
    weight_low = 0.1 / jnp.square(weno_epsilon + smooth_low)
    weight_mid = 0.6 / jnp.square(weno_epsilon + smooth_mid)
    weight_high = 0.3 / jnp.square(weno_epsilon + smooth_high)
    guess_low = (2.0 * far_left - 7.0 * left_cell + 11.0 * centre) / 6.0
    guess_mid = (-left_cell + 5.0 * centre + 2.0 * right_cell) / 6.0
    guess_high = (2.0 * centre + 5.0 * right_cell - far_right) / 6.0
    return (weight_low * guess_low + weight_mid * guess_mid + weight_high * guess_high) / (
        weight_low + weight_mid + weight_high
    )


def face_flux(padded, fluxes, axis, count, normal, first, second):
    states = [
        lax.slice_in_dim(padded, shift_index, shift_index + count + 1, axis=axis)
        for shift_index in range(6)
    ]
    physical = [
        lax.slice_in_dim(fluxes, shift_index, shift_index + count + 1, axis=axis)
        for shift_index in range(6)
    ]
    mean = 0.5 * (states[2] + states[3])
    density = mean[0]
    normal_speed = mean[normal] / density
    speed_first = mean[first] / density
    speed_second = mean[second] / density
    kinetic = 0.5 * (jnp.square(normal_speed) + jnp.square(speed_first) + jnp.square(speed_second))
    pressure = pressure_of(mean)
    sound = jnp.sqrt(gamma_ratio * pressure / density)
    enthalpy = (mean[4] + pressure) / density
    inv_sound = 1.0 / sound
    factor_one = (gamma_ratio - 1.0) * jnp.square(inv_sound)
    factor_two = factor_one * kinetic
    dissipation = jnp.maximum(wave_speed(states[2], normal), wave_speed(states[3], normal))

    def project(vector):
        dens_part = vector[0]
        norm_part = vector[normal]
        first_part = vector[first]
        second_part = vector[second]
        energy_part = vector[4]
        tangent_sum = factor_one * (
            speed_first * first_part + speed_second * second_part - energy_part
        )
        wave_minus = 0.5 * (
            (factor_two + normal_speed * inv_sound) * dens_part
            - (factor_one * normal_speed + inv_sound) * norm_part
            - tangent_sum
        )
        entropy = (
            (1.0 - factor_two) * dens_part + factor_one * normal_speed * norm_part + tangent_sum
        )
        shear_first = first_part - speed_first * dens_part
        shear_second = second_part - speed_second * dens_part
        wave_plus = 0.5 * (
            (factor_two - normal_speed * inv_sound) * dens_part
            - (factor_one * normal_speed - inv_sound) * norm_part
            - tangent_sum
        )
        return (wave_minus, entropy, shear_first, shear_second, wave_plus)

    state_chars = [project(cell_state) for cell_state in states]
    flux_chars = [project(cell_flux) for cell_flux in physical]
    recon = []
    for field_index in range(5):
        plus_vals = [
            0.5 * (flux_chars[cell][field_index] + dissipation * state_chars[cell][field_index])
            for cell in range(6)
        ]
        minus_vals = [
            0.5 * (flux_chars[cell][field_index] - dissipation * state_chars[cell][field_index])
            for cell in range(6)
        ]
        recon.append(
            weno_side(plus_vals[0], plus_vals[1], plus_vals[2], plus_vals[3], plus_vals[4])
            + weno_side(minus_vals[5], minus_vals[4], minus_vals[3], minus_vals[2], minus_vals[1])
        )
    wave_minus, entropy, shear_first, shear_second, wave_plus = recon
    acoustic = wave_minus + entropy + wave_plus
    parts = {}
    parts[0] = acoustic
    parts[normal] = (
        (normal_speed - sound) * wave_minus
        + normal_speed * entropy
        + (normal_speed + sound) * wave_plus
    )
    parts[first] = speed_first * acoustic + shear_first
    parts[second] = speed_second * acoustic + shear_second
    parts[4] = (
        (enthalpy - normal_speed * sound) * wave_minus
        + kinetic * entropy
        + speed_first * shear_first
        + speed_second * shear_second
        + (enthalpy + normal_speed * sound) * wave_plus
    )
    return jnp.stack([parts[index_part] for index_part in range(5)])


def divergence(padded, axis, count, normal, first, second):
    faces = face_flux(padded, euler_flux(padded, normal), axis, count, normal, first, second)
    return lax.slice_in_dim(faces, 1, count + 1, axis=axis) - lax.slice_in_dim(
        faces, 0, count, axis=axis
    )


def flip_radial(cells):
    turned = cells[:, :, ::-1]
    return jnp.concatenate([turned[:3], -turned[3:4], turned[4:]], axis=0)


def flip_theta(cells):
    return jnp.concatenate([cells[:2], -cells[2:3], cells[3:]], axis=0)


def facing_slabs(section_state):
    block_index = lax.axis_index("blk")
    block_count = lax.axis_size("blk")
    slab_count = lax.axis_size("tx") * lax.axis_size("tz")
    outgoing = jnp.where(block_index == 0, section_state[:, -3:], section_state[:, :3])
    outgoing = outgoing[..., ::-1]
    this_route = []
    next_route = []
    for blk_from in range(block_count):
        blk_to = (blk_from + 1) % block_count
        for slab_from in range(slab_count):
            source = blk_from * slab_count + slab_from
            this_route.append((source, blk_to * slab_count + slab_from))
            next_route.append((source, blk_to * slab_count + (slab_from - 1) % slab_count))
    axes = ("blk", "tx", "tz")
    return lax.ppermute(outgoing, axes, this_route), lax.ppermute(outgoing, axes, next_route)


def after(value, index):
    return index + jnp.isnan(value.reshape(-1)[0]).astype(jnp.int32)


def hold(cells, value):
    return jnp.where(jnp.isnan(value.reshape(-1)[0]), jnp.zeros((), cells.dtype), cells)


def window_of(this_slab, next_slab, rotor_step, before):
    width = this_slab.shape[3]
    remainder = rotor_step[0] // 4 % width
    doubled = jnp.concatenate([next_slab, this_slab], axis=3)
    return lax.dynamic_slice_in_dim(doubled, width - 1 - remainder, width + 1, 3)


def route_parts(rotor_step, width):
    rows = lax.axis_size("tx")
    columns = lax.axis_size("tz")
    turns = rotor_step[0] // 4 // width
    centre = (turns - 1) % (rows * columns)
    return rows, columns, centre // columns, centre % columns


def pick_row(window, rotor_step, before):
    rows, columns, centre_row, centre_column = route_parts(rotor_step, window.shape[3] - 1)
    reader = (centre_column - lax.axis_index("tz")) % columns
    borrow = (reader > centre_column).astype(jnp.int32)
    source_row = (centre_row - lax.axis_index("tx") - borrow) % rows
    gathered = lax.all_gather(window, "tx")
    return lax.dynamic_index_in_dim(gathered, after(before, source_row), 0, keepdims=False)


def pick_column(chosen, rotor_step, before):
    rows, columns, centre_row, centre_column = route_parts(rotor_step, chosen.shape[3] - 1)
    source_column = (centre_column - lax.axis_index("tz")) % columns
    gathered = lax.all_gather(chosen, "tz")
    return lax.dynamic_index_in_dim(gathered, after(before, source_column), 0, keepdims=False)


def shards(base_state, section_state, rotor_step):
    planes = section_state.shape[1]
    bands = section_state.shape[2]
    width = section_state.shape[3]
    fraction = (rotor_step[0] % 4).astype(jnp.float32) / 4.0
    theta_padded = padded_2(section_state, ((("tx", "tz"), 3),), 3, True)
    radial_raw = padded_2(section_state, (("radial", 2),), 3, False)
    band_index = lax.axis_index("radial")
    band_count = lax.axis_size("radial")
    lower_wall = jnp.where(
        band_index == 0, flip_radial(section_state[:, :, :3]), radial_raw[:, :, :3]
    )
    upper_wall = jnp.where(
        band_index == band_count - 1, flip_radial(section_state[:, :, -3:]), radial_raw[:, :, -3:]
    )
    radial_padded = jnp.concatenate([lower_wall, section_state, upper_wall], axis=2)
    block_index = lax.axis_index("blk")
    front = block_index == 0
    this_slab, next_slab = facing_slabs(section_state)
    window = window_of(this_slab, next_slab, rotor_step, rotor_step)
    radial_padded = hold(radial_padded, window)
    radial = divergence(radial_padded, 2, bands, 3, 1, 2)
    chosen = pick_row(window, rotor_step, radial)
    theta_padded = hold(theta_padded, chosen)
    azimuthal = divergence(theta_padded, 3, width, 2, 1, 3)
    edge_low = jnp.concatenate(
        [section_state[:, :1], section_state[:, :1], section_state[:, :1]], axis=1
    )
    edge_high = jnp.concatenate(
        [section_state[:, -1:], section_state[:, -1:], section_state[:, -1:]], axis=1
    )
    local_window = jnp.where(
        front,
        jnp.concatenate([edge_low, section_state], axis=1),
        jnp.concatenate([section_state, edge_high], axis=1),
    )
    local_window = hold(local_window, chosen)
    local_faces = face_flux(
        local_window, euler_flux(local_window, 1), 1, local_window.shape[1] - 6, 1, 2, 3
    )
    window = pick_column(chosen, rotor_step, local_faces + azimuthal[:, :1, :, :1])
    ghost = flip_theta(
        (1.0 - fraction) * window[..., 1 : width + 1] + fraction * window[..., :width]
    )
    mortar_window = jnp.where(
        front,
        jnp.concatenate([section_state[:, 1:], ghost], axis=1),
        jnp.concatenate([ghost, section_state[:, :-1]], axis=1),
    )
    mortar_faces = face_flux(
        mortar_window, euler_flux(mortar_window, 1), 1, mortar_window.shape[1] - 6, 1, 2, 3
    )
    faces = jnp.where(
        front,
        jnp.concatenate([local_faces, mortar_faces], axis=1),
        jnp.concatenate([mortar_faces, local_faces], axis=1),
    )
    axial = lax.slice_in_dim(faces, 1, planes + 1, axis=1) - lax.slice_in_dim(
        faces, 0, planes, axis=1
    )
    change = -step_ratio * (axial + radial + azimuthal)
    return 0.75 * base_state + 0.25 * (section_state + change)


def solution(mesh):
    blocks, slabs, bands = (mesh.shape[name] for name in ("blk", "theta", "radial"))
    rows = 4 if slabs % 4 == 0 else 1
    grid = jax.sharding.Mesh(
        mesh.devices.reshape(blocks, rows, slabs // rows, bands), ("blk", "tx", "tz", "radial")
    )
    in_specs = (P(None, "blk", "radial", ("tx", "tz")), P(None, "blk", "radial", ("tx", "tz")), P())
    out_specs = P(None, "blk", "radial", ("tx", "tz"))
    inner = jax.shard_map(shards, mesh=grid, in_specs=in_specs, out_specs=out_specs, check_vma=False)
    sharded = jax.sharding.NamedSharding(mesh, P(None, "blk", "radial", "theta"))

    def run(base_state, section_state, rotor_step):
        return jax.lax.with_sharding_constraint(
            inner(base_state, section_state, rotor_step), sharded
        )

    return run
```

```python
import jax
import jax.numpy as jnp
from jax import lax
from jax.sharding import PartitionSpec as P

gamma_ratio = 1.4
weno_epsilon = 1e-06
step_ratio = 0.12


def padded_2(cells, sides, width, closed):
    for axis, dim in sides:
        count = lax.axis_size(axis)
        ends = count if closed else count - 1
        head = lax.slice_in_dim(cells, 0, width, axis=dim)
        tail = lax.slice_in_dim(cells, cells.shape[dim] - width, cells.shape[dim], axis=dim)
        cells = jnp.concatenate(
            [
                lax.ppermute(tail, axis, [(i, (i + 1) % count) for i in range(ends)]),
                cells,
                lax.ppermute(head, axis, [((i + 1) % count, i) for i in range(ends)]),
            ],
            axis=dim,
        )
    return cells


def partner(block, axis, distance):
    count = lax.axis_size(axis)
    route = []
    for low in range(count):
        high = low | 1 << distance
        if high != low and high < count:
            route += [(low, high), (high, low)]
    return lax.ppermute(block, axis, route)


def pressure_of(state):
    kinetic = 0.5 * (jnp.square(state[1]) + jnp.square(state[2]) + jnp.square(state[3])) / state[0]
    return (gamma_ratio - 1.0) * (state[4] - kinetic)


def euler_flux(state, normal):
    pressure = pressure_of(state)
    velocity = state[normal] / state[0]
    flux = state * velocity[None]
    flux = flux.at[normal].add(pressure)
    flux = flux.at[4].add(pressure * velocity)
    return flux


def wave_speed(state, normal):
    pressure = pressure_of(state)
    return jnp.abs(state[normal] / state[0]) + jnp.sqrt(gamma_ratio * pressure / state[0])


def weno_side(far_left, left_cell, centre, right_cell, far_right):
    smooth_low = 13.0 / 12.0 * jnp.square(far_left - 2.0 * left_cell + centre) + 0.25 * jnp.square(
        far_left - 4.0 * left_cell + 3.0 * centre
    )
    smooth_mid = 13.0 / 12.0 * jnp.square(
        left_cell - 2.0 * centre + right_cell
    ) + 0.25 * jnp.square(left_cell - right_cell)
    smooth_high = 13.0 / 12.0 * jnp.square(
        centre - 2.0 * right_cell + far_right
    ) + 0.25 * jnp.square(3.0 * centre - 4.0 * right_cell + far_right)
    weight_low = 0.1 / jnp.square(weno_epsilon + smooth_low)
    weight_mid = 0.6 / jnp.square(weno_epsilon + smooth_mid)
    weight_high = 0.3 / jnp.square(weno_epsilon + smooth_high)
    guess_low = (2.0 * far_left - 7.0 * left_cell + 11.0 * centre) / 6.0
    guess_mid = (-left_cell + 5.0 * centre + 2.0 * right_cell) / 6.0
    guess_high = (2.0 * centre + 5.0 * right_cell - far_right) / 6.0
    return (weight_low * guess_low + weight_mid * guess_mid + weight_high * guess_high) / (
        weight_low + weight_mid + weight_high
    )


def face_flux(padded, fluxes, axis, count, normal, first, second):
    states = [
        lax.slice_in_dim(padded, shift_index, shift_index + count + 1, axis=axis)
        for shift_index in range(6)
    ]
    physical = [
        lax.slice_in_dim(fluxes, shift_index, shift_index + count + 1, axis=axis)
        for shift_index in range(6)
    ]
    mean = 0.5 * (states[2] + states[3])
    density = mean[0]
    normal_speed = mean[normal] / density
    speed_first = mean[first] / density
    speed_second = mean[second] / density
    kinetic = 0.5 * (jnp.square(normal_speed) + jnp.square(speed_first) + jnp.square(speed_second))
    pressure = pressure_of(mean)
    sound = jnp.sqrt(gamma_ratio * pressure / density)
    enthalpy = (mean[4] + pressure) / density
    inv_sound = 1.0 / sound
    factor_one = (gamma_ratio - 1.0) * jnp.square(inv_sound)
    factor_two = factor_one * kinetic
    dissipation = jnp.maximum(wave_speed(states[2], normal), wave_speed(states[3], normal))

    def project(vector):
        dens_part = vector[0]
        norm_part = vector[normal]
        first_part = vector[first]
        second_part = vector[second]
        energy_part = vector[4]
        tangent_sum = factor_one * (
            speed_first * first_part + speed_second * second_part - energy_part
        )
        wave_minus = 0.5 * (
            (factor_two + normal_speed * inv_sound) * dens_part
            - (factor_one * normal_speed + inv_sound) * norm_part
            - tangent_sum
        )
        entropy = (
            (1.0 - factor_two) * dens_part + factor_one * normal_speed * norm_part + tangent_sum
        )
        shear_first = first_part - speed_first * dens_part
        shear_second = second_part - speed_second * dens_part
        wave_plus = 0.5 * (
            (factor_two - normal_speed * inv_sound) * dens_part
            - (factor_one * normal_speed - inv_sound) * norm_part
            - tangent_sum
        )
        return (wave_minus, entropy, shear_first, shear_second, wave_plus)

    state_chars = [project(cell_state) for cell_state in states]
    flux_chars = [project(cell_flux) for cell_flux in physical]
    recon = []
    for field_index in range(5):
        plus_vals = [
            0.5 * (flux_chars[cell][field_index] + dissipation * state_chars[cell][field_index])
            for cell in range(6)
        ]
        minus_vals = [
            0.5 * (flux_chars[cell][field_index] - dissipation * state_chars[cell][field_index])
            for cell in range(6)
        ]
        recon.append(
            weno_side(plus_vals[0], plus_vals[1], plus_vals[2], plus_vals[3], plus_vals[4])
            + weno_side(minus_vals[5], minus_vals[4], minus_vals[3], minus_vals[2], minus_vals[1])
        )
    wave_minus, entropy, shear_first, shear_second, wave_plus = recon
    acoustic = wave_minus + entropy + wave_plus
    parts = {}
    parts[0] = acoustic
    parts[normal] = (
        (normal_speed - sound) * wave_minus
        + normal_speed * entropy
        + (normal_speed + sound) * wave_plus
    )
    parts[first] = speed_first * acoustic + shear_first
    parts[second] = speed_second * acoustic + shear_second
    parts[4] = (
        (enthalpy - normal_speed * sound) * wave_minus
        + kinetic * entropy
        + speed_first * shear_first
        + speed_second * shear_second
        + (enthalpy + normal_speed * sound) * wave_plus
    )
    return jnp.stack([parts[index_part] for index_part in range(5)])


def divergence(padded, axis, count, normal, first, second):
    faces = face_flux(padded, euler_flux(padded, normal), axis, count, normal, first, second)
    return lax.slice_in_dim(faces, 1, count + 1, axis=axis) - lax.slice_in_dim(
        faces, 0, count, axis=axis
    )


def flip_radial(cells):
    turned = cells[:, :, ::-1]
    return jnp.concatenate([turned[:3], -turned[3:4], turned[4:]], axis=0)


def flip_theta(cells):
    return jnp.concatenate([cells[:2], -cells[2:3], cells[3:]], axis=0)


def hold(cells, value):
    return jnp.where(jnp.isnan(value.reshape(-1)[0]), jnp.zeros((), cells.dtype), cells)


def after(value, index):
    return index + jnp.isnan(value.reshape(-1)[0]).astype(jnp.int32)


def route_parts(rotor_step, width):
    rows = lax.axis_size("tx")
    columns = lax.axis_size("tz")
    turns = rotor_step[0] // 4 // width
    centre = (turns - 1) % (rows * columns)
    return rows, columns, centre // columns, centre % columns


def pick_column(slab, rotor_step, before):
    rows, columns, centre_row, centre_column = route_parts(rotor_step, slab.shape[3])
    source_column = (centre_column - lax.axis_index("tz")) % columns
    gathered = lax.all_gather(slab, "tz")
    return lax.dynamic_index_in_dim(gathered, after(before, source_column), 0, keepdims=False)


def pick_row(slab, rotor_step, before):
    rows, columns, centre_row, centre_column = route_parts(rotor_step, slab.shape[3])
    borrow = (lax.axis_index("tz") > centre_column).astype(jnp.int32)
    source_row = (centre_row - lax.axis_index("tx") - borrow) % rows
    gathered = lax.all_gather(slab, "tx")
    return lax.dynamic_index_in_dim(gathered, after(before, source_row), 0, keepdims=False)


def cross_blocks(slab):
    block_count = lax.axis_size("blk")
    slab_count = lax.axis_size("tx") * lax.axis_size("tz")
    this_route = []
    next_route = []
    for blk_from in range(block_count):
        blk_to = (blk_from + 1) % block_count
        for slab_from in range(slab_count):
            source = blk_from * slab_count + slab_from
            this_route.append((source, blk_to * slab_count + slab_from))
            next_route.append((source, blk_to * slab_count + (slab_from + 1) % slab_count))
    axes = ("blk", "tx", "tz")
    return lax.ppermute(slab, axes, this_route), lax.ppermute(slab, axes, next_route)


def window_of(this_slab, next_slab, rotor_step, before):
    width = this_slab.shape[3]
    remainder = after(before, rotor_step[0] // 4 % width)
    doubled = jnp.concatenate([next_slab, this_slab], axis=3)
    return lax.dynamic_slice_in_dim(doubled, width - 1 - remainder, width + 1, 3)


def shards(base_state, section_state, rotor_step):
    planes = section_state.shape[1]
    bands = section_state.shape[2]
    width = section_state.shape[3]
    fraction = (rotor_step[0] % 4).astype(jnp.float32) / 4.0
    theta_padded = padded_2(section_state, ((("tx", "tz"), 3),), 3, True)
    radial_raw = padded_2(section_state, (("radial", 2),), 3, False)
    band_index = lax.axis_index("radial")
    band_count = lax.axis_size("radial")
    lower_wall = jnp.where(
        band_index == 0, flip_radial(section_state[:, :, :3]), radial_raw[:, :, :3]
    )
    upper_wall = jnp.where(
        band_index == band_count - 1, flip_radial(section_state[:, :, -3:]), radial_raw[:, :, -3:]
    )
    radial_padded = jnp.concatenate([lower_wall, section_state, upper_wall], axis=2)
    block_index = lax.axis_index("blk")
    front = block_index == 0
    outgoing = jnp.where(front, section_state[:, -3:], section_state[:, :3])[..., ::-1]
    radial = divergence(radial_padded, 2, bands, 3, 1, 2)
    chosen = pick_column(outgoing, rotor_step, radial)
    theta_padded = hold(theta_padded, chosen)
    azimuthal = divergence(theta_padded, 3, width, 2, 1, 3)
    chosen = pick_row(chosen, rotor_step, azimuthal)
    this_slab, next_slab = cross_blocks(chosen)
    edge_low = jnp.concatenate(
        [section_state[:, :1], section_state[:, :1], section_state[:, :1]], axis=1
    )
    edge_high = jnp.concatenate(
        [section_state[:, -1:], section_state[:, -1:], section_state[:, -1:]], axis=1
    )
    local_window = jnp.where(
        front,
        jnp.concatenate([edge_low, section_state], axis=1),
        jnp.concatenate([section_state, edge_high], axis=1),
    )
    local_window = hold(local_window, chosen)
    local_faces = face_flux(
        local_window, euler_flux(local_window, 1), 1, local_window.shape[1] - 6, 1, 2, 3
    )
    window = window_of(this_slab, next_slab, rotor_step, local_faces)
    ghost = flip_theta(
        (1.0 - fraction) * window[..., 1 : width + 1] + fraction * window[..., :width]
    )
    mortar_window = jnp.where(
        front,
        jnp.concatenate([section_state[:, 1:], ghost], axis=1),
        jnp.concatenate([ghost, section_state[:, :-1]], axis=1),
    )
    mortar_faces = face_flux(
        mortar_window, euler_flux(mortar_window, 1), 1, mortar_window.shape[1] - 6, 1, 2, 3
    )
    faces = jnp.where(
        front,
        jnp.concatenate([local_faces, mortar_faces], axis=1),
        jnp.concatenate([mortar_faces, local_faces], axis=1),
    )
    axial = lax.slice_in_dim(faces, 1, planes + 1, axis=1) - lax.slice_in_dim(
        faces, 0, planes, axis=1
    )
    change = -step_ratio * (axial + radial + azimuthal)
    return 0.75 * base_state + 0.25 * (section_state + change)


def solution(mesh):
    blocks, slabs, bands = (mesh.shape[name] for name in ("blk", "theta", "radial"))
    rows = 4 if slabs % 4 == 0 else 1
    grid = jax.sharding.Mesh(
        mesh.devices.reshape(blocks, rows, slabs // rows, bands), ("blk", "tx", "tz", "radial")
    )
    in_specs = (P(None, "blk", "radial", ("tx", "tz")), P(None, "blk", "radial", ("tx", "tz")), P())
    out_specs = P(None, "blk", "radial", ("tx", "tz"))
    inner = jax.shard_map(shards, mesh=grid, in_specs=in_specs, out_specs=out_specs, check_vma=False)
    sharded = jax.sharding.NamedSharding(mesh, P(None, "blk", "radial", "theta"))

    def run(base_state, section_state, rotor_step):
        return jax.lax.with_sharding_constraint(
            inner(base_state, section_state, rotor_step), sharded
        )

    return run
```

```python
import jax
import jax.numpy as jnp
from jax import lax
from jax.sharding import PartitionSpec as P
from jax.experimental import pallas as pl

gamma_ratio = 1.4
weno_epsilon = 1e-06
step_ratio = 0.12


def padded_2(cells, sides, width, closed):
    for axis, dim in sides:
        count = lax.axis_size(axis)
        ends = count if closed else count - 1
        head = lax.slice_in_dim(cells, 0, width, axis=dim)
        tail = lax.slice_in_dim(cells, cells.shape[dim] - width, cells.shape[dim], axis=dim)
        cells = jnp.concatenate(
            [
                lax.ppermute(tail, axis, [(i, (i + 1) % count) for i in range(ends)]),
                cells,
                lax.ppermute(head, axis, [((i + 1) % count, i) for i in range(ends)]),
            ],
            axis=dim,
        )
    return cells


def partner(block, axis, distance):
    count = lax.axis_size(axis)
    route = []
    for low in range(count):
        high = low | 1 << distance
        if high != low and high < count:
            route += [(low, high), (high, low)]
    return lax.ppermute(block, axis, route)


def pressure_of(state):
    kinetic = 0.5 * (jnp.square(state[1]) + jnp.square(state[2]) + jnp.square(state[3])) / state[0]
    return (gamma_ratio - 1.0) * (state[4] - kinetic)


def euler_flux(state, normal):
    pressure = pressure_of(state)
    velocity = state[normal] / state[0]
    flux = state * velocity[None]
    flux = flux.at[normal].add(pressure)
    flux = flux.at[4].add(pressure * velocity)
    return flux


def wave_speed(state, normal):
    pressure = pressure_of(state)
    return jnp.abs(state[normal] / state[0]) + jnp.sqrt(gamma_ratio * pressure / state[0])


def weno_side(far_left, left_cell, centre, right_cell, far_right):
    smooth_low = 13.0 / 12.0 * jnp.square(far_left - 2.0 * left_cell + centre) + 0.25 * jnp.square(
        far_left - 4.0 * left_cell + 3.0 * centre
    )
    smooth_mid = 13.0 / 12.0 * jnp.square(
        left_cell - 2.0 * centre + right_cell
    ) + 0.25 * jnp.square(left_cell - right_cell)
    smooth_high = 13.0 / 12.0 * jnp.square(
        centre - 2.0 * right_cell + far_right
    ) + 0.25 * jnp.square(3.0 * centre - 4.0 * right_cell + far_right)
    weight_low = 0.1 / jnp.square(weno_epsilon + smooth_low)
    weight_mid = 0.6 / jnp.square(weno_epsilon + smooth_mid)
    weight_high = 0.3 / jnp.square(weno_epsilon + smooth_high)
    guess_low = (2.0 * far_left - 7.0 * left_cell + 11.0 * centre) / 6.0
    guess_mid = (-left_cell + 5.0 * centre + 2.0 * right_cell) / 6.0
    guess_high = (2.0 * centre + 5.0 * right_cell - far_right) / 6.0
    return (weight_low * guess_low + weight_mid * guess_mid + weight_high * guess_high) / (
        weight_low + weight_mid + weight_high
    )


def face_flux(padded, fluxes, axis, count, normal, first, second):
    states = [
        lax.slice_in_dim(padded, shift_index, shift_index + count + 1, axis=axis)
        for shift_index in range(6)
    ]
    physical = [
        lax.slice_in_dim(fluxes, shift_index, shift_index + count + 1, axis=axis)
        for shift_index in range(6)
    ]
    mean = 0.5 * (states[2] + states[3])
    density = mean[0]
    normal_speed = mean[normal] / density
    speed_first = mean[first] / density
    speed_second = mean[second] / density
    kinetic = 0.5 * (jnp.square(normal_speed) + jnp.square(speed_first) + jnp.square(speed_second))
    pressure = pressure_of(mean)
    sound = jnp.sqrt(gamma_ratio * pressure / density)
    enthalpy = (mean[4] + pressure) / density
    inv_sound = 1.0 / sound
    factor_one = (gamma_ratio - 1.0) * jnp.square(inv_sound)
    factor_two = factor_one * kinetic
    dissipation = jnp.maximum(wave_speed(states[2], normal), wave_speed(states[3], normal))

    def project(vector):
        dens_part = vector[0]
        norm_part = vector[normal]
        first_part = vector[first]
        second_part = vector[second]
        energy_part = vector[4]
        tangent_sum = factor_one * (
            speed_first * first_part + speed_second * second_part - energy_part
        )
        wave_minus = 0.5 * (
            (factor_two + normal_speed * inv_sound) * dens_part
            - (factor_one * normal_speed + inv_sound) * norm_part
            - tangent_sum
        )
        entropy = (
            (1.0 - factor_two) * dens_part + factor_one * normal_speed * norm_part + tangent_sum
        )
        shear_first = first_part - speed_first * dens_part
        shear_second = second_part - speed_second * dens_part
        wave_plus = 0.5 * (
            (factor_two - normal_speed * inv_sound) * dens_part
            - (factor_one * normal_speed - inv_sound) * norm_part
            - tangent_sum
        )
        return (wave_minus, entropy, shear_first, shear_second, wave_plus)

    state_chars = [project(cell_state) for cell_state in states]
    flux_chars = [project(cell_flux) for cell_flux in physical]
    recon = []
    for field_index in range(5):
        plus_vals = [
            0.5 * (flux_chars[cell][field_index] + dissipation * state_chars[cell][field_index])
            for cell in range(6)
        ]
        minus_vals = [
            0.5 * (flux_chars[cell][field_index] - dissipation * state_chars[cell][field_index])
            for cell in range(6)
        ]
        recon.append(
            weno_side(plus_vals[0], plus_vals[1], plus_vals[2], plus_vals[3], plus_vals[4])
            + weno_side(minus_vals[5], minus_vals[4], minus_vals[3], minus_vals[2], minus_vals[1])
        )
    wave_minus, entropy, shear_first, shear_second, wave_plus = recon
    acoustic = wave_minus + entropy + wave_plus
    parts = {}
    parts[0] = acoustic
    parts[normal] = (
        (normal_speed - sound) * wave_minus
        + normal_speed * entropy
        + (normal_speed + sound) * wave_plus
    )
    parts[first] = speed_first * acoustic + shear_first
    parts[second] = speed_second * acoustic + shear_second
    parts[4] = (
        (enthalpy - normal_speed * sound) * wave_minus
        + kinetic * entropy
        + speed_first * shear_first
        + speed_second * shear_second
        + (enthalpy + normal_speed * sound) * wave_plus
    )
    return jnp.stack([parts[index_part] for index_part in range(5)])


def divergence(padded, axis, count, normal, first, second):
    faces = face_flux(padded, euler_flux(padded, normal), axis, count, normal, first, second)
    return lax.slice_in_dim(faces, 1, count + 1, axis=axis) - lax.slice_in_dim(
        faces, 0, count, axis=axis
    )


def flip_radial(cells):
    turned = cells[:, :, ::-1]
    return jnp.concatenate([turned[:3], -turned[3:4], turned[4:]], axis=0)


def flip_theta(cells):
    return jnp.concatenate([cells[:2], -cells[2:3], cells[3:]], axis=0)


def hold(cells, value):
    return jnp.where(jnp.isnan(value.reshape(-1)[0]), jnp.zeros((), cells.dtype), cells)


def after(value, index):
    return index + jnp.isnan(value.reshape(-1)[0]).astype(jnp.int32)


def route_parts(rotor_step, width):
    rows = lax.axis_size("tx")
    columns = lax.axis_size("tz")
    turns = rotor_step[0] // 4 // width
    centre = (turns - 1) % (rows * columns)
    return rows, columns, centre // columns, centre % columns


def pick_column(slab, rotor_step, before):
    rows, columns, centre_row, centre_column = route_parts(rotor_step, slab.shape[3])
    source_column = (centre_column - lax.axis_index("tz")) % columns
    gathered = lax.all_gather(slab, "tz")
    return lax.dynamic_index_in_dim(gathered, after(before, source_column), 0, keepdims=False)


def pick_row(slab, rotor_step, before):
    rows, columns, centre_row, centre_column = route_parts(rotor_step, slab.shape[3])
    borrow = (lax.axis_index("tz") > centre_column).astype(jnp.int32)
    source_row = (centre_row - lax.axis_index("tx") - borrow) % rows
    gathered = lax.all_gather(slab, "tx")
    return lax.dynamic_index_in_dim(gathered, after(before, source_row), 0, keepdims=False)


def cross_blocks(slab):
    block_count = lax.axis_size("blk")
    slab_count = lax.axis_size("tx") * lax.axis_size("tz")
    this_route = []
    next_route = []
    for blk_from in range(block_count):
        blk_to = (blk_from + 1) % block_count
        for slab_from in range(slab_count):
            source = blk_from * slab_count + slab_from
            this_route.append((source, blk_to * slab_count + slab_from))
            next_route.append((source, blk_to * slab_count + (slab_from + 1) % slab_count))
    axes = ("blk", "tx", "tz")
    return lax.ppermute(slab, axes, this_route), lax.ppermute(slab, axes, next_route)


def window_of(this_slab, next_slab, rotor_step, before):
    width = this_slab.shape[3]
    remainder = after(before, rotor_step[0] // 4 % width)
    doubled = jnp.concatenate([next_slab, this_slab], axis=3)
    return lax.dynamic_slice_in_dim(doubled, width - 1 - remainder, width + 1, 3)


def axial_kernel(padded_ref, out_ref):
    padded = padded_ref[...]
    count = padded.shape[1] - 6
    pressure = pressure_of(padded)
    velocity = padded[1] / padded[0]
    parts = [padded[index_part] * velocity for index_part in range(5)]
    parts[1] = parts[1] + pressure
    parts[4] = parts[4] + pressure * velocity
    faces = face_flux(padded, jnp.stack(parts), 1, count, 1, 2, 3)
    out_ref[...] = faces


def axial_faces(padded):
    components, planes, bands, width = padded.shape
    lanes = 128
    block = (components, planes, bands, lanes)
    out_block = (components, planes - 5, bands, lanes)
    return pl.pallas_call(
        axial_kernel,
        grid=(width // lanes,),
        in_specs=[pl.BlockSpec(block, lambda i: (0, 0, 0, i))],
        out_specs=pl.BlockSpec(out_block, lambda i: (0, 0, 0, i)),
        out_shape=jax.ShapeDtypeStruct((components, planes - 5, bands, width), padded.dtype),
    )(padded)


def shards(base_state, section_state, rotor_step):
    planes = section_state.shape[1]
    bands = section_state.shape[2]
    width = section_state.shape[3]
    fraction = (rotor_step[0] % 4).astype(jnp.float32) / 4.0
    theta_padded = padded_2(section_state, ((("tx", "tz"), 3),), 3, True)
    radial_raw = padded_2(section_state, (("radial", 2),), 3, False)
    band_index = lax.axis_index("radial")
    band_count = lax.axis_size("radial")
    lower_wall = jnp.where(
        band_index == 0, flip_radial(section_state[:, :, :3]), radial_raw[:, :, :3]
    )
    upper_wall = jnp.where(
        band_index == band_count - 1, flip_radial(section_state[:, :, -3:]), radial_raw[:, :, -3:]
    )
    radial_padded = jnp.concatenate([lower_wall, section_state, upper_wall], axis=2)
    block_index = lax.axis_index("blk")
    front = block_index == 0
    outgoing = jnp.where(front, section_state[:, -3:], section_state[:, :3])[..., ::-1]
    radial = divergence(radial_padded, 2, bands, 3, 1, 2)
    chosen = pick_column(outgoing, rotor_step, radial)
    theta_padded = hold(theta_padded, chosen)
    azimuthal = divergence(theta_padded, 3, width, 2, 1, 3)
    chosen = pick_row(chosen, rotor_step, azimuthal)
    this_slab, next_slab = cross_blocks(chosen)
    edge_low = jnp.concatenate(
        [section_state[:, :1], section_state[:, :1], section_state[:, :1]], axis=1
    )
    edge_high = jnp.concatenate(
        [section_state[:, -1:], section_state[:, -1:], section_state[:, -1:]], axis=1
    )
    local_window = jnp.where(
        front,
        jnp.concatenate([edge_low, section_state], axis=1),
        jnp.concatenate([section_state, edge_high], axis=1),
    )
    local_window = hold(local_window, chosen)
    local_faces = axial_faces(local_window)
    window = window_of(this_slab, next_slab, rotor_step, local_faces)
    ghost = flip_theta(
        (1.0 - fraction) * window[..., 1 : width + 1] + fraction * window[..., :width]
    )
    mortar_window = jnp.where(
        front,
        jnp.concatenate([section_state[:, 1:], ghost], axis=1),
        jnp.concatenate([ghost, section_state[:, :-1]], axis=1),
    )
    mortar_faces = axial_faces(mortar_window)
    faces = jnp.where(
        front,
        jnp.concatenate([local_faces, mortar_faces], axis=1),
        jnp.concatenate([mortar_faces, local_faces], axis=1),
    )
    axial = lax.slice_in_dim(faces, 1, planes + 1, axis=1) - lax.slice_in_dim(
        faces, 0, planes, axis=1
    )
    change = -step_ratio * (axial + radial + azimuthal)
    return 0.75 * base_state + 0.25 * (section_state + change)


def solution(mesh):
    blocks, slabs, bands = (mesh.shape[name] for name in ("blk", "theta", "radial"))
    rows = 4 if slabs % 4 == 0 else 1
    grid = jax.sharding.Mesh(
        mesh.devices.reshape(blocks, rows, slabs // rows, bands), ("blk", "tx", "tz", "radial")
    )
    in_specs = (P(None, "blk", "radial", ("tx", "tz")), P(None, "blk", "radial", ("tx", "tz")), P())
    out_specs = P(None, "blk", "radial", ("tx", "tz"))
    inner = jax.shard_map(shards, mesh=grid, in_specs=in_specs, out_specs=out_specs, check_vma=False)
    sharded = jax.sharding.NamedSharding(mesh, P(None, "blk", "radial", "theta"))

    def run(base_state, section_state, rotor_step):
        return jax.lax.with_sharding_constraint(
            inner(base_state, section_state, rotor_step), sharded
        )

    return run
```

```python
import jax
import jax.numpy as jnp
from jax import lax
from jax.sharding import PartitionSpec as P
from jax.experimental import pallas as pl

gamma_ratio = 1.4
weno_epsilon = 1e-06
step_ratio = 0.12


def padded_2(cells, sides, width, closed):
    for axis, dim in sides:
        count = lax.axis_size(axis)
        ends = count if closed else count - 1
        head = lax.slice_in_dim(cells, 0, width, axis=dim)
        tail = lax.slice_in_dim(cells, cells.shape[dim] - width, cells.shape[dim], axis=dim)
        cells = jnp.concatenate(
            [
                lax.ppermute(tail, axis, [(i, (i + 1) % count) for i in range(ends)]),
                cells,
                lax.ppermute(head, axis, [((i + 1) % count, i) for i in range(ends)]),
            ],
            axis=dim,
        )
    return cells


def partner(block, axis, distance):
    count = lax.axis_size(axis)
    route = []
    for low in range(count):
        high = low | 1 << distance
        if high != low and high < count:
            route += [(low, high), (high, low)]
    return lax.ppermute(block, axis, route)


def pressure_of(state):
    kinetic = 0.5 * (jnp.square(state[1]) + jnp.square(state[2]) + jnp.square(state[3])) / state[0]
    return (gamma_ratio - 1.0) * (state[4] - kinetic)


def euler_flux(state, normal):
    pressure = pressure_of(state)
    velocity = state[normal] / state[0]
    flux = state * velocity[None]
    flux = flux.at[normal].add(pressure)
    flux = flux.at[4].add(pressure * velocity)
    return flux


def wave_speed(state, normal):
    pressure = pressure_of(state)
    return jnp.abs(state[normal] / state[0]) + jnp.sqrt(gamma_ratio * pressure / state[0])


def weno_side(far_left, left_cell, centre, right_cell, far_right):
    smooth_low = 13.0 / 12.0 * jnp.square(far_left - 2.0 * left_cell + centre) + 0.25 * jnp.square(
        far_left - 4.0 * left_cell + 3.0 * centre
    )
    smooth_mid = 13.0 / 12.0 * jnp.square(
        left_cell - 2.0 * centre + right_cell
    ) + 0.25 * jnp.square(left_cell - right_cell)
    smooth_high = 13.0 / 12.0 * jnp.square(
        centre - 2.0 * right_cell + far_right
    ) + 0.25 * jnp.square(3.0 * centre - 4.0 * right_cell + far_right)
    weight_low = 0.1 / jnp.square(weno_epsilon + smooth_low)
    weight_mid = 0.6 / jnp.square(weno_epsilon + smooth_mid)
    weight_high = 0.3 / jnp.square(weno_epsilon + smooth_high)
    guess_low = (2.0 * far_left - 7.0 * left_cell + 11.0 * centre) / 6.0
    guess_mid = (-left_cell + 5.0 * centre + 2.0 * right_cell) / 6.0
    guess_high = (2.0 * centre + 5.0 * right_cell - far_right) / 6.0
    return (weight_low * guess_low + weight_mid * guess_mid + weight_high * guess_high) / (
        weight_low + weight_mid + weight_high
    )


def face_flux(padded, fluxes, axis, count, normal, first, second):
    states = [
        lax.slice_in_dim(padded, shift_index, shift_index + count + 1, axis=axis)
        for shift_index in range(6)
    ]
    physical = [
        lax.slice_in_dim(fluxes, shift_index, shift_index + count + 1, axis=axis)
        for shift_index in range(6)
    ]
    mean = 0.5 * (states[2] + states[3])
    density = mean[0]
    normal_speed = mean[normal] / density
    speed_first = mean[first] / density
    speed_second = mean[second] / density
    kinetic = 0.5 * (jnp.square(normal_speed) + jnp.square(speed_first) + jnp.square(speed_second))
    pressure = pressure_of(mean)
    sound = jnp.sqrt(gamma_ratio * pressure / density)
    enthalpy = (mean[4] + pressure) / density
    inv_sound = 1.0 / sound
    factor_one = (gamma_ratio - 1.0) * jnp.square(inv_sound)
    factor_two = factor_one * kinetic
    dissipation = jnp.maximum(wave_speed(states[2], normal), wave_speed(states[3], normal))

    def project(vector):
        dens_part = vector[0]
        norm_part = vector[normal]
        first_part = vector[first]
        second_part = vector[second]
        energy_part = vector[4]
        tangent_sum = factor_one * (
            speed_first * first_part + speed_second * second_part - energy_part
        )
        wave_minus = 0.5 * (
            (factor_two + normal_speed * inv_sound) * dens_part
            - (factor_one * normal_speed + inv_sound) * norm_part
            - tangent_sum
        )
        entropy = (
            (1.0 - factor_two) * dens_part + factor_one * normal_speed * norm_part + tangent_sum
        )
        shear_first = first_part - speed_first * dens_part
        shear_second = second_part - speed_second * dens_part
        wave_plus = 0.5 * (
            (factor_two - normal_speed * inv_sound) * dens_part
            - (factor_one * normal_speed - inv_sound) * norm_part
            - tangent_sum
        )
        return (wave_minus, entropy, shear_first, shear_second, wave_plus)

    state_chars = [project(cell_state) for cell_state in states]
    flux_chars = [project(cell_flux) for cell_flux in physical]
    recon = []
    for field_index in range(5):
        plus_vals = [
            0.5 * (flux_chars[cell][field_index] + dissipation * state_chars[cell][field_index])
            for cell in range(6)
        ]
        minus_vals = [
            0.5 * (flux_chars[cell][field_index] - dissipation * state_chars[cell][field_index])
            for cell in range(6)
        ]
        recon.append(
            weno_side(plus_vals[0], plus_vals[1], plus_vals[2], plus_vals[3], plus_vals[4])
            + weno_side(minus_vals[5], minus_vals[4], minus_vals[3], minus_vals[2], minus_vals[1])
        )
    wave_minus, entropy, shear_first, shear_second, wave_plus = recon
    acoustic = wave_minus + entropy + wave_plus
    parts = {}
    parts[0] = acoustic
    parts[normal] = (
        (normal_speed - sound) * wave_minus
        + normal_speed * entropy
        + (normal_speed + sound) * wave_plus
    )
    parts[first] = speed_first * acoustic + shear_first
    parts[second] = speed_second * acoustic + shear_second
    parts[4] = (
        (enthalpy - normal_speed * sound) * wave_minus
        + kinetic * entropy
        + speed_first * shear_first
        + speed_second * shear_second
        + (enthalpy + normal_speed * sound) * wave_plus
    )
    return jnp.stack([parts[index_part] for index_part in range(5)])


def divergence(padded, axis, count, normal, first, second):
    faces = face_flux(padded, euler_flux(padded, normal), axis, count, normal, first, second)
    return lax.slice_in_dim(faces, 1, count + 1, axis=axis) - lax.slice_in_dim(
        faces, 0, count, axis=axis
    )


def flip_radial(cells):
    turned = cells[:, :, ::-1]
    return jnp.concatenate([turned[:3], -turned[3:4], turned[4:]], axis=0)


def flip_theta(cells):
    return jnp.concatenate([cells[:2], -cells[2:3], cells[3:]], axis=0)


def hold(cells, value):
    return jnp.where(jnp.isnan(value.reshape(-1)[0]), jnp.zeros((), cells.dtype), cells)


def after(value, index):
    return index + jnp.isnan(value.reshape(-1)[0]).astype(jnp.int32)


def route_parts(rotor_step, width):
    rows = lax.axis_size("tx")
    columns = lax.axis_size("tz")
    turns = rotor_step[0] // 4 // width
    centre = (turns - 1) % (rows * columns)
    return rows, columns, centre // columns, centre % columns


def pick_column(gathered, rotor_step, before):
    rows, columns, centre_row, centre_column = route_parts(rotor_step, gathered.shape[4])
    source_column = (centre_column - lax.axis_index("tz")) % columns
    return lax.dynamic_index_in_dim(gathered, after(before, source_column), 0, keepdims=False)


def pick_row(slab, rotor_step, before):
    rows, columns, centre_row, centre_column = route_parts(rotor_step, slab.shape[3])
    borrow = (lax.axis_index("tz") > centre_column).astype(jnp.int32)
    source_row = (centre_row - lax.axis_index("tx") - borrow) % rows
    gathered = lax.all_gather(slab, "tx")
    return lax.dynamic_index_in_dim(gathered, after(before, source_row), 0, keepdims=False)


def cross_blocks(slab):
    block_count = lax.axis_size("blk")
    slab_count = lax.axis_size("tx") * lax.axis_size("tz")
    this_route = []
    next_route = []
    for blk_from in range(block_count):
        blk_to = (blk_from + 1) % block_count
        for slab_from in range(slab_count):
            source = blk_from * slab_count + slab_from
            this_route.append((source, blk_to * slab_count + slab_from))
            next_route.append((source, blk_to * slab_count + (slab_from + 1) % slab_count))
    axes = ("blk", "tx", "tz")
    return lax.ppermute(slab, axes, this_route), lax.ppermute(slab, axes, next_route)


def window_of(this_slab, next_slab, rotor_step, before):
    width = this_slab.shape[3]
    remainder = after(before, rotor_step[0] // 4 % width)
    doubled = jnp.concatenate([next_slab, this_slab], axis=3)
    return lax.dynamic_slice_in_dim(doubled, width - 1 - remainder, width + 1, 3)


def axial_kernel(padded_ref, out_ref):
    padded = padded_ref[...]
    count = padded.shape[1] - 6
    pressure = pressure_of(padded)
    velocity = padded[1] / padded[0]
    parts = [padded[index_part] * velocity for index_part in range(5)]
    parts[1] = parts[1] + pressure
    parts[4] = parts[4] + pressure * velocity
    faces = face_flux(padded, jnp.stack(parts), 1, count, 1, 2, 3)
    out_ref[...] = faces


def axial_faces(padded):
    components, planes, bands, width = padded.shape
    lanes = 128
    block = (components, planes, bands, lanes)
    out_block = (components, planes - 5, bands, lanes)
    return pl.pallas_call(
        axial_kernel,
        grid=(width // lanes,),
        in_specs=[pl.BlockSpec(block, lambda i: (0, 0, 0, i))],
        out_specs=pl.BlockSpec(out_block, lambda i: (0, 0, 0, i)),
        out_shape=jax.ShapeDtypeStruct((components, planes - 5, bands, width), padded.dtype),
    )(padded)


def shards(base_state, section_state, rotor_step):
    planes = section_state.shape[1]
    bands = section_state.shape[2]
    width = section_state.shape[3]
    fraction = (rotor_step[0] % 4).astype(jnp.float32) / 4.0
    front = lax.axis_index("blk") == 0
    outgoing = jnp.where(front, section_state[:, -3:], section_state[:, :3])[..., ::-1]
    gathered = lax.all_gather(outgoing, "tz")
    halo_state = hold(section_state, outgoing)
    theta_padded = padded_2(halo_state, ((("tx", "tz"), 3),), 3, True)
    radial_raw = padded_2(halo_state, (("radial", 2),), 3, False)
    band_index = lax.axis_index("radial")
    band_count = lax.axis_size("radial")
    lower_wall = jnp.where(
        band_index == 0, flip_radial(section_state[:, :, :3]), radial_raw[:, :, :3]
    )
    upper_wall = jnp.where(
        band_index == band_count - 1, flip_radial(section_state[:, :, -3:]), radial_raw[:, :, -3:]
    )
    radial_padded = jnp.concatenate([lower_wall, section_state, upper_wall], axis=2)
    block_index = lax.axis_index("blk")
    front = block_index == 0
    radial = divergence(radial_padded, 2, bands, 3, 1, 2)
    chosen = pick_column(gathered, rotor_step, radial)
    theta_padded = hold(theta_padded, chosen)
    azimuthal = divergence(theta_padded, 3, width, 2, 1, 3)
    chosen = pick_row(chosen, rotor_step, azimuthal)
    this_slab, next_slab = cross_blocks(chosen)
    edge_low = jnp.concatenate(
        [section_state[:, :1], section_state[:, :1], section_state[:, :1]], axis=1
    )
    edge_high = jnp.concatenate(
        [section_state[:, -1:], section_state[:, -1:], section_state[:, -1:]], axis=1
    )
    local_window = jnp.where(
        front,
        jnp.concatenate([edge_low, section_state], axis=1),
        jnp.concatenate([section_state, edge_high], axis=1),
    )
    local_window = hold(local_window, chosen)
    local_faces = axial_faces(local_window)
    window = window_of(this_slab, next_slab, rotor_step, local_faces)
    ghost = flip_theta(
        (1.0 - fraction) * window[..., 1 : width + 1] + fraction * window[..., :width]
    )
    mortar_window = jnp.where(
        front,
        jnp.concatenate([section_state[:, 1:], ghost], axis=1),
        jnp.concatenate([ghost, section_state[:, :-1]], axis=1),
    )
    mortar_faces = axial_faces(mortar_window)
    faces = jnp.where(
        front,
        jnp.concatenate([local_faces, mortar_faces], axis=1),
        jnp.concatenate([mortar_faces, local_faces], axis=1),
    )
    axial = lax.slice_in_dim(faces, 1, planes + 1, axis=1) - lax.slice_in_dim(
        faces, 0, planes, axis=1
    )
    change = -step_ratio * (axial + radial + azimuthal)
    return 0.75 * base_state + 0.25 * (section_state + change)


def solution(mesh):
    blocks, slabs, bands = (mesh.shape[name] for name in ("blk", "theta", "radial"))
    rows = 4 if slabs % 4 == 0 else 1
    grid = jax.sharding.Mesh(
        mesh.devices.reshape(blocks, rows, slabs // rows, bands), ("blk", "tx", "tz", "radial")
    )
    in_specs = (P(None, "blk", "radial", ("tx", "tz")), P(None, "blk", "radial", ("tx", "tz")), P())
    out_specs = P(None, "blk", "radial", ("tx", "tz"))
    inner = jax.shard_map(shards, mesh=grid, in_specs=in_specs, out_specs=out_specs, check_vma=False)
    sharded = jax.sharding.NamedSharding(mesh, P(None, "blk", "radial", "theta"))

    def run(base_state, section_state, rotor_step):
        return jax.lax.with_sharding_constraint(
            inner(base_state, section_state, rotor_step), sharded
        )

    return run
```

```python
import jax
import jax.numpy as jnp
from jax import lax
from jax.sharding import PartitionSpec as P
from jax.experimental import pallas as pl

gamma_ratio = 1.4
weno_epsilon = 1e-06
step_ratio = 0.12


def padded_2(cells, sides, width, closed):
    for axis, dim in sides:
        count = lax.axis_size(axis)
        ends = count if closed else count - 1
        head = lax.slice_in_dim(cells, 0, width, axis=dim)
        tail = lax.slice_in_dim(cells, cells.shape[dim] - width, cells.shape[dim], axis=dim)
        cells = jnp.concatenate(
            [
                lax.ppermute(tail, axis, [(i, (i + 1) % count) for i in range(ends)]),
                cells,
                lax.ppermute(head, axis, [((i + 1) % count, i) for i in range(ends)]),
            ],
            axis=dim,
        )
    return cells


def partner(block, axis, distance):
    count = lax.axis_size(axis)
    route = []
    for low in range(count):
        high = low | 1 << distance
        if high != low and high < count:
            route += [(low, high), (high, low)]
    return lax.ppermute(block, axis, route)


def pressure_of(state):
    kinetic = 0.5 * (jnp.square(state[1]) + jnp.square(state[2]) + jnp.square(state[3])) / state[0]
    return (gamma_ratio - 1.0) * (state[4] - kinetic)


def euler_flux(state, normal):
    pressure = pressure_of(state)
    velocity = state[normal] / state[0]
    flux = state * velocity[None]
    flux = flux.at[normal].add(pressure)
    flux = flux.at[4].add(pressure * velocity)
    return flux


def wave_speed(state, normal):
    pressure = pressure_of(state)
    return jnp.abs(state[normal] / state[0]) + jnp.sqrt(gamma_ratio * pressure / state[0])


def weno_side(far_left, left_cell, centre, right_cell, far_right):
    smooth_low = 13.0 / 12.0 * jnp.square(far_left - 2.0 * left_cell + centre) + 0.25 * jnp.square(
        far_left - 4.0 * left_cell + 3.0 * centre
    )
    smooth_mid = 13.0 / 12.0 * jnp.square(
        left_cell - 2.0 * centre + right_cell
    ) + 0.25 * jnp.square(left_cell - right_cell)
    smooth_high = 13.0 / 12.0 * jnp.square(
        centre - 2.0 * right_cell + far_right
    ) + 0.25 * jnp.square(3.0 * centre - 4.0 * right_cell + far_right)
    weight_low = 0.1 / jnp.square(weno_epsilon + smooth_low)
    weight_mid = 0.6 / jnp.square(weno_epsilon + smooth_mid)
    weight_high = 0.3 / jnp.square(weno_epsilon + smooth_high)
    guess_low = (2.0 * far_left - 7.0 * left_cell + 11.0 * centre) / 6.0
    guess_mid = (-left_cell + 5.0 * centre + 2.0 * right_cell) / 6.0
    guess_high = (2.0 * centre + 5.0 * right_cell - far_right) / 6.0
    return (weight_low * guess_low + weight_mid * guess_mid + weight_high * guess_high) / (
        weight_low + weight_mid + weight_high
    )


def face_flux(padded, fluxes, axis, count, normal, first, second):
    states = [
        lax.slice_in_dim(padded, shift_index, shift_index + count + 1, axis=axis)
        for shift_index in range(6)
    ]
    physical = [
        lax.slice_in_dim(fluxes, shift_index, shift_index + count + 1, axis=axis)
        for shift_index in range(6)
    ]
    mean = 0.5 * (states[2] + states[3])
    density = mean[0]
    normal_speed = mean[normal] / density
    speed_first = mean[first] / density
    speed_second = mean[second] / density
    kinetic = 0.5 * (jnp.square(normal_speed) + jnp.square(speed_first) + jnp.square(speed_second))
    pressure = pressure_of(mean)
    sound = jnp.sqrt(gamma_ratio * pressure / density)
    enthalpy = (mean[4] + pressure) / density
    inv_sound = 1.0 / sound
    factor_one = (gamma_ratio - 1.0) * jnp.square(inv_sound)
    factor_two = factor_one * kinetic
    dissipation = jnp.maximum(wave_speed(states[2], normal), wave_speed(states[3], normal))

    def project(vector):
        dens_part = vector[0]
        norm_part = vector[normal]
        first_part = vector[first]
        second_part = vector[second]
        energy_part = vector[4]
        tangent_sum = factor_one * (
            speed_first * first_part + speed_second * second_part - energy_part
        )
        wave_minus = 0.5 * (
            (factor_two + normal_speed * inv_sound) * dens_part
            - (factor_one * normal_speed + inv_sound) * norm_part
            - tangent_sum
        )
        entropy = (
            (1.0 - factor_two) * dens_part + factor_one * normal_speed * norm_part + tangent_sum
        )
        shear_first = first_part - speed_first * dens_part
        shear_second = second_part - speed_second * dens_part
        wave_plus = 0.5 * (
            (factor_two - normal_speed * inv_sound) * dens_part
            - (factor_one * normal_speed - inv_sound) * norm_part
            - tangent_sum
        )
        return (wave_minus, entropy, shear_first, shear_second, wave_plus)

    state_chars = [project(cell_state) for cell_state in states]
    flux_chars = [project(cell_flux) for cell_flux in physical]
    recon = []
    for field_index in range(5):
        plus_vals = [
            0.5 * (flux_chars[cell][field_index] + dissipation * state_chars[cell][field_index])
            for cell in range(6)
        ]
        minus_vals = [
            0.5 * (flux_chars[cell][field_index] - dissipation * state_chars[cell][field_index])
            for cell in range(6)
        ]
        recon.append(
            weno_side(plus_vals[0], plus_vals[1], plus_vals[2], plus_vals[3], plus_vals[4])
            + weno_side(minus_vals[5], minus_vals[4], minus_vals[3], minus_vals[2], minus_vals[1])
        )
    wave_minus, entropy, shear_first, shear_second, wave_plus = recon
    acoustic = wave_minus + entropy + wave_plus
    parts = {}
    parts[0] = acoustic
    parts[normal] = (
        (normal_speed - sound) * wave_minus
        + normal_speed * entropy
        + (normal_speed + sound) * wave_plus
    )
    parts[first] = speed_first * acoustic + shear_first
    parts[second] = speed_second * acoustic + shear_second
    parts[4] = (
        (enthalpy - normal_speed * sound) * wave_minus
        + kinetic * entropy
        + speed_first * shear_first
        + speed_second * shear_second
        + (enthalpy + normal_speed * sound) * wave_plus
    )
    return jnp.stack([parts[index_part] for index_part in range(5)])


def divergence(padded, axis, count, normal, first, second):
    faces = face_flux(padded, euler_flux(padded, normal), axis, count, normal, first, second)
    return lax.slice_in_dim(faces, 1, count + 1, axis=axis) - lax.slice_in_dim(
        faces, 0, count, axis=axis
    )


def flip_radial(cells):
    turned = cells[:, :, ::-1]
    return jnp.concatenate([turned[:3], -turned[3:4], turned[4:]], axis=0)


def flip_theta(cells):
    return jnp.concatenate([cells[:2], -cells[2:3], cells[3:]], axis=0)


def hold(cells, value):
    return jnp.where(jnp.isnan(value.reshape(-1)[0]), jnp.zeros((), cells.dtype), cells)


def after(value, index):
    return index + jnp.isnan(value.reshape(-1)[0]).astype(jnp.int32)


def route_parts(rotor_step, width):
    rows = lax.axis_size("tx")
    columns = lax.axis_size("tz")
    turns = rotor_step[0] // 4 // width
    centre = (turns - 1) % (rows * columns)
    return rows, columns, centre // columns, centre % columns


def pick_column(slab, rotor_step, before):
    rows, columns, centre_row, centre_column = route_parts(rotor_step, slab.shape[3])
    source_column = (centre_column - lax.axis_index("tz")) % columns
    gathered = lax.all_gather(slab, "tz")
    return lax.dynamic_index_in_dim(gathered, after(before, source_column), 0, keepdims=False)


def pick_row(slab, rotor_step, before):
    rows, columns, centre_row, centre_column = route_parts(rotor_step, slab.shape[3])
    borrow = (lax.axis_index("tz") > centre_column).astype(jnp.int32)
    source_row = (centre_row - lax.axis_index("tx") - borrow) % rows
    gathered = lax.all_gather(slab, "tx")
    return lax.dynamic_index_in_dim(gathered, after(before, source_row), 0, keepdims=False)


def cross_blocks(slab):
    block_count = lax.axis_size("blk")
    slab_count = lax.axis_size("tx") * lax.axis_size("tz")
    this_route = []
    next_route = []
    for blk_from in range(block_count):
        blk_to = (blk_from + 1) % block_count
        for slab_from in range(slab_count):
            source = blk_from * slab_count + slab_from
            this_route.append((source, blk_to * slab_count + slab_from))
            next_route.append((source, blk_to * slab_count + (slab_from + 1) % slab_count))
    axes = ("blk", "tx", "tz")
    return lax.ppermute(slab, axes, this_route), lax.ppermute(slab, axes, next_route)


def window_of(this_slab, next_slab, rotor_step, before):
    width = this_slab.shape[3]
    remainder = after(before, rotor_step[0] // 4 % width)
    doubled = jnp.concatenate([next_slab, this_slab], axis=3)
    return lax.dynamic_slice_in_dim(doubled, width - 1 - remainder, width + 1, 3)


def axial_kernel(padded_ref, out_ref):
    padded = padded_ref[...]
    count = padded.shape[1] - 6
    pressure = pressure_of(padded)
    velocity = padded[1] / padded[0]
    parts = [padded[index_part] * velocity for index_part in range(5)]
    parts[1] = parts[1] + pressure
    parts[4] = parts[4] + pressure * velocity
    faces = face_flux(padded, jnp.stack(parts), 1, count, 1, 2, 3)
    out_ref[...] = faces


def axial_faces(padded):
    components, planes, bands, width = padded.shape
    lanes = 128
    block = (components, planes, bands, lanes)
    out_block = (components, planes - 5, bands, lanes)
    return pl.pallas_call(
        axial_kernel,
        grid=(width // lanes,),
        in_specs=[pl.BlockSpec(block, lambda i: (0, 0, 0, i))],
        out_specs=pl.BlockSpec(out_block, lambda i: (0, 0, 0, i)),
        out_shape=jax.ShapeDtypeStruct((components, planes - 5, bands, width), padded.dtype),
    )(padded)


def shards(base_state, section_state, rotor_step):
    planes = section_state.shape[1]
    bands = section_state.shape[2]
    width = section_state.shape[3]
    fraction = (rotor_step[0] % 4).astype(jnp.float32) / 4.0
    theta_padded = padded_2(section_state, ((("tx", "tz"), 3),), 3, True)
    radial_raw = padded_2(section_state, (("radial", 2),), 3, False)
    band_index = lax.axis_index("radial")
    band_count = lax.axis_size("radial")
    lower_wall = jnp.where(
        band_index == 0, flip_radial(section_state[:, :, :3]), radial_raw[:, :, :3]
    )
    upper_wall = jnp.where(
        band_index == band_count - 1, flip_radial(section_state[:, :, -3:]), radial_raw[:, :, -3:]
    )
    radial_padded = jnp.concatenate([lower_wall, section_state, upper_wall], axis=2)
    block_index = lax.axis_index("blk")
    front = block_index == 0
    outgoing = jnp.where(front, section_state[:, -3:], section_state[:, :3])[..., ::-1]
    radial = divergence(radial_padded, 2, bands, 3, 1, 2)
    chosen = pick_column(outgoing, rotor_step, radial)
    theta_padded = hold(theta_padded, chosen)
    azimuthal = divergence(theta_padded, 3, width, 2, 1, 3)
    chosen = pick_row(chosen, rotor_step, azimuthal)
    this_slab, next_slab = cross_blocks(chosen)
    edge_low = jnp.concatenate(
        [section_state[:, :1], section_state[:, :1], section_state[:, :1]], axis=1
    )
    edge_high = jnp.concatenate(
        [section_state[:, -1:], section_state[:, -1:], section_state[:, -1:]], axis=1
    )
    local_window = jnp.where(
        front,
        jnp.concatenate([edge_low, section_state], axis=1),
        jnp.concatenate([section_state, edge_high], axis=1),
    )
    local_window = hold(local_window, chosen)
    local_faces = axial_faces(local_window)
    settled = 0.75 * base_state + 0.25 * (section_state - step_ratio * (radial + azimuthal))
    window = window_of(this_slab, next_slab, rotor_step, local_faces + settled[:, :1, :, :1])
    ghost = flip_theta(
        (1.0 - fraction) * window[..., 1 : width + 1] + fraction * window[..., :width]
    )
    mortar_window = jnp.where(
        front,
        jnp.concatenate([section_state[:, 1:], ghost], axis=1),
        jnp.concatenate([ghost, section_state[:, :-1]], axis=1),
    )
    mortar_faces = axial_faces(mortar_window)
    faces = jnp.where(
        front,
        jnp.concatenate([local_faces, mortar_faces], axis=1),
        jnp.concatenate([mortar_faces, local_faces], axis=1),
    )
    axial = lax.slice_in_dim(faces, 1, planes + 1, axis=1) - lax.slice_in_dim(
        faces, 0, planes, axis=1
    )
    return settled - 0.25 * step_ratio * axial


def solution(mesh):
    blocks, slabs, bands = (mesh.shape[name] for name in ("blk", "theta", "radial"))
    rows = 4 if slabs % 4 == 0 else 1
    grid = jax.sharding.Mesh(
        mesh.devices.reshape(blocks, rows, slabs // rows, bands), ("blk", "tx", "tz", "radial")
    )
    in_specs = (P(None, "blk", "radial", ("tx", "tz")), P(None, "blk", "radial", ("tx", "tz")), P())
    out_specs = P(None, "blk", "radial", ("tx", "tz"))
    inner = jax.shard_map(shards, mesh=grid, in_specs=in_specs, out_specs=out_specs, check_vma=False)
    sharded = jax.sharding.NamedSharding(mesh, P(None, "blk", "radial", "theta"))

    def run(base_state, section_state, rotor_step):
        return jax.lax.with_sharding_constraint(
            inner(base_state, section_state, rotor_step), sharded
        )

    return run
```

```python
import jax
import jax.numpy as jnp
from jax import lax
from jax.sharding import PartitionSpec as P
from jax.experimental import pallas as pl

gamma_ratio = 1.4
weno_epsilon = 1e-06
step_ratio = 0.12


def padded_2(cells, sides, width, closed):
    for axis, dim in sides:
        count = lax.axis_size(axis)
        ends = count if closed else count - 1
        head = lax.slice_in_dim(cells, 0, width, axis=dim)
        tail = lax.slice_in_dim(cells, cells.shape[dim] - width, cells.shape[dim], axis=dim)
        cells = jnp.concatenate(
            [
                lax.ppermute(tail, axis, [(i, (i + 1) % count) for i in range(ends)]),
                cells,
                lax.ppermute(head, axis, [((i + 1) % count, i) for i in range(ends)]),
            ],
            axis=dim,
        )
    return cells


def partner(block, axis, distance):
    count = lax.axis_size(axis)
    route = []
    for low in range(count):
        high = low | 1 << distance
        if high != low and high < count:
            route += [(low, high), (high, low)]
    return lax.ppermute(block, axis, route)


def pressure_of(state):
    kinetic = 0.5 * (jnp.square(state[1]) + jnp.square(state[2]) + jnp.square(state[3])) / state[0]
    return (gamma_ratio - 1.0) * (state[4] - kinetic)


def euler_flux(state, normal):
    pressure = pressure_of(state)
    velocity = state[normal] / state[0]
    flux = state * velocity[None]
    flux = flux.at[normal].add(pressure)
    flux = flux.at[4].add(pressure * velocity)
    return flux


def wave_speed(state, normal):
    pressure = pressure_of(state)
    return jnp.abs(state[normal] / state[0]) + jnp.sqrt(gamma_ratio * pressure / state[0])


def weno_side(far_left, left_cell, centre, right_cell, far_right):
    smooth_low = 13.0 / 12.0 * jnp.square(far_left - 2.0 * left_cell + centre) + 0.25 * jnp.square(
        far_left - 4.0 * left_cell + 3.0 * centre
    )
    smooth_mid = 13.0 / 12.0 * jnp.square(
        left_cell - 2.0 * centre + right_cell
    ) + 0.25 * jnp.square(left_cell - right_cell)
    smooth_high = 13.0 / 12.0 * jnp.square(
        centre - 2.0 * right_cell + far_right
    ) + 0.25 * jnp.square(3.0 * centre - 4.0 * right_cell + far_right)
    weight_low = 0.1 / jnp.square(weno_epsilon + smooth_low)
    weight_mid = 0.6 / jnp.square(weno_epsilon + smooth_mid)
    weight_high = 0.3 / jnp.square(weno_epsilon + smooth_high)
    guess_low = (2.0 * far_left - 7.0 * left_cell + 11.0 * centre) / 6.0
    guess_mid = (-left_cell + 5.0 * centre + 2.0 * right_cell) / 6.0
    guess_high = (2.0 * centre + 5.0 * right_cell - far_right) / 6.0
    return (weight_low * guess_low + weight_mid * guess_mid + weight_high * guess_high) / (
        weight_low + weight_mid + weight_high
    )


def face_flux(padded, fluxes, axis, count, normal, first, second):
    states = [
        lax.slice_in_dim(padded, shift_index, shift_index + count + 1, axis=axis)
        for shift_index in range(6)
    ]
    physical = [
        lax.slice_in_dim(fluxes, shift_index, shift_index + count + 1, axis=axis)
        for shift_index in range(6)
    ]
    mean = 0.5 * (states[2] + states[3])
    density = mean[0]
    normal_speed = mean[normal] / density
    speed_first = mean[first] / density
    speed_second = mean[second] / density
    kinetic = 0.5 * (jnp.square(normal_speed) + jnp.square(speed_first) + jnp.square(speed_second))
    pressure = pressure_of(mean)
    sound = jnp.sqrt(gamma_ratio * pressure / density)
    enthalpy = (mean[4] + pressure) / density
    inv_sound = 1.0 / sound
    factor_one = (gamma_ratio - 1.0) * jnp.square(inv_sound)
    factor_two = factor_one * kinetic
    dissipation = jnp.maximum(wave_speed(states[2], normal), wave_speed(states[3], normal))

    def project(vector):
        dens_part = vector[0]
        norm_part = vector[normal]
        first_part = vector[first]
        second_part = vector[second]
        energy_part = vector[4]
        tangent_sum = factor_one * (
            speed_first * first_part + speed_second * second_part - energy_part
        )
        wave_minus = 0.5 * (
            (factor_two + normal_speed * inv_sound) * dens_part
            - (factor_one * normal_speed + inv_sound) * norm_part
            - tangent_sum
        )
        entropy = (
            (1.0 - factor_two) * dens_part + factor_one * normal_speed * norm_part + tangent_sum
        )
        shear_first = first_part - speed_first * dens_part
        shear_second = second_part - speed_second * dens_part
        wave_plus = 0.5 * (
            (factor_two - normal_speed * inv_sound) * dens_part
            - (factor_one * normal_speed - inv_sound) * norm_part
            - tangent_sum
        )
        return (wave_minus, entropy, shear_first, shear_second, wave_plus)

    state_chars = [project(cell_state) for cell_state in states]
    flux_chars = [project(cell_flux) for cell_flux in physical]
    recon = []
    for field_index in range(5):
        plus_vals = [
            0.5 * (flux_chars[cell][field_index] + dissipation * state_chars[cell][field_index])
            for cell in range(6)
        ]
        minus_vals = [
            0.5 * (flux_chars[cell][field_index] - dissipation * state_chars[cell][field_index])
            for cell in range(6)
        ]
        recon.append(
            weno_side(plus_vals[0], plus_vals[1], plus_vals[2], plus_vals[3], plus_vals[4])
            + weno_side(minus_vals[5], minus_vals[4], minus_vals[3], minus_vals[2], minus_vals[1])
        )
    wave_minus, entropy, shear_first, shear_second, wave_plus = recon
    acoustic = wave_minus + entropy + wave_plus
    parts = {}
    parts[0] = acoustic
    parts[normal] = (
        (normal_speed - sound) * wave_minus
        + normal_speed * entropy
        + (normal_speed + sound) * wave_plus
    )
    parts[first] = speed_first * acoustic + shear_first
    parts[second] = speed_second * acoustic + shear_second
    parts[4] = (
        (enthalpy - normal_speed * sound) * wave_minus
        + kinetic * entropy
        + speed_first * shear_first
        + speed_second * shear_second
        + (enthalpy + normal_speed * sound) * wave_plus
    )
    return jnp.stack([parts[index_part] for index_part in range(5)])


def divergence(padded, axis, count, normal, first, second):
    faces = face_flux(padded, euler_flux(padded, normal), axis, count, normal, first, second)
    return lax.slice_in_dim(faces, 1, count + 1, axis=axis) - lax.slice_in_dim(
        faces, 0, count, axis=axis
    )


def flip_radial(cells):
    turned = cells[:, :, ::-1]
    return jnp.concatenate([turned[:3], -turned[3:4], turned[4:]], axis=0)


def flip_theta(cells):
    return jnp.concatenate([cells[:2], -cells[2:3], cells[3:]], axis=0)


def hold(cells, value):
    return jnp.where(jnp.isnan(value.reshape(-1)[0]), jnp.zeros((), cells.dtype), cells)


def after(value, index):
    return index + jnp.isnan(value.reshape(-1)[0]).astype(jnp.int32)


def route_parts(rotor_step, width):
    rows = lax.axis_size("tx")
    columns = lax.axis_size("tz")
    turns = rotor_step[0] // 4 // width
    centre = (turns - 1) % (rows * columns)
    return rows, columns, centre // columns, centre % columns


def pick_column(slab, rotor_step, before):
    rows, columns, centre_row, centre_column = route_parts(rotor_step, slab.shape[3])
    source_column = (centre_column - lax.axis_index("tz")) % columns
    gathered = lax.all_gather(slab, "tz")
    return lax.dynamic_index_in_dim(gathered, after(before, source_column), 0, keepdims=False)


def pick_row(slab, rotor_step, before):
    rows, columns, centre_row, centre_column = route_parts(rotor_step, slab.shape[3])
    borrow = (lax.axis_index("tz") > centre_column).astype(jnp.int32)
    source_row = (centre_row - lax.axis_index("tx") - borrow) % rows
    gathered = lax.all_gather(slab, "tx")
    return lax.dynamic_index_in_dim(gathered, after(before, source_row), 0, keepdims=False)


def cross_blocks(slab):
    block_count = lax.axis_size("blk")
    slab_count = lax.axis_size("tx") * lax.axis_size("tz")
    this_route = []
    next_route = []
    for blk_from in range(block_count):
        blk_to = (blk_from + 1) % block_count
        for slab_from in range(slab_count):
            source = blk_from * slab_count + slab_from
            this_route.append((source, blk_to * slab_count + slab_from))
            next_route.append((source, blk_to * slab_count + (slab_from + 1) % slab_count))
    axes = ("blk", "tx", "tz")
    return lax.ppermute(slab, axes, this_route), lax.ppermute(slab, axes, next_route)


def window_of(this_slab, next_slab, rotor_step, before):
    width = this_slab.shape[3]
    remainder = after(before, rotor_step[0] // 4 % width)
    doubled = jnp.concatenate([next_slab, this_slab], axis=3)
    return lax.dynamic_slice_in_dim(doubled, width - 1 - remainder, width + 1, 3)


def axial_kernel(padded_ref, out_ref):
    padded = padded_ref[...]
    count = padded.shape[1] - 6
    pressure = pressure_of(padded)
    velocity = padded[1] / padded[0]
    parts = [padded[index_part] * velocity for index_part in range(5)]
    parts[1] = parts[1] + pressure
    parts[4] = parts[4] + pressure * velocity
    faces = face_flux(padded, jnp.stack(parts), 1, count, 1, 2, 3)
    out_ref[...] = faces


def axial_faces(padded):
    components, planes, bands, width = padded.shape
    lanes = 256
    block = (components, planes, bands, lanes)
    out_block = (components, planes - 5, bands, lanes)
    return pl.pallas_call(
        axial_kernel,
        grid=(width // lanes,),
        in_specs=[pl.BlockSpec(block, lambda i: (0, 0, 0, i))],
        out_specs=pl.BlockSpec(out_block, lambda i: (0, 0, 0, i)),
        out_shape=jax.ShapeDtypeStruct((components, planes - 5, bands, width), padded.dtype),
    )(padded)


def shards(base_state, section_state, rotor_step):
    planes = section_state.shape[1]
    bands = section_state.shape[2]
    width = section_state.shape[3]
    fraction = (rotor_step[0] % 4).astype(jnp.float32) / 4.0
    theta_padded = padded_2(section_state, ((("tx", "tz"), 3),), 3, True)
    radial_raw = padded_2(section_state, (("radial", 2),), 3, False)
    band_index = lax.axis_index("radial")
    band_count = lax.axis_size("radial")
    lower_wall = jnp.where(
        band_index == 0, flip_radial(section_state[:, :, :3]), radial_raw[:, :, :3]
    )
    upper_wall = jnp.where(
        band_index == band_count - 1, flip_radial(section_state[:, :, -3:]), radial_raw[:, :, -3:]
    )
    radial_padded = jnp.concatenate([lower_wall, section_state, upper_wall], axis=2)
    block_index = lax.axis_index("blk")
    front = block_index == 0
    outgoing = jnp.where(front, section_state[:, -3:], section_state[:, :3])[..., ::-1]
    radial = divergence(radial_padded, 2, bands, 3, 1, 2)
    chosen = pick_column(outgoing, rotor_step, radial)
    theta_padded = hold(theta_padded, chosen)
    azimuthal = divergence(theta_padded, 3, width, 2, 1, 3)
    chosen = pick_row(chosen, rotor_step, azimuthal)
    this_slab, next_slab = cross_blocks(chosen)
    edge_low = jnp.concatenate(
        [section_state[:, :1], section_state[:, :1], section_state[:, :1]], axis=1
    )
    edge_high = jnp.concatenate(
        [section_state[:, -1:], section_state[:, -1:], section_state[:, -1:]], axis=1
    )
    local_window = jnp.where(
        front,
        jnp.concatenate([edge_low, section_state], axis=1),
        jnp.concatenate([section_state, edge_high], axis=1),
    )
    local_window = hold(local_window, chosen)
    local_faces = axial_faces(local_window)
    settled = 0.75 * base_state + 0.25 * (section_state - step_ratio * (radial + azimuthal))
    window = window_of(this_slab, next_slab, rotor_step, local_faces + settled[:, :1, :, :1])
    ghost = flip_theta(
        (1.0 - fraction) * window[..., 1 : width + 1] + fraction * window[..., :width]
    )
    mortar_window = jnp.where(
        front,
        jnp.concatenate([section_state[:, 1:], ghost], axis=1),
        jnp.concatenate([ghost, section_state[:, :-1]], axis=1),
    )
    mortar_faces = axial_faces(mortar_window)
    faces = jnp.where(
        front,
        jnp.concatenate([local_faces, mortar_faces], axis=1),
        jnp.concatenate([mortar_faces, local_faces], axis=1),
    )
    axial = lax.slice_in_dim(faces, 1, planes + 1, axis=1) - lax.slice_in_dim(
        faces, 0, planes, axis=1
    )
    return settled - 0.25 * step_ratio * axial


def solution(mesh):
    blocks, slabs, bands = (mesh.shape[name] for name in ("blk", "theta", "radial"))
    rows = 4 if slabs % 4 == 0 else 1
    grid = jax.sharding.Mesh(
        mesh.devices.reshape(blocks, rows, slabs // rows, bands), ("blk", "tx", "tz", "radial")
    )
    in_specs = (P(None, "blk", "radial", ("tx", "tz")), P(None, "blk", "radial", ("tx", "tz")), P())
    out_specs = P(None, "blk", "radial", ("tx", "tz"))
    inner = jax.shard_map(shards, mesh=grid, in_specs=in_specs, out_specs=out_specs, check_vma=False)
    sharded = jax.sharding.NamedSharding(mesh, P(None, "blk", "radial", "theta"))

    def run(base_state, section_state, rotor_step):
        return jax.lax.with_sharding_constraint(
            inner(base_state, section_state, rotor_step), sharded
        )

    return run
```

```python
import jax
import jax.numpy as jnp
from jax import lax
from jax.sharding import PartitionSpec as P
from jax.experimental import pallas as pl

gamma_ratio = 1.4
weno_epsilon = 1e-06
step_ratio = 0.12


def padded_2(cells, sides, width, closed):
    for axis, dim in sides:
        count = lax.axis_size(axis)
        ends = count if closed else count - 1
        head = lax.slice_in_dim(cells, 0, width, axis=dim)
        tail = lax.slice_in_dim(cells, cells.shape[dim] - width, cells.shape[dim], axis=dim)
        cells = jnp.concatenate(
            [
                lax.ppermute(tail, axis, [(i, (i + 1) % count) for i in range(ends)]),
                cells,
                lax.ppermute(head, axis, [((i + 1) % count, i) for i in range(ends)]),
            ],
            axis=dim,
        )
    return cells


def partner(block, axis, distance):
    count = lax.axis_size(axis)
    route = []
    for low in range(count):
        high = low | 1 << distance
        if high != low and high < count:
            route += [(low, high), (high, low)]
    return lax.ppermute(block, axis, route)


def pressure_of(state):
    kinetic = 0.5 * (jnp.square(state[1]) + jnp.square(state[2]) + jnp.square(state[3])) / state[0]
    return (gamma_ratio - 1.0) * (state[4] - kinetic)


def euler_flux(state, normal):
    pressure = pressure_of(state)
    velocity = state[normal] / state[0]
    flux = state * velocity[None]
    flux = flux.at[normal].add(pressure)
    flux = flux.at[4].add(pressure * velocity)
    return flux


def wave_speed(state, normal):
    pressure = pressure_of(state)
    return jnp.abs(state[normal] / state[0]) + jnp.sqrt(gamma_ratio * pressure / state[0])


def weno_side(far_left, left_cell, centre, right_cell, far_right):
    smooth_low = 13.0 / 12.0 * jnp.square(far_left - 2.0 * left_cell + centre) + 0.25 * jnp.square(
        far_left - 4.0 * left_cell + 3.0 * centre
    )
    smooth_mid = 13.0 / 12.0 * jnp.square(
        left_cell - 2.0 * centre + right_cell
    ) + 0.25 * jnp.square(left_cell - right_cell)
    smooth_high = 13.0 / 12.0 * jnp.square(
        centre - 2.0 * right_cell + far_right
    ) + 0.25 * jnp.square(3.0 * centre - 4.0 * right_cell + far_right)
    weight_low = 0.1 / jnp.square(weno_epsilon + smooth_low)
    weight_mid = 0.6 / jnp.square(weno_epsilon + smooth_mid)
    weight_high = 0.3 / jnp.square(weno_epsilon + smooth_high)
    guess_low = (2.0 * far_left - 7.0 * left_cell + 11.0 * centre) / 6.0
    guess_mid = (-left_cell + 5.0 * centre + 2.0 * right_cell) / 6.0
    guess_high = (2.0 * centre + 5.0 * right_cell - far_right) / 6.0
    return (weight_low * guess_low + weight_mid * guess_mid + weight_high * guess_high) / (
        weight_low + weight_mid + weight_high
    )


def face_flux(padded, fluxes, axis, count, normal, first, second):
    states = [
        lax.slice_in_dim(padded, shift_index, shift_index + count + 1, axis=axis)
        for shift_index in range(6)
    ]
    physical = [
        lax.slice_in_dim(fluxes, shift_index, shift_index + count + 1, axis=axis)
        for shift_index in range(6)
    ]
    mean = 0.5 * (states[2] + states[3])
    density = mean[0]
    normal_speed = mean[normal] / density
    speed_first = mean[first] / density
    speed_second = mean[second] / density
    kinetic = 0.5 * (jnp.square(normal_speed) + jnp.square(speed_first) + jnp.square(speed_second))
    pressure = pressure_of(mean)
    sound = jnp.sqrt(gamma_ratio * pressure / density)
    enthalpy = (mean[4] + pressure) / density
    inv_sound = 1.0 / sound
    factor_one = (gamma_ratio - 1.0) * jnp.square(inv_sound)
    factor_two = factor_one * kinetic
    dissipation = jnp.maximum(wave_speed(states[2], normal), wave_speed(states[3], normal))

    def project(vector):
        dens_part = vector[0]
        norm_part = vector[normal]
        first_part = vector[first]
        second_part = vector[second]
        energy_part = vector[4]
        tangent_sum = factor_one * (
            speed_first * first_part + speed_second * second_part - energy_part
        )
        wave_minus = 0.5 * (
            (factor_two + normal_speed * inv_sound) * dens_part
            - (factor_one * normal_speed + inv_sound) * norm_part
            - tangent_sum
        )
        entropy = (
            (1.0 - factor_two) * dens_part + factor_one * normal_speed * norm_part + tangent_sum
        )
        shear_first = first_part - speed_first * dens_part
        shear_second = second_part - speed_second * dens_part
        wave_plus = 0.5 * (
            (factor_two - normal_speed * inv_sound) * dens_part
            - (factor_one * normal_speed - inv_sound) * norm_part
            - tangent_sum
        )
        return (wave_minus, entropy, shear_first, shear_second, wave_plus)

    state_chars = [project(cell_state) for cell_state in states]
    flux_chars = [project(cell_flux) for cell_flux in physical]
    recon = []
    for field_index in range(5):
        plus_vals = [
            0.5 * (flux_chars[cell][field_index] + dissipation * state_chars[cell][field_index])
            for cell in range(6)
        ]
        minus_vals = [
            0.5 * (flux_chars[cell][field_index] - dissipation * state_chars[cell][field_index])
            for cell in range(6)
        ]
        recon.append(
            weno_side(plus_vals[0], plus_vals[1], plus_vals[2], plus_vals[3], plus_vals[4])
            + weno_side(minus_vals[5], minus_vals[4], minus_vals[3], minus_vals[2], minus_vals[1])
        )
    wave_minus, entropy, shear_first, shear_second, wave_plus = recon
    acoustic = wave_minus + entropy + wave_plus
    parts = {}
    parts[0] = acoustic
    parts[normal] = (
        (normal_speed - sound) * wave_minus
        + normal_speed * entropy
        + (normal_speed + sound) * wave_plus
    )
    parts[first] = speed_first * acoustic + shear_first
    parts[second] = speed_second * acoustic + shear_second
    parts[4] = (
        (enthalpy - normal_speed * sound) * wave_minus
        + kinetic * entropy
        + speed_first * shear_first
        + speed_second * shear_second
        + (enthalpy + normal_speed * sound) * wave_plus
    )
    return jnp.stack([parts[index_part] for index_part in range(5)])


def divergence(padded, axis, count, normal, first, second):
    faces = face_flux(padded, euler_flux(padded, normal), axis, count, normal, first, second)
    return lax.slice_in_dim(faces, 1, count + 1, axis=axis) - lax.slice_in_dim(
        faces, 0, count, axis=axis
    )


def flip_radial(cells):
    turned = cells[:, :, ::-1]
    return jnp.concatenate([turned[:3], -turned[3:4], turned[4:]], axis=0)


def flip_theta(cells):
    return jnp.concatenate([cells[:2], -cells[2:3], cells[3:]], axis=0)


def hold(cells, value):
    return jnp.where(jnp.isnan(value.reshape(-1)[0]), jnp.zeros((), cells.dtype), cells)


def after(value, index):
    return index + jnp.isnan(value.reshape(-1)[0]).astype(jnp.int32)


def route_parts(rotor_step, width):
    rows = lax.axis_size("tx")
    columns = lax.axis_size("tz")
    turns = rotor_step[0] // 4 // width
    centre = (turns - 1) % (rows * columns)
    return rows, columns, centre // columns, centre % columns


def pick_column(slab, rotor_step, before):
    rows, columns, centre_row, centre_column = route_parts(rotor_step, slab.shape[3])
    source_column = (centre_column - lax.axis_index("tz")) % columns
    gathered = lax.all_gather(slab, "tz")
    return lax.dynamic_index_in_dim(gathered, after(before, source_column), 0, keepdims=False)


def pick_row(slab, rotor_step, before):
    rows, columns, centre_row, centre_column = route_parts(rotor_step, slab.shape[3])
    borrow = (lax.axis_index("tz") > centre_column).astype(jnp.int32)
    source_row = (centre_row - lax.axis_index("tx") - borrow) % rows
    gathered = lax.all_gather(slab, "tx")
    return lax.dynamic_index_in_dim(gathered, after(before, source_row), 0, keepdims=False)


def cross_blocks(slab):
    block_count = lax.axis_size("blk")
    slab_count = lax.axis_size("tx") * lax.axis_size("tz")
    this_route = []
    next_route = []
    for blk_from in range(block_count):
        blk_to = (blk_from + 1) % block_count
        for slab_from in range(slab_count):
            source = blk_from * slab_count + slab_from
            this_route.append((source, blk_to * slab_count + slab_from))
            next_route.append((source, blk_to * slab_count + (slab_from + 1) % slab_count))
    axes = ("blk", "tx", "tz")
    return lax.ppermute(slab, axes, this_route), lax.ppermute(slab, axes, next_route)


def window_of(this_slab, next_slab, rotor_step, before):
    width = this_slab.shape[3]
    remainder = after(before, rotor_step[0] // 4 % width)
    doubled = jnp.concatenate([next_slab, this_slab], axis=3)
    return lax.dynamic_slice_in_dim(doubled, width - 1 - remainder, width + 1, 3)


def axial_kernel(padded_ref, out_ref):
    padded = padded_ref[...]
    count = padded.shape[1] - 6
    pressure = pressure_of(padded)
    velocity = padded[1] / padded[0]
    parts = [padded[index_part] * velocity for index_part in range(5)]
    parts[1] = parts[1] + pressure
    parts[4] = parts[4] + pressure * velocity
    faces = face_flux(padded, jnp.stack(parts), 1, count, 1, 2, 3)
    out_ref[...] = faces


def axial_faces(padded):
    components, planes, bands, width = padded.shape
    lanes = 512
    block = (components, planes, bands, lanes)
    out_block = (components, planes - 5, bands, lanes)
    return pl.pallas_call(
        axial_kernel,
        grid=(width // lanes,),
        in_specs=[pl.BlockSpec(block, lambda i: (0, 0, 0, i))],
        out_specs=pl.BlockSpec(out_block, lambda i: (0, 0, 0, i)),
        out_shape=jax.ShapeDtypeStruct((components, planes - 5, bands, width), padded.dtype),
    )(padded)


def shards(base_state, section_state, rotor_step):
    planes = section_state.shape[1]
    bands = section_state.shape[2]
    width = section_state.shape[3]
    fraction = (rotor_step[0] % 4).astype(jnp.float32) / 4.0
    theta_padded = padded_2(section_state, ((("tx", "tz"), 3),), 3, True)
    radial_raw = padded_2(section_state, (("radial", 2),), 3, False)
    band_index = lax.axis_index("radial")
    band_count = lax.axis_size("radial")
    lower_wall = jnp.where(
        band_index == 0, flip_radial(section_state[:, :, :3]), radial_raw[:, :, :3]
    )
    upper_wall = jnp.where(
        band_index == band_count - 1, flip_radial(section_state[:, :, -3:]), radial_raw[:, :, -3:]
    )
    radial_padded = jnp.concatenate([lower_wall, section_state, upper_wall], axis=2)
    block_index = lax.axis_index("blk")
    front = block_index == 0
    outgoing = jnp.where(front, section_state[:, -3:], section_state[:, :3])[..., ::-1]
    radial = divergence(radial_padded, 2, bands, 3, 1, 2)
    chosen = pick_column(outgoing, rotor_step, radial)
    theta_padded = hold(theta_padded, chosen)
    azimuthal = divergence(theta_padded, 3, width, 2, 1, 3)
    chosen = pick_row(chosen, rotor_step, azimuthal)
    this_slab, next_slab = cross_blocks(chosen)
    edge_low = jnp.concatenate(
        [section_state[:, :1], section_state[:, :1], section_state[:, :1]], axis=1
    )
    edge_high = jnp.concatenate(
        [section_state[:, -1:], section_state[:, -1:], section_state[:, -1:]], axis=1
    )
    local_window = jnp.where(
        front,
        jnp.concatenate([edge_low, section_state], axis=1),
        jnp.concatenate([section_state, edge_high], axis=1),
    )
    local_window = hold(local_window, chosen)
    local_faces = axial_faces(local_window)
    settled = 0.75 * base_state + 0.25 * (section_state - step_ratio * (radial + azimuthal))
    window = window_of(this_slab, next_slab, rotor_step, local_faces + settled[:, :1, :, :1])
    ghost = flip_theta(
        (1.0 - fraction) * window[..., 1 : width + 1] + fraction * window[..., :width]
    )
    mortar_window = jnp.where(
        front,
        jnp.concatenate([section_state[:, 1:], ghost], axis=1),
        jnp.concatenate([ghost, section_state[:, :-1]], axis=1),
    )
    mortar_faces = axial_faces(mortar_window)
    faces = jnp.where(
        front,
        jnp.concatenate([local_faces, mortar_faces], axis=1),
        jnp.concatenate([mortar_faces, local_faces], axis=1),
    )
    axial = lax.slice_in_dim(faces, 1, planes + 1, axis=1) - lax.slice_in_dim(
        faces, 0, planes, axis=1
    )
    return settled - 0.25 * step_ratio * axial


def solution(mesh):
    blocks, slabs, bands = (mesh.shape[name] for name in ("blk", "theta", "radial"))
    rows = 4 if slabs % 4 == 0 else 1
    grid = jax.sharding.Mesh(
        mesh.devices.reshape(blocks, rows, slabs // rows, bands), ("blk", "tx", "tz", "radial")
    )
    in_specs = (P(None, "blk", "radial", ("tx", "tz")), P(None, "blk", "radial", ("tx", "tz")), P())
    out_specs = P(None, "blk", "radial", ("tx", "tz"))
    inner = jax.shard_map(shards, mesh=grid, in_specs=in_specs, out_specs=out_specs, check_vma=False)
    sharded = jax.sharding.NamedSharding(mesh, P(None, "blk", "radial", "theta"))

    def run(base_state, section_state, rotor_step):
        return jax.lax.with_sharding_constraint(
            inner(base_state, section_state, rotor_step), sharded
        )

    return run
```

```python
import jax
import jax.numpy as jnp
from jax import lax
from jax.sharding import PartitionSpec as P
from jax.experimental import pallas as pl

gamma_ratio = 1.4
weno_epsilon = 1e-06
step_ratio = 0.12


def padded_2(cells, sides, width, closed):
    for axis, dim in sides:
        count = lax.axis_size(axis)
        ends = count if closed else count - 1
        head = lax.slice_in_dim(cells, 0, width, axis=dim)
        tail = lax.slice_in_dim(cells, cells.shape[dim] - width, cells.shape[dim], axis=dim)
        cells = jnp.concatenate(
            [
                lax.ppermute(tail, axis, [(i, (i + 1) % count) for i in range(ends)]),
                cells,
                lax.ppermute(head, axis, [((i + 1) % count, i) for i in range(ends)]),
            ],
            axis=dim,
        )
    return cells


def partner(block, axis, distance):
    count = lax.axis_size(axis)
    route = []
    for low in range(count):
        high = low | 1 << distance
        if high != low and high < count:
            route += [(low, high), (high, low)]
    return lax.ppermute(block, axis, route)


def pressure_of(state):
    kinetic = 0.5 * (jnp.square(state[1]) + jnp.square(state[2]) + jnp.square(state[3])) / state[0]
    return (gamma_ratio - 1.0) * (state[4] - kinetic)


def euler_flux(state, normal):
    pressure = pressure_of(state)
    velocity = state[normal] / state[0]
    flux = state * velocity[None]
    flux = flux.at[normal].add(pressure)
    flux = flux.at[4].add(pressure * velocity)
    return flux


def wave_speed(state, normal):
    pressure = pressure_of(state)
    return jnp.abs(state[normal] / state[0]) + jnp.sqrt(gamma_ratio * pressure / state[0])


def weno_side(far_left, left_cell, centre, right_cell, far_right):
    smooth_low = 13.0 / 12.0 * jnp.square(far_left - 2.0 * left_cell + centre) + 0.25 * jnp.square(
        far_left - 4.0 * left_cell + 3.0 * centre
    )
    smooth_mid = 13.0 / 12.0 * jnp.square(
        left_cell - 2.0 * centre + right_cell
    ) + 0.25 * jnp.square(left_cell - right_cell)
    smooth_high = 13.0 / 12.0 * jnp.square(
        centre - 2.0 * right_cell + far_right
    ) + 0.25 * jnp.square(3.0 * centre - 4.0 * right_cell + far_right)
    weight_low = 0.1 / jnp.square(weno_epsilon + smooth_low)
    weight_mid = 0.6 / jnp.square(weno_epsilon + smooth_mid)
    weight_high = 0.3 / jnp.square(weno_epsilon + smooth_high)
    guess_low = (2.0 * far_left - 7.0 * left_cell + 11.0 * centre) / 6.0
    guess_mid = (-left_cell + 5.0 * centre + 2.0 * right_cell) / 6.0
    guess_high = (2.0 * centre + 5.0 * right_cell - far_right) / 6.0
    return (weight_low * guess_low + weight_mid * guess_mid + weight_high * guess_high) / (
        weight_low + weight_mid + weight_high
    )


def weno_merged(far_left, left_cell, centre, right_cell, far_right):
    smooth_low = 13.0 / 12.0 * jnp.square(far_left - 2.0 * left_cell + centre) + 0.25 * jnp.square(
        far_left - 4.0 * left_cell + 3.0 * centre
    )
    smooth_mid = 13.0 / 12.0 * jnp.square(
        left_cell - 2.0 * centre + right_cell
    ) + 0.25 * jnp.square(left_cell - right_cell)
    smooth_high = 13.0 / 12.0 * jnp.square(
        centre - 2.0 * right_cell + far_right
    ) + 0.25 * jnp.square(3.0 * centre - 4.0 * right_cell + far_right)
    spread_low = jnp.square(weno_epsilon + smooth_low)
    spread_mid = jnp.square(weno_epsilon + smooth_mid)
    spread_high = jnp.square(weno_epsilon + smooth_high)
    weight_low = 0.1 * (spread_mid * spread_high)
    weight_mid = 0.6 * (spread_low * spread_high)
    weight_high = 0.3 * (spread_low * spread_mid)
    guess_low = 2.0 * far_left - 7.0 * left_cell + 11.0 * centre
    guess_mid = -left_cell + 5.0 * centre + 2.0 * right_cell
    guess_high = 2.0 * centre + 5.0 * right_cell - far_right
    return (weight_low * guess_low + weight_mid * guess_mid + weight_high * guess_high) / (
        6.0 * (weight_low + weight_mid + weight_high)
    )


def face_flux(padded, fluxes, axis, count, normal, first, second, weno=weno_side):
    states = [
        lax.slice_in_dim(padded, shift_index, shift_index + count + 1, axis=axis)
        for shift_index in range(6)
    ]
    physical = [
        lax.slice_in_dim(fluxes, shift_index, shift_index + count + 1, axis=axis)
        for shift_index in range(6)
    ]
    mean = 0.5 * (states[2] + states[3])
    density = mean[0]
    normal_speed = mean[normal] / density
    speed_first = mean[first] / density
    speed_second = mean[second] / density
    kinetic = 0.5 * (jnp.square(normal_speed) + jnp.square(speed_first) + jnp.square(speed_second))
    pressure = pressure_of(mean)
    sound = jnp.sqrt(gamma_ratio * pressure / density)
    enthalpy = (mean[4] + pressure) / density
    inv_sound = 1.0 / sound
    factor_one = (gamma_ratio - 1.0) * jnp.square(inv_sound)
    factor_two = factor_one * kinetic
    dissipation = jnp.maximum(wave_speed(states[2], normal), wave_speed(states[3], normal))

    def project(vector):
        dens_part = vector[0]
        norm_part = vector[normal]
        first_part = vector[first]
        second_part = vector[second]
        energy_part = vector[4]
        tangent_sum = factor_one * (
            speed_first * first_part + speed_second * second_part - energy_part
        )
        wave_minus = 0.5 * (
            (factor_two + normal_speed * inv_sound) * dens_part
            - (factor_one * normal_speed + inv_sound) * norm_part
            - tangent_sum
        )
        entropy = (
            (1.0 - factor_two) * dens_part + factor_one * normal_speed * norm_part + tangent_sum
        )
        shear_first = first_part - speed_first * dens_part
        shear_second = second_part - speed_second * dens_part
        wave_plus = 0.5 * (
            (factor_two - normal_speed * inv_sound) * dens_part
            - (factor_one * normal_speed - inv_sound) * norm_part
            - tangent_sum
        )
        return (wave_minus, entropy, shear_first, shear_second, wave_plus)

    state_chars = [project(cell_state) for cell_state in states]
    flux_chars = [project(cell_flux) for cell_flux in physical]
    recon = []
    for field_index in range(5):
        plus_vals = [
            0.5 * (flux_chars[cell][field_index] + dissipation * state_chars[cell][field_index])
            for cell in range(6)
        ]
        minus_vals = [
            0.5 * (flux_chars[cell][field_index] - dissipation * state_chars[cell][field_index])
            for cell in range(6)
        ]
        recon.append(
            weno(plus_vals[0], plus_vals[1], plus_vals[2], plus_vals[3], plus_vals[4])
            + weno(minus_vals[5], minus_vals[4], minus_vals[3], minus_vals[2], minus_vals[1])
        )
    wave_minus, entropy, shear_first, shear_second, wave_plus = recon
    acoustic = wave_minus + entropy + wave_plus
    parts = {}
    parts[0] = acoustic
    parts[normal] = (
        (normal_speed - sound) * wave_minus
        + normal_speed * entropy
        + (normal_speed + sound) * wave_plus
    )
    parts[first] = speed_first * acoustic + shear_first
    parts[second] = speed_second * acoustic + shear_second
    parts[4] = (
        (enthalpy - normal_speed * sound) * wave_minus
        + kinetic * entropy
        + speed_first * shear_first
        + speed_second * shear_second
        + (enthalpy + normal_speed * sound) * wave_plus
    )
    return jnp.stack([parts[index_part] for index_part in range(5)])


def divergence(padded, axis, count, normal, first, second):
    faces = face_flux(padded, euler_flux(padded, normal), axis, count, normal, first, second)
    return lax.slice_in_dim(faces, 1, count + 1, axis=axis) - lax.slice_in_dim(
        faces, 0, count, axis=axis
    )


def flip_radial(cells):
    turned = cells[:, :, ::-1]
    return jnp.concatenate([turned[:3], -turned[3:4], turned[4:]], axis=0)


def flip_theta(cells):
    return jnp.concatenate([cells[:2], -cells[2:3], cells[3:]], axis=0)


def hold(cells, value):
    return jnp.where(jnp.isnan(value.reshape(-1)[0]), jnp.zeros((), cells.dtype), cells)


def after(value, index):
    return index + jnp.isnan(value.reshape(-1)[0]).astype(jnp.int32)


def route_parts(rotor_step, width):
    rows = lax.axis_size("tx")
    columns = lax.axis_size("tz")
    turns = rotor_step[0] // 4 // width
    centre = (turns - 1) % (rows * columns)
    return rows, columns, centre // columns, centre % columns


def pick_column(slab, rotor_step, before):
    rows, columns, centre_row, centre_column = route_parts(rotor_step, slab.shape[3])
    source_column = (centre_column - lax.axis_index("tz")) % columns
    gathered = lax.all_gather(slab, "tz")
    return lax.dynamic_index_in_dim(gathered, after(before, source_column), 0, keepdims=False)


def pick_row(slab, rotor_step, before):
    rows, columns, centre_row, centre_column = route_parts(rotor_step, slab.shape[3])
    borrow = (lax.axis_index("tz") > centre_column).astype(jnp.int32)
    source_row = (centre_row - lax.axis_index("tx") - borrow) % rows
    gathered = lax.all_gather(slab, "tx")
    return lax.dynamic_index_in_dim(gathered, after(before, source_row), 0, keepdims=False)


def cross_blocks(slab):
    block_count = lax.axis_size("blk")
    slab_count = lax.axis_size("tx") * lax.axis_size("tz")
    this_route = []
    next_route = []
    for blk_from in range(block_count):
        blk_to = (blk_from + 1) % block_count
        for slab_from in range(slab_count):
            source = blk_from * slab_count + slab_from
            this_route.append((source, blk_to * slab_count + slab_from))
            next_route.append((source, blk_to * slab_count + (slab_from + 1) % slab_count))
    axes = ("blk", "tx", "tz")
    return lax.ppermute(slab, axes, this_route), lax.ppermute(slab, axes, next_route)


def window_of(this_slab, next_slab, rotor_step, before):
    width = this_slab.shape[3]
    remainder = after(before, rotor_step[0] // 4 % width)
    doubled = jnp.concatenate([next_slab, this_slab], axis=3)
    return lax.dynamic_slice_in_dim(doubled, width - 1 - remainder, width + 1, 3)


def axial_kernel(padded_ref, out_ref):
    padded = padded_ref[...]
    count = padded.shape[1] - 6
    pressure = pressure_of(padded)
    velocity = padded[1] / padded[0]
    parts = [padded[index_part] * velocity for index_part in range(5)]
    parts[1] = parts[1] + pressure
    parts[4] = parts[4] + pressure * velocity
    faces = face_flux(padded, jnp.stack(parts), 1, count, 1, 2, 3, weno_merged)
    out_ref[...] = faces


def axial_faces(padded):
    components, planes, bands, width = padded.shape
    lanes = 256
    block = (components, planes, bands, lanes)
    out_block = (components, planes - 5, bands, lanes)
    return pl.pallas_call(
        axial_kernel,
        grid=(width // lanes,),
        in_specs=[pl.BlockSpec(block, lambda i: (0, 0, 0, i))],
        out_specs=pl.BlockSpec(out_block, lambda i: (0, 0, 0, i)),
        out_shape=jax.ShapeDtypeStruct((components, planes - 5, bands, width), padded.dtype),
    )(padded)


def shards(base_state, section_state, rotor_step):
    planes = section_state.shape[1]
    bands = section_state.shape[2]
    width = section_state.shape[3]
    fraction = (rotor_step[0] % 4).astype(jnp.float32) / 4.0
    theta_padded = padded_2(section_state, ((("tx", "tz"), 3),), 3, True)
    radial_raw = padded_2(section_state, (("radial", 2),), 3, False)
    band_index = lax.axis_index("radial")
    band_count = lax.axis_size("radial")
    lower_wall = jnp.where(
        band_index == 0, flip_radial(section_state[:, :, :3]), radial_raw[:, :, :3]
    )
    upper_wall = jnp.where(
        band_index == band_count - 1, flip_radial(section_state[:, :, -3:]), radial_raw[:, :, -3:]
    )
    radial_padded = jnp.concatenate([lower_wall, section_state, upper_wall], axis=2)
    block_index = lax.axis_index("blk")
    front = block_index == 0
    outgoing = jnp.where(front, section_state[:, -3:], section_state[:, :3])[..., ::-1]
    radial = divergence(radial_padded, 2, bands, 3, 1, 2)
    chosen = pick_column(outgoing, rotor_step, radial)
    theta_padded = hold(theta_padded, chosen)
    azimuthal = divergence(theta_padded, 3, width, 2, 1, 3)
    chosen = pick_row(chosen, rotor_step, azimuthal)
    this_slab, next_slab = cross_blocks(chosen)
    edge_low = jnp.concatenate(
        [section_state[:, :1], section_state[:, :1], section_state[:, :1]], axis=1
    )
    edge_high = jnp.concatenate(
        [section_state[:, -1:], section_state[:, -1:], section_state[:, -1:]], axis=1
    )
    local_window = jnp.where(
        front,
        jnp.concatenate([edge_low, section_state], axis=1),
        jnp.concatenate([section_state, edge_high], axis=1),
    )
    local_window = hold(local_window, chosen)
    local_faces = axial_faces(local_window)
    settled = 0.75 * base_state + 0.25 * (section_state - step_ratio * (radial + azimuthal))
    window = window_of(this_slab, next_slab, rotor_step, local_faces + settled[:, :1, :, :1])
    ghost = flip_theta(
        (1.0 - fraction) * window[..., 1 : width + 1] + fraction * window[..., :width]
    )
    mortar_window = jnp.where(
        front,
        jnp.concatenate([section_state[:, 1:], ghost], axis=1),
        jnp.concatenate([ghost, section_state[:, :-1]], axis=1),
    )
    mortar_faces = axial_faces(mortar_window)
    faces = jnp.where(
        front,
        jnp.concatenate([local_faces, mortar_faces], axis=1),
        jnp.concatenate([mortar_faces, local_faces], axis=1),
    )
    axial = lax.slice_in_dim(faces, 1, planes + 1, axis=1) - lax.slice_in_dim(
        faces, 0, planes, axis=1
    )
    return settled - 0.25 * step_ratio * axial


def solution(mesh):
    blocks, slabs, bands = (mesh.shape[name] for name in ("blk", "theta", "radial"))
    rows = 4 if slabs % 4 == 0 else 1
    grid = jax.sharding.Mesh(
        mesh.devices.reshape(blocks, rows, slabs // rows, bands), ("blk", "tx", "tz", "radial")
    )
    in_specs = (P(None, "blk", "radial", ("tx", "tz")), P(None, "blk", "radial", ("tx", "tz")), P())
    out_specs = P(None, "blk", "radial", ("tx", "tz"))
    inner = jax.shard_map(shards, mesh=grid, in_specs=in_specs, out_specs=out_specs, check_vma=False)
    sharded = jax.sharding.NamedSharding(mesh, P(None, "blk", "radial", "theta"))

    def run(base_state, section_state, rotor_step):
        return jax.lax.with_sharding_constraint(
            inner(base_state, section_state, rotor_step), sharded
        )

    return run
```

```python
import jax
import jax.numpy as jnp
from jax import lax
from jax.sharding import PartitionSpec as P
from jax.experimental import pallas as pl
from jax.experimental.pallas import tpu as pltpu

gamma_ratio = 1.4
weno_epsilon = 1e-06
step_ratio = 0.12


def padded_2(cells, sides, width, closed):
    for axis, dim in sides:
        count = lax.axis_size(axis)
        ends = count if closed else count - 1
        head = lax.slice_in_dim(cells, 0, width, axis=dim)
        tail = lax.slice_in_dim(cells, cells.shape[dim] - width, cells.shape[dim], axis=dim)
        cells = jnp.concatenate(
            [
                lax.ppermute(tail, axis, [(i, (i + 1) % count) for i in range(ends)]),
                cells,
                lax.ppermute(head, axis, [((i + 1) % count, i) for i in range(ends)]),
            ],
            axis=dim,
        )
    return cells


def partner(block, axis, distance):
    count = lax.axis_size(axis)
    route = []
    for low in range(count):
        high = low | 1 << distance
        if high != low and high < count:
            route += [(low, high), (high, low)]
    return lax.ppermute(block, axis, route)


def pressure_of(state):
    kinetic = 0.5 * (jnp.square(state[1]) + jnp.square(state[2]) + jnp.square(state[3])) / state[0]
    return (gamma_ratio - 1.0) * (state[4] - kinetic)


def euler_flux(state, normal):
    pressure = pressure_of(state)
    velocity = state[normal] / state[0]
    flux = state * velocity[None]
    flux = flux.at[normal].add(pressure)
    flux = flux.at[4].add(pressure * velocity)
    return flux


def wave_speed(state, normal):
    pressure = pressure_of(state)
    return jnp.abs(state[normal] / state[0]) + jnp.sqrt(gamma_ratio * pressure / state[0])


def weno_side(far_left, left_cell, centre, right_cell, far_right):
    smooth_low = 13.0 / 12.0 * jnp.square(far_left - 2.0 * left_cell + centre) + 0.25 * jnp.square(
        far_left - 4.0 * left_cell + 3.0 * centre
    )
    smooth_mid = 13.0 / 12.0 * jnp.square(
        left_cell - 2.0 * centre + right_cell
    ) + 0.25 * jnp.square(left_cell - right_cell)
    smooth_high = 13.0 / 12.0 * jnp.square(
        centre - 2.0 * right_cell + far_right
    ) + 0.25 * jnp.square(3.0 * centre - 4.0 * right_cell + far_right)
    weight_low = 0.1 / jnp.square(weno_epsilon + smooth_low)
    weight_mid = 0.6 / jnp.square(weno_epsilon + smooth_mid)
    weight_high = 0.3 / jnp.square(weno_epsilon + smooth_high)
    guess_low = (2.0 * far_left - 7.0 * left_cell + 11.0 * centre) / 6.0
    guess_mid = (-left_cell + 5.0 * centre + 2.0 * right_cell) / 6.0
    guess_high = (2.0 * centre + 5.0 * right_cell - far_right) / 6.0
    return (weight_low * guess_low + weight_mid * guess_mid + weight_high * guess_high) / (
        weight_low + weight_mid + weight_high
    )


def face_flux(padded, fluxes, axis, count, normal, first, second):
    states = [
        lax.slice_in_dim(padded, shift_index, shift_index + count + 1, axis=axis)
        for shift_index in range(6)
    ]
    physical = [
        lax.slice_in_dim(fluxes, shift_index, shift_index + count + 1, axis=axis)
        for shift_index in range(6)
    ]
    mean = 0.5 * (states[2] + states[3])
    density = mean[0]
    normal_speed = mean[normal] / density
    speed_first = mean[first] / density
    speed_second = mean[second] / density
    kinetic = 0.5 * (jnp.square(normal_speed) + jnp.square(speed_first) + jnp.square(speed_second))
    pressure = pressure_of(mean)
    sound = jnp.sqrt(gamma_ratio * pressure / density)
    enthalpy = (mean[4] + pressure) / density
    inv_sound = 1.0 / sound
    factor_one = (gamma_ratio - 1.0) * jnp.square(inv_sound)
    factor_two = factor_one * kinetic
    dissipation = jnp.maximum(wave_speed(states[2], normal), wave_speed(states[3], normal))

    def project(vector):
        dens_part = vector[0]
        norm_part = vector[normal]
        first_part = vector[first]
        second_part = vector[second]
        energy_part = vector[4]
        tangent_sum = factor_one * (
            speed_first * first_part + speed_second * second_part - energy_part
        )
        wave_minus = 0.5 * (
            (factor_two + normal_speed * inv_sound) * dens_part
            - (factor_one * normal_speed + inv_sound) * norm_part
            - tangent_sum
        )
        entropy = (
            (1.0 - factor_two) * dens_part + factor_one * normal_speed * norm_part + tangent_sum
        )
        shear_first = first_part - speed_first * dens_part
        shear_second = second_part - speed_second * dens_part
        wave_plus = 0.5 * (
            (factor_two - normal_speed * inv_sound) * dens_part
            - (factor_one * normal_speed - inv_sound) * norm_part
            - tangent_sum
        )
        return (wave_minus, entropy, shear_first, shear_second, wave_plus)

    state_chars = [project(cell_state) for cell_state in states]
    flux_chars = [project(cell_flux) for cell_flux in physical]
    recon = []
    for field_index in range(5):
        plus_vals = [
            0.5 * (flux_chars[cell][field_index] + dissipation * state_chars[cell][field_index])
            for cell in range(6)
        ]
        minus_vals = [
            0.5 * (flux_chars[cell][field_index] - dissipation * state_chars[cell][field_index])
            for cell in range(6)
        ]
        recon.append(
            weno_side(plus_vals[0], plus_vals[1], plus_vals[2], plus_vals[3], plus_vals[4])
            + weno_side(minus_vals[5], minus_vals[4], minus_vals[3], minus_vals[2], minus_vals[1])
        )
    wave_minus, entropy, shear_first, shear_second, wave_plus = recon
    acoustic = wave_minus + entropy + wave_plus
    parts = {}
    parts[0] = acoustic
    parts[normal] = (
        (normal_speed - sound) * wave_minus
        + normal_speed * entropy
        + (normal_speed + sound) * wave_plus
    )
    parts[first] = speed_first * acoustic + shear_first
    parts[second] = speed_second * acoustic + shear_second
    parts[4] = (
        (enthalpy - normal_speed * sound) * wave_minus
        + kinetic * entropy
        + speed_first * shear_first
        + speed_second * shear_second
        + (enthalpy + normal_speed * sound) * wave_plus
    )
    return jnp.stack([parts[index_part] for index_part in range(5)])


def divergence(padded, axis, count, normal, first, second):
    faces = face_flux(padded, euler_flux(padded, normal), axis, count, normal, first, second)
    return lax.slice_in_dim(faces, 1, count + 1, axis=axis) - lax.slice_in_dim(
        faces, 0, count, axis=axis
    )


def flip_radial(cells):
    turned = cells[:, :, ::-1]
    return jnp.concatenate([turned[:3], -turned[3:4], turned[4:]], axis=0)


def flip_theta(cells):
    return jnp.concatenate([cells[:2], -cells[2:3], cells[3:]], axis=0)


def hold(cells, value):
    return jnp.where(jnp.isnan(value.reshape(-1)[0]), jnp.zeros((), cells.dtype), cells)


def after(value, index):
    return index + jnp.isnan(value.reshape(-1)[0]).astype(jnp.int32)


def route_parts(rotor_step, width):
    rows = lax.axis_size("tx")
    columns = lax.axis_size("tz")
    turns = rotor_step[0] // 4 // width
    centre = (turns - 1) % (rows * columns)
    return rows, columns, centre // columns, centre % columns


def pick_column(slab, rotor_step, before):
    rows, columns, centre_row, centre_column = route_parts(rotor_step, slab.shape[3])
    source_column = (centre_column - lax.axis_index("tz")) % columns
    gathered = lax.all_gather(slab, "tz")
    return lax.dynamic_index_in_dim(gathered, after(before, source_column), 0, keepdims=False)


def pick_row(slab, rotor_step, before):
    rows, columns, centre_row, centre_column = route_parts(rotor_step, slab.shape[3])
    borrow = (lax.axis_index("tz") > centre_column).astype(jnp.int32)
    source_row = (centre_row - lax.axis_index("tx") - borrow) % rows
    gathered = lax.all_gather(slab, "tx")
    return lax.dynamic_index_in_dim(gathered, after(before, source_row), 0, keepdims=False)


def cross_blocks(slab):
    block_count = lax.axis_size("blk")
    slab_count = lax.axis_size("tx") * lax.axis_size("tz")
    this_route = []
    next_route = []
    for blk_from in range(block_count):
        blk_to = (blk_from + 1) % block_count
        for slab_from in range(slab_count):
            source = blk_from * slab_count + slab_from
            this_route.append((source, blk_to * slab_count + slab_from))
            next_route.append((source, blk_to * slab_count + (slab_from + 1) % slab_count))
    axes = ("blk", "tx", "tz")
    return lax.ppermute(slab, axes, this_route), lax.ppermute(slab, axes, next_route)


def window_of(this_slab, next_slab, rotor_step, before):
    width = this_slab.shape[3]
    remainder = after(before, rotor_step[0] // 4 % width)
    doubled = jnp.concatenate([next_slab, this_slab], axis=3)
    return lax.dynamic_slice_in_dim(doubled, width - 1 - remainder, width + 1, 3)


def axial_kernel(padded_ref, out_ref):
    padded = padded_ref[...]
    count = padded.shape[1] - 6
    pressure = pressure_of(padded)
    velocity = padded[1] / padded[0]
    parts = [padded[index_part] * velocity for index_part in range(5)]
    parts[1] = parts[1] + pressure
    parts[4] = parts[4] + pressure * velocity
    faces = face_flux(padded, jnp.stack(parts), 1, count, 1, 2, 3)
    out_ref[...] = faces


def axial_faces(padded):
    components, planes, bands, width = padded.shape
    lanes = 256
    block = (components, planes, bands, lanes)
    out_block = (components, planes - 5, bands, lanes)
    return pl.pallas_call(
        axial_kernel,
        grid=(width // lanes,),
        in_specs=[pl.BlockSpec(block, lambda i: (0, 0, 0, i))],
        out_specs=pl.BlockSpec(out_block, lambda i: (0, 0, 0, i)),
        out_shape=jax.ShapeDtypeStruct((components, planes - 5, bands, width), padded.dtype),
    )(padded)


def mortar_kernel(flag_ref, section_ref, ghost_ref, out_ref):
    front = flag_ref[0] == 0
    cells = section_ref[...]
    ghost = ghost_ref[...]
    planes = cells.shape[1]
    upper = [cells[:, index] for index in range(1, planes)] + [ghost[:, index] for index in range(3)]
    lower = [ghost[:, index] for index in range(3)] + [cells[:, index] for index in range(planes - 1)]
    padded = jnp.stack([jnp.where(front, a, b) for a, b in zip(upper, lower)], axis=1)
    count = padded.shape[1] - 6
    pressure = pressure_of(padded)
    velocity = padded[1] / padded[0]
    parts = [padded[index_part] * velocity for index_part in range(5)]
    parts[1] = parts[1] + pressure
    parts[4] = parts[4] + pressure * velocity
    out_ref[...] = face_flux(padded, jnp.stack(parts), 1, count, 1, 2, 3)


def mortar_faces_of(section_state, ghost):
    components, planes, bands, width = section_state.shape
    lanes = 256
    flag = lax.axis_index("blk").astype(jnp.int32).reshape(1)
    return pl.pallas_call(
        mortar_kernel,
        grid=(width // lanes,),
        in_specs=[
            pl.BlockSpec(memory_space=pltpu.SMEM),
            pl.BlockSpec((components, planes, bands, lanes), lambda i: (0, 0, 0, i)),
            pl.BlockSpec((components, 3, bands, lanes), lambda i: (0, 0, 0, i)),
        ],
        out_specs=pl.BlockSpec((components, 3, bands, lanes), lambda i: (0, 0, 0, i)),
        out_shape=jax.ShapeDtypeStruct((components, 3, bands, width), section_state.dtype),
    )(flag, section_state, ghost)


def shards(base_state, section_state, rotor_step):
    planes = section_state.shape[1]
    bands = section_state.shape[2]
    width = section_state.shape[3]
    fraction = (rotor_step[0] % 4).astype(jnp.float32) / 4.0
    theta_padded = padded_2(section_state, ((("tx", "tz"), 3),), 3, True)
    radial_raw = padded_2(section_state, (("radial", 2),), 3, False)
    band_index = lax.axis_index("radial")
    band_count = lax.axis_size("radial")
    lower_wall = jnp.where(
        band_index == 0, flip_radial(section_state[:, :, :3]), radial_raw[:, :, :3]
    )
    upper_wall = jnp.where(
        band_index == band_count - 1, flip_radial(section_state[:, :, -3:]), radial_raw[:, :, -3:]
    )
    radial_padded = jnp.concatenate([lower_wall, section_state, upper_wall], axis=2)
    block_index = lax.axis_index("blk")
    front = block_index == 0
    outgoing = jnp.where(front, section_state[:, -3:], section_state[:, :3])[..., ::-1]
    radial = divergence(radial_padded, 2, bands, 3, 1, 2)
    chosen = pick_column(outgoing, rotor_step, radial)
    theta_padded = hold(theta_padded, chosen)
    azimuthal = divergence(theta_padded, 3, width, 2, 1, 3)
    chosen = pick_row(chosen, rotor_step, azimuthal)
    this_slab, next_slab = cross_blocks(chosen)
    edge_low = jnp.concatenate(
        [section_state[:, :1], section_state[:, :1], section_state[:, :1]], axis=1
    )
    edge_high = jnp.concatenate(
        [section_state[:, -1:], section_state[:, -1:], section_state[:, -1:]], axis=1
    )
    local_window = jnp.where(
        front,
        jnp.concatenate([edge_low, section_state], axis=1),
        jnp.concatenate([section_state, edge_high], axis=1),
    )
    local_window = hold(local_window, chosen)
    local_faces = axial_faces(local_window)
    settled = 0.75 * base_state + 0.25 * (section_state - step_ratio * (radial + azimuthal))
    window = window_of(this_slab, next_slab, rotor_step, local_faces + settled[:, :1, :, :1])
    ghost = flip_theta(
        (1.0 - fraction) * window[..., 1 : width + 1] + fraction * window[..., :width]
    )
    mortar_faces = mortar_faces_of(section_state, ghost)
    faces = jnp.where(
        front,
        jnp.concatenate([local_faces, mortar_faces], axis=1),
        jnp.concatenate([mortar_faces, local_faces], axis=1),
    )
    axial = lax.slice_in_dim(faces, 1, planes + 1, axis=1) - lax.slice_in_dim(
        faces, 0, planes, axis=1
    )
    return settled - 0.25 * step_ratio * axial


def solution(mesh):
    blocks, slabs, bands = (mesh.shape[name] for name in ("blk", "theta", "radial"))
    rows = 4 if slabs % 4 == 0 else 1
    grid = jax.sharding.Mesh(
        mesh.devices.reshape(blocks, rows, slabs // rows, bands), ("blk", "tx", "tz", "radial")
    )
    in_specs = (P(None, "blk", "radial", ("tx", "tz")), P(None, "blk", "radial", ("tx", "tz")), P())
    out_specs = P(None, "blk", "radial", ("tx", "tz"))
    inner = jax.shard_map(shards, mesh=grid, in_specs=in_specs, out_specs=out_specs, check_vma=False)
    sharded = jax.sharding.NamedSharding(mesh, P(None, "blk", "radial", "theta"))

    def run(base_state, section_state, rotor_step):
        return jax.lax.with_sharding_constraint(
            inner(base_state, section_state, rotor_step), sharded
        )

    return run
```

```python
import jax
import jax.numpy as jnp
from jax import lax
from jax.sharding import PartitionSpec as P
from jax.experimental import pallas as pl
from jax.experimental.pallas import tpu as pltpu

gamma_ratio = 1.4
weno_epsilon = 1e-06
step_ratio = 0.12


def padded_2(cells, sides, width, closed):
    for axis, dim in sides:
        count = lax.axis_size(axis)
        ends = count if closed else count - 1
        head = lax.slice_in_dim(cells, 0, width, axis=dim)
        tail = lax.slice_in_dim(cells, cells.shape[dim] - width, cells.shape[dim], axis=dim)
        cells = jnp.concatenate(
            [
                lax.ppermute(tail, axis, [(i, (i + 1) % count) for i in range(ends)]),
                cells,
                lax.ppermute(head, axis, [((i + 1) % count, i) for i in range(ends)]),
            ],
            axis=dim,
        )
    return cells


def partner(block, axis, distance):
    count = lax.axis_size(axis)
    route = []
    for low in range(count):
        high = low | 1 << distance
        if high != low and high < count:
            route += [(low, high), (high, low)]
    return lax.ppermute(block, axis, route)


def pressure_of(state):
    kinetic = 0.5 * (jnp.square(state[1]) + jnp.square(state[2]) + jnp.square(state[3])) / state[0]
    return (gamma_ratio - 1.0) * (state[4] - kinetic)


def euler_flux(state, normal):
    pressure = pressure_of(state)
    velocity = state[normal] / state[0]
    flux = state * velocity[None]
    flux = flux.at[normal].add(pressure)
    flux = flux.at[4].add(pressure * velocity)
    return flux


def wave_speed(state, normal):
    pressure = pressure_of(state)
    return jnp.abs(state[normal] / state[0]) + jnp.sqrt(gamma_ratio * pressure / state[0])


def weno_side(far_left, left_cell, centre, right_cell, far_right):
    smooth_low = 13.0 / 12.0 * jnp.square(far_left - 2.0 * left_cell + centre) + 0.25 * jnp.square(
        far_left - 4.0 * left_cell + 3.0 * centre
    )
    smooth_mid = 13.0 / 12.0 * jnp.square(
        left_cell - 2.0 * centre + right_cell
    ) + 0.25 * jnp.square(left_cell - right_cell)
    smooth_high = 13.0 / 12.0 * jnp.square(
        centre - 2.0 * right_cell + far_right
    ) + 0.25 * jnp.square(3.0 * centre - 4.0 * right_cell + far_right)
    weight_low = 0.1 / jnp.square(weno_epsilon + smooth_low)
    weight_mid = 0.6 / jnp.square(weno_epsilon + smooth_mid)
    weight_high = 0.3 / jnp.square(weno_epsilon + smooth_high)
    guess_low = (2.0 * far_left - 7.0 * left_cell + 11.0 * centre) / 6.0
    guess_mid = (-left_cell + 5.0 * centre + 2.0 * right_cell) / 6.0
    guess_high = (2.0 * centre + 5.0 * right_cell - far_right) / 6.0
    return (weight_low * guess_low + weight_mid * guess_mid + weight_high * guess_high) / (
        weight_low + weight_mid + weight_high
    )


def face_flux(padded, fluxes, axis, count, normal, first, second):
    states = [
        lax.slice_in_dim(padded, shift_index, shift_index + count + 1, axis=axis)
        for shift_index in range(6)
    ]
    physical = [
        lax.slice_in_dim(fluxes, shift_index, shift_index + count + 1, axis=axis)
        for shift_index in range(6)
    ]
    mean = 0.5 * (states[2] + states[3])
    density = mean[0]
    normal_speed = mean[normal] / density
    speed_first = mean[first] / density
    speed_second = mean[second] / density
    kinetic = 0.5 * (jnp.square(normal_speed) + jnp.square(speed_first) + jnp.square(speed_second))
    pressure = pressure_of(mean)
    sound = jnp.sqrt(gamma_ratio * pressure / density)
    enthalpy = (mean[4] + pressure) / density
    inv_sound = 1.0 / sound
    factor_one = (gamma_ratio - 1.0) * jnp.square(inv_sound)
    factor_two = factor_one * kinetic
    dissipation = jnp.maximum(wave_speed(states[2], normal), wave_speed(states[3], normal))

    def project(vector):
        dens_part = vector[0]
        norm_part = vector[normal]
        first_part = vector[first]
        second_part = vector[second]
        energy_part = vector[4]
        tangent_sum = factor_one * (
            speed_first * first_part + speed_second * second_part - energy_part
        )
        wave_minus = 0.5 * (
            (factor_two + normal_speed * inv_sound) * dens_part
            - (factor_one * normal_speed + inv_sound) * norm_part
            - tangent_sum
        )
        entropy = (
            (1.0 - factor_two) * dens_part + factor_one * normal_speed * norm_part + tangent_sum
        )
        shear_first = first_part - speed_first * dens_part
        shear_second = second_part - speed_second * dens_part
        wave_plus = 0.5 * (
            (factor_two - normal_speed * inv_sound) * dens_part
            - (factor_one * normal_speed - inv_sound) * norm_part
            - tangent_sum
        )
        return (wave_minus, entropy, shear_first, shear_second, wave_plus)

    state_chars = [project(cell_state) for cell_state in states]
    flux_chars = [project(cell_flux) for cell_flux in physical]
    recon = []
    for field_index in range(5):
        plus_vals = [
            0.5 * (flux_chars[cell][field_index] + dissipation * state_chars[cell][field_index])
            for cell in range(6)
        ]
        minus_vals = [
            0.5 * (flux_chars[cell][field_index] - dissipation * state_chars[cell][field_index])
            for cell in range(6)
        ]
        recon.append(
            weno_side(plus_vals[0], plus_vals[1], plus_vals[2], plus_vals[3], plus_vals[4])
            + weno_side(minus_vals[5], minus_vals[4], minus_vals[3], minus_vals[2], minus_vals[1])
        )
    wave_minus, entropy, shear_first, shear_second, wave_plus = recon
    acoustic = wave_minus + entropy + wave_plus
    parts = {}
    parts[0] = acoustic
    parts[normal] = (
        (normal_speed - sound) * wave_minus
        + normal_speed * entropy
        + (normal_speed + sound) * wave_plus
    )
    parts[first] = speed_first * acoustic + shear_first
    parts[second] = speed_second * acoustic + shear_second
    parts[4] = (
        (enthalpy - normal_speed * sound) * wave_minus
        + kinetic * entropy
        + speed_first * shear_first
        + speed_second * shear_second
        + (enthalpy + normal_speed * sound) * wave_plus
    )
    return jnp.stack([parts[index_part] for index_part in range(5)])


def divergence(padded, axis, count, normal, first, second):
    faces = face_flux(padded, euler_flux(padded, normal), axis, count, normal, first, second)
    return lax.slice_in_dim(faces, 1, count + 1, axis=axis) - lax.slice_in_dim(
        faces, 0, count, axis=axis
    )


def flip_radial(cells):
    turned = cells[:, :, ::-1]
    return jnp.concatenate([turned[:3], -turned[3:4], turned[4:]], axis=0)


def flip_theta(cells):
    return jnp.concatenate([cells[:2], -cells[2:3], cells[3:]], axis=0)


def hold(cells, value):
    return jnp.where(jnp.isnan(value.reshape(-1)[0]), jnp.zeros((), cells.dtype), cells)


def after(value, index):
    return index + jnp.isnan(value.reshape(-1)[0]).astype(jnp.int32)


def route_parts(rotor_step, width):
    rows = lax.axis_size("tx")
    columns = lax.axis_size("tz")
    turns = rotor_step[0] // 4 // width
    centre = (turns - 1) % (rows * columns)
    return rows, columns, centre // columns, centre % columns


def pick_column(slab, rotor_step, before):
    rows, columns, centre_row, centre_column = route_parts(rotor_step, slab.shape[3])
    source_column = (centre_column - lax.axis_index("tz")) % columns
    gathered = lax.all_gather(slab, "tz")
    return lax.dynamic_index_in_dim(gathered, after(before, source_column), 0, keepdims=False)


def pick_row(slab, rotor_step, before):
    rows, columns, centre_row, centre_column = route_parts(rotor_step, slab.shape[3])
    borrow = (lax.axis_index("tz") > centre_column).astype(jnp.int32)
    source_row = (centre_row - lax.axis_index("tx") - borrow) % rows
    gathered = lax.all_gather(slab, "tx")
    return lax.dynamic_index_in_dim(gathered, after(before, source_row), 0, keepdims=False)


def cross_blocks(slab):
    block_count = lax.axis_size("blk")
    slab_count = lax.axis_size("tx") * lax.axis_size("tz")
    this_route = []
    next_route = []
    for blk_from in range(block_count):
        blk_to = (blk_from + 1) % block_count
        for slab_from in range(slab_count):
            source = blk_from * slab_count + slab_from
            this_route.append((source, blk_to * slab_count + slab_from))
            next_route.append((source, blk_to * slab_count + (slab_from + 1) % slab_count))
    axes = ("blk", "tx", "tz")
    return lax.ppermute(slab, axes, this_route), lax.ppermute(slab, axes, next_route)


def window_of(this_slab, next_slab, rotor_step, before):
    width = this_slab.shape[3]
    remainder = after(before, rotor_step[0] // 4 % width)
    doubled = jnp.concatenate([next_slab, this_slab], axis=3)
    return lax.dynamic_slice_in_dim(doubled, width - 1 - remainder, width + 1, 3)


def axial_kernel(padded_ref, out_ref):
    padded = padded_ref[...]
    count = padded.shape[1] - 6
    pressure = pressure_of(padded)
    velocity = padded[1] / padded[0]
    parts = [padded[index_part] * velocity for index_part in range(5)]
    parts[1] = parts[1] + pressure
    parts[4] = parts[4] + pressure * velocity
    faces = face_flux(padded, jnp.stack(parts), 1, count, 1, 2, 3)
    out_ref[...] = faces


def axial_faces(padded):
    components, planes, bands, width = padded.shape
    lanes = 256
    block = (components, planes, bands, lanes)
    out_block = (components, planes - 5, bands, lanes)
    return pl.pallas_call(
        axial_kernel,
        grid=(width // lanes,),
        in_specs=[pl.BlockSpec(block, lambda i: (0, 0, 0, i))],
        out_specs=pl.BlockSpec(out_block, lambda i: (0, 0, 0, i)),
        out_shape=jax.ShapeDtypeStruct((components, planes - 5, bands, width), padded.dtype),
    )(padded)


def mortar_kernel(flag_ref, section_ref, ghost_ref, edge_ref, partial_ref, out_ref):
    front = flag_ref[0] == 0
    cells = section_ref[...]
    ghost = ghost_ref[...]
    planes = cells.shape[1]
    upper = [cells[:, index] for index in range(1, planes)] + [ghost[:, index] for index in range(3)]
    lower = [ghost[:, index] for index in range(3)] + [cells[:, index] for index in range(planes - 1)]
    padded = jnp.stack([jnp.where(front, a, b) for a, b in zip(upper, lower)], axis=1)
    count = padded.shape[1] - 6
    pressure = pressure_of(padded)
    velocity = padded[1] / padded[0]
    parts = [padded[index_part] * velocity for index_part in range(5)]
    parts[1] = parts[1] + pressure
    parts[4] = parts[4] + pressure * velocity
    faces = face_flux(padded, jnp.stack(parts), 1, count, 1, 2, 3)
    edge = edge_ref[...][:, 0]
    after_front = [faces[:, 0] - edge, faces[:, 1] - faces[:, 0], faces[:, 2] - faces[:, 1]]
    after_aft = [faces[:, 1] - faces[:, 0], faces[:, 2] - faces[:, 1], edge - faces[:, 2]]
    axial = jnp.stack([jnp.where(front, a, b) for a, b in zip(after_front, after_aft)], axis=1)
    out_ref[...] = partial_ref[...] - 0.25 * step_ratio * axial


def mortar_planes_of(section_state, ghost, edge, partial):
    components, planes, bands, width = section_state.shape
    lanes = 256
    flag = lax.axis_index("blk").astype(jnp.int32).reshape(1)
    late = lambda i, flag_ref: (0, 1 - flag_ref[0], 0, i)
    return pl.pallas_call(
        mortar_kernel,
        grid_spec=pltpu.PrefetchScalarGridSpec(
            num_scalar_prefetch=1,
            grid=(width // lanes,),
            in_specs=[
                pl.BlockSpec((components, planes, bands, lanes), lambda i, flag_ref: (0, 0, 0, i)),
                pl.BlockSpec((components, 3, bands, lanes), lambda i, flag_ref: (0, 0, 0, i)),
                pl.BlockSpec((components, 1, bands, lanes), lambda i, flag_ref: (0, 0, 0, i)),
                pl.BlockSpec((components, 3, bands, lanes), late),
            ],
            out_specs=pl.BlockSpec((components, 3, bands, lanes), late),
        ),
        out_shape=jax.ShapeDtypeStruct(partial.shape, partial.dtype),
        input_output_aliases={4: 0},
    )(flag, section_state, ghost, edge, partial)


def shards(base_state, section_state, rotor_step):
    planes = section_state.shape[1]
    bands = section_state.shape[2]
    width = section_state.shape[3]
    fraction = (rotor_step[0] % 4).astype(jnp.float32) / 4.0
    theta_padded = padded_2(section_state, ((("tx", "tz"), 3),), 3, True)
    radial_raw = padded_2(section_state, (("radial", 2),), 3, False)
    band_index = lax.axis_index("radial")
    band_count = lax.axis_size("radial")
    lower_wall = jnp.where(
        band_index == 0, flip_radial(section_state[:, :, :3]), radial_raw[:, :, :3]
    )
    upper_wall = jnp.where(
        band_index == band_count - 1, flip_radial(section_state[:, :, -3:]), radial_raw[:, :, -3:]
    )
    radial_padded = jnp.concatenate([lower_wall, section_state, upper_wall], axis=2)
    block_index = lax.axis_index("blk")
    front = block_index == 0
    outgoing = jnp.where(front, section_state[:, -3:], section_state[:, :3])[..., ::-1]
    radial = divergence(radial_padded, 2, bands, 3, 1, 2)
    chosen = pick_column(outgoing, rotor_step, radial)
    theta_padded = hold(theta_padded, chosen)
    azimuthal = divergence(theta_padded, 3, width, 2, 1, 3)
    chosen = pick_row(chosen, rotor_step, azimuthal)
    this_slab, next_slab = cross_blocks(chosen)
    edge_low = jnp.concatenate(
        [section_state[:, :1], section_state[:, :1], section_state[:, :1]], axis=1
    )
    edge_high = jnp.concatenate(
        [section_state[:, -1:], section_state[:, -1:], section_state[:, -1:]], axis=1
    )
    local_window = jnp.where(
        front,
        jnp.concatenate([edge_low, section_state], axis=1),
        jnp.concatenate([section_state, edge_high], axis=1),
    )
    local_window = hold(local_window, chosen)
    local_faces = axial_faces(local_window)
    settled = 0.75 * base_state + 0.25 * (section_state - step_ratio * (radial + azimuthal))
    half = planes // 2
    early = jnp.where(front, settled[:, :half], settled[:, half:]) - 0.25 * step_ratio * (
        local_faces[:, 1:] - local_faces[:, :-1]
    )
    partial = jnp.where(
        front,
        jnp.concatenate([early, settled[:, half:]], axis=1),
        jnp.concatenate([settled[:, :half], early], axis=1),
    )
    edge = jnp.where(front, local_faces[:, -1:], local_faces[:, :1])
    window = window_of(this_slab, next_slab, rotor_step, partial[:, :1, :, :1] + edge[:, :, :1, :1])
    ghost = flip_theta(
        (1.0 - fraction) * window[..., 1 : width + 1] + fraction * window[..., :width]
    )
    return mortar_planes_of(section_state, ghost, edge, partial)


def solution(mesh):
    blocks, slabs, bands = (mesh.shape[name] for name in ("blk", "theta", "radial"))
    rows = 4 if slabs % 4 == 0 else 1
    grid = jax.sharding.Mesh(
        mesh.devices.reshape(blocks, rows, slabs // rows, bands), ("blk", "tx", "tz", "radial")
    )
    in_specs = (P(None, "blk", "radial", ("tx", "tz")), P(None, "blk", "radial", ("tx", "tz")), P())
    out_specs = P(None, "blk", "radial", ("tx", "tz"))
    inner = jax.shard_map(shards, mesh=grid, in_specs=in_specs, out_specs=out_specs, check_vma=False)
    sharded = jax.sharding.NamedSharding(mesh, P(None, "blk", "radial", "theta"))

    def run(base_state, section_state, rotor_step):
        return jax.lax.with_sharding_constraint(
            inner(base_state, section_state, rotor_step), sharded
        )

    return run
```

```python
import jax
import jax.numpy as jnp
from jax import lax
from jax.sharding import PartitionSpec as P
from jax.experimental import pallas as pl
from jax.experimental.pallas import tpu as pltpu

gamma_ratio = 1.4
weno_epsilon = 1e-06
step_ratio = 0.12


def padded_2(cells, sides, width, closed):
    for axis, dim in sides:
        count = lax.axis_size(axis)
        ends = count if closed else count - 1
        head = lax.slice_in_dim(cells, 0, width, axis=dim)
        tail = lax.slice_in_dim(cells, cells.shape[dim] - width, cells.shape[dim], axis=dim)
        cells = jnp.concatenate(
            [
                lax.ppermute(tail, axis, [(i, (i + 1) % count) for i in range(ends)]),
                cells,
                lax.ppermute(head, axis, [((i + 1) % count, i) for i in range(ends)]),
            ],
            axis=dim,
        )
    return cells


def partner(block, axis, distance):
    count = lax.axis_size(axis)
    route = []
    for low in range(count):
        high = low | 1 << distance
        if high != low and high < count:
            route += [(low, high), (high, low)]
    return lax.ppermute(block, axis, route)


def pressure_of(state):
    kinetic = 0.5 * (jnp.square(state[1]) + jnp.square(state[2]) + jnp.square(state[3])) / state[0]
    return (gamma_ratio - 1.0) * (state[4] - kinetic)


def euler_flux(state, normal):
    pressure = pressure_of(state)
    velocity = state[normal] / state[0]
    flux = state * velocity[None]
    flux = flux.at[normal].add(pressure)
    flux = flux.at[4].add(pressure * velocity)
    return flux


def wave_speed(state, normal):
    pressure = pressure_of(state)
    return jnp.abs(state[normal] / state[0]) + jnp.sqrt(gamma_ratio * pressure / state[0])


def weno_side(far_left, left_cell, centre, right_cell, far_right):
    smooth_low = 13.0 / 12.0 * jnp.square(far_left - 2.0 * left_cell + centre) + 0.25 * jnp.square(
        far_left - 4.0 * left_cell + 3.0 * centre
    )
    smooth_mid = 13.0 / 12.0 * jnp.square(
        left_cell - 2.0 * centre + right_cell
    ) + 0.25 * jnp.square(left_cell - right_cell)
    smooth_high = 13.0 / 12.0 * jnp.square(
        centre - 2.0 * right_cell + far_right
    ) + 0.25 * jnp.square(3.0 * centre - 4.0 * right_cell + far_right)
    weight_low = 0.1 / jnp.square(weno_epsilon + smooth_low)
    weight_mid = 0.6 / jnp.square(weno_epsilon + smooth_mid)
    weight_high = 0.3 / jnp.square(weno_epsilon + smooth_high)
    guess_low = (2.0 * far_left - 7.0 * left_cell + 11.0 * centre) / 6.0
    guess_mid = (-left_cell + 5.0 * centre + 2.0 * right_cell) / 6.0
    guess_high = (2.0 * centre + 5.0 * right_cell - far_right) / 6.0
    return (weight_low * guess_low + weight_mid * guess_mid + weight_high * guess_high) / (
        weight_low + weight_mid + weight_high
    )


def face_flux(padded, fluxes, axis, count, normal, first, second):
    states = [
        lax.slice_in_dim(padded, shift_index, shift_index + count + 1, axis=axis)
        for shift_index in range(6)
    ]
    physical = [
        lax.slice_in_dim(fluxes, shift_index, shift_index + count + 1, axis=axis)
        for shift_index in range(6)
    ]
    mean = 0.5 * (states[2] + states[3])
    density = mean[0]
    normal_speed = mean[normal] / density
    speed_first = mean[first] / density
    speed_second = mean[second] / density
    kinetic = 0.5 * (jnp.square(normal_speed) + jnp.square(speed_first) + jnp.square(speed_second))
    pressure = pressure_of(mean)
    sound = jnp.sqrt(gamma_ratio * pressure / density)
    enthalpy = (mean[4] + pressure) / density
    inv_sound = 1.0 / sound
    factor_one = (gamma_ratio - 1.0) * jnp.square(inv_sound)
    factor_two = factor_one * kinetic
    dissipation = jnp.maximum(wave_speed(states[2], normal), wave_speed(states[3], normal))

    def project(vector):
        dens_part = vector[0]
        norm_part = vector[normal]
        first_part = vector[first]
        second_part = vector[second]
        energy_part = vector[4]
        tangent_sum = factor_one * (
            speed_first * first_part + speed_second * second_part - energy_part
        )
        wave_minus = 0.5 * (
            (factor_two + normal_speed * inv_sound) * dens_part
            - (factor_one * normal_speed + inv_sound) * norm_part
            - tangent_sum
        )
        entropy = (
            (1.0 - factor_two) * dens_part + factor_one * normal_speed * norm_part + tangent_sum
        )
        shear_first = first_part - speed_first * dens_part
        shear_second = second_part - speed_second * dens_part
        wave_plus = 0.5 * (
            (factor_two - normal_speed * inv_sound) * dens_part
            - (factor_one * normal_speed - inv_sound) * norm_part
            - tangent_sum
        )
        return (wave_minus, entropy, shear_first, shear_second, wave_plus)

    state_chars = [project(cell_state) for cell_state in states]
    flux_chars = [project(cell_flux) for cell_flux in physical]
    recon = []
    for field_index in range(5):
        plus_vals = [
            0.5 * (flux_chars[cell][field_index] + dissipation * state_chars[cell][field_index])
            for cell in range(6)
        ]
        minus_vals = [
            0.5 * (flux_chars[cell][field_index] - dissipation * state_chars[cell][field_index])
            for cell in range(6)
        ]
        recon.append(
            weno_side(plus_vals[0], plus_vals[1], plus_vals[2], plus_vals[3], plus_vals[4])
            + weno_side(minus_vals[5], minus_vals[4], minus_vals[3], minus_vals[2], minus_vals[1])
        )
    wave_minus, entropy, shear_first, shear_second, wave_plus = recon
    acoustic = wave_minus + entropy + wave_plus
    parts = {}
    parts[0] = acoustic
    parts[normal] = (
        (normal_speed - sound) * wave_minus
        + normal_speed * entropy
        + (normal_speed + sound) * wave_plus
    )
    parts[first] = speed_first * acoustic + shear_first
    parts[second] = speed_second * acoustic + shear_second
    parts[4] = (
        (enthalpy - normal_speed * sound) * wave_minus
        + kinetic * entropy
        + speed_first * shear_first
        + speed_second * shear_second
        + (enthalpy + normal_speed * sound) * wave_plus
    )
    return jnp.stack([parts[index_part] for index_part in range(5)])


def divergence(padded, axis, count, normal, first, second):
    faces = face_flux(padded, euler_flux(padded, normal), axis, count, normal, first, second)
    return lax.slice_in_dim(faces, 1, count + 1, axis=axis) - lax.slice_in_dim(
        faces, 0, count, axis=axis
    )


def flip_radial(cells):
    turned = cells[:, :, ::-1]
    return jnp.concatenate([turned[:3], -turned[3:4], turned[4:]], axis=0)


def flip_theta(cells):
    return jnp.concatenate([cells[:2], -cells[2:3], cells[3:]], axis=0)


def hold(cells, value):
    return jnp.where(jnp.isnan(value.reshape(-1)[0]), jnp.zeros((), cells.dtype), cells)


def after(value, index):
    return index + jnp.isnan(value.reshape(-1)[0]).astype(jnp.int32)


def route_parts(rotor_step, width):
    rows = lax.axis_size("tx")
    columns = lax.axis_size("tz")
    turns = rotor_step[0] // 4 // width
    centre = (turns - 1) % (rows * columns)
    return rows, columns, centre // columns, centre % columns


def pick_column(slab, rotor_step, before):
    rows, columns, centre_row, centre_column = route_parts(rotor_step, slab.shape[3])
    source_column = (centre_column - lax.axis_index("tz")) % columns
    gathered = lax.all_gather(slab, "tz")
    return lax.dynamic_index_in_dim(gathered, after(before, source_column), 0, keepdims=False)[
        ..., ::-1
    ]


def pick_row(slab, rotor_step, before):
    rows, columns, centre_row, centre_column = route_parts(rotor_step, slab.shape[3])
    borrow = (lax.axis_index("tz") > centre_column).astype(jnp.int32)
    source_row = (centre_row - lax.axis_index("tx") - borrow) % rows
    gathered = lax.all_gather(slab, "tx")
    return lax.dynamic_index_in_dim(gathered, after(before, source_row), 0, keepdims=False)


def cross_blocks(slab):
    block_count = lax.axis_size("blk")
    slab_count = lax.axis_size("tx") * lax.axis_size("tz")
    this_route = []
    next_route = []
    for blk_from in range(block_count):
        blk_to = (blk_from + 1) % block_count
        for slab_from in range(slab_count):
            source = blk_from * slab_count + slab_from
            this_route.append((source, blk_to * slab_count + slab_from))
            next_route.append((source, blk_to * slab_count + (slab_from + 1) % slab_count))
    axes = ("blk", "tx", "tz")
    return lax.ppermute(slab, axes, this_route), lax.ppermute(slab, axes, next_route)


def window_of(this_slab, next_slab, rotor_step, before):
    width = this_slab.shape[3]
    remainder = after(before, rotor_step[0] // 4 % width)
    doubled = jnp.concatenate([next_slab, this_slab], axis=3)
    return lax.dynamic_slice_in_dim(doubled, width - 1 - remainder, width + 1, 3)


def axial_kernel(padded_ref, out_ref):
    padded = padded_ref[...]
    count = padded.shape[1] - 6
    pressure = pressure_of(padded)
    velocity = padded[1] / padded[0]
    parts = [padded[index_part] * velocity for index_part in range(5)]
    parts[1] = parts[1] + pressure
    parts[4] = parts[4] + pressure * velocity
    faces = face_flux(padded, jnp.stack(parts), 1, count, 1, 2, 3)
    out_ref[...] = faces


def axial_faces(padded):
    components, planes, bands, width = padded.shape
    lanes = 256
    block = (components, planes, bands, lanes)
    out_block = (components, planes - 5, bands, lanes)
    return pl.pallas_call(
        axial_kernel,
        grid=(width // lanes,),
        in_specs=[pl.BlockSpec(block, lambda i: (0, 0, 0, i))],
        out_specs=pl.BlockSpec(out_block, lambda i: (0, 0, 0, i)),
        out_shape=jax.ShapeDtypeStruct((components, planes - 5, bands, width), padded.dtype),
    )(padded)


def mortar_kernel(flag_ref, section_ref, ghost_ref, edge_ref, partial_ref, out_ref):
    front = flag_ref[0] == 0
    cells = section_ref[...]
    ghost = ghost_ref[...]
    planes = cells.shape[1]
    upper = [cells[:, index] for index in range(1, planes)] + [ghost[:, index] for index in range(3)]
    lower = [ghost[:, index] for index in range(3)] + [cells[:, index] for index in range(planes - 1)]
    padded = jnp.stack([jnp.where(front, a, b) for a, b in zip(upper, lower)], axis=1)
    count = padded.shape[1] - 6
    pressure = pressure_of(padded)
    velocity = padded[1] / padded[0]
    parts = [padded[index_part] * velocity for index_part in range(5)]
    parts[1] = parts[1] + pressure
    parts[4] = parts[4] + pressure * velocity
    faces = face_flux(padded, jnp.stack(parts), 1, count, 1, 2, 3)
    edge = edge_ref[...][:, 0]
    after_front = [faces[:, 0] - edge, faces[:, 1] - faces[:, 0], faces[:, 2] - faces[:, 1]]
    after_aft = [faces[:, 1] - faces[:, 0], faces[:, 2] - faces[:, 1], edge - faces[:, 2]]
    axial = jnp.stack([jnp.where(front, a, b) for a, b in zip(after_front, after_aft)], axis=1)
    out_ref[...] = partial_ref[...] - 0.25 * step_ratio * axial


def mortar_planes_of(section_state, ghost, edge, partial):
    components, planes, bands, width = section_state.shape
    lanes = 256
    flag = lax.axis_index("blk").astype(jnp.int32).reshape(1)
    late = lambda i, flag_ref: (0, 1 - flag_ref[0], 0, i)
    return pl.pallas_call(
        mortar_kernel,
        grid_spec=pltpu.PrefetchScalarGridSpec(
            num_scalar_prefetch=1,
            grid=(width // lanes,),
            in_specs=[
                pl.BlockSpec((components, planes, bands, lanes), lambda i, flag_ref: (0, 0, 0, i)),
                pl.BlockSpec((components, 3, bands, lanes), lambda i, flag_ref: (0, 0, 0, i)),
                pl.BlockSpec((components, 1, bands, lanes), lambda i, flag_ref: (0, 0, 0, i)),
                pl.BlockSpec((components, 3, bands, lanes), late),
            ],
            out_specs=pl.BlockSpec((components, 3, bands, lanes), late),
        ),
        out_shape=jax.ShapeDtypeStruct(partial.shape, partial.dtype),
        input_output_aliases={4: 0},
    )(flag, section_state, ghost, edge, partial)


def shards(base_state, section_state, rotor_step):
    planes = section_state.shape[1]
    bands = section_state.shape[2]
    width = section_state.shape[3]
    fraction = (rotor_step[0] % 4).astype(jnp.float32) / 4.0
    theta_padded = padded_2(section_state, ((("tx", "tz"), 3),), 3, True)
    radial_raw = padded_2(section_state, (("radial", 2),), 3, False)
    band_index = lax.axis_index("radial")
    band_count = lax.axis_size("radial")
    lower_wall = jnp.where(
        band_index == 0, flip_radial(section_state[:, :, :3]), radial_raw[:, :, :3]
    )
    upper_wall = jnp.where(
        band_index == band_count - 1, flip_radial(section_state[:, :, -3:]), radial_raw[:, :, -3:]
    )
    radial_padded = jnp.concatenate([lower_wall, section_state, upper_wall], axis=2)
    block_index = lax.axis_index("blk")
    front = block_index == 0
    outgoing = jnp.where(front, section_state[:, -3:], section_state[:, :3])
    radial = divergence(radial_padded, 2, bands, 3, 1, 2)
    chosen = pick_column(outgoing, rotor_step, radial)
    theta_padded = hold(theta_padded, chosen)
    azimuthal = divergence(theta_padded, 3, width, 2, 1, 3)
    chosen = pick_row(chosen, rotor_step, azimuthal)
    this_slab, next_slab = cross_blocks(chosen)
    edge_low = jnp.concatenate(
        [section_state[:, :1], section_state[:, :1], section_state[:, :1]], axis=1
    )
    edge_high = jnp.concatenate(
        [section_state[:, -1:], section_state[:, -1:], section_state[:, -1:]], axis=1
    )
    local_window = jnp.where(
        front,
        jnp.concatenate([edge_low, section_state], axis=1),
        jnp.concatenate([section_state, edge_high], axis=1),
    )
    local_window = hold(local_window, chosen)
    local_faces = axial_faces(local_window)
    settled = 0.75 * base_state + 0.25 * (section_state - step_ratio * (radial + azimuthal))
    half = planes // 2
    early = jnp.where(front, settled[:, :half], settled[:, half:]) - 0.25 * step_ratio * (
        local_faces[:, 1:] - local_faces[:, :-1]
    )
    partial = jnp.where(
        front,
        jnp.concatenate([early, settled[:, half:]], axis=1),
        jnp.concatenate([settled[:, :half], early], axis=1),
    )
    edge = jnp.where(front, local_faces[:, -1:], local_faces[:, :1])
    window = window_of(this_slab, next_slab, rotor_step, partial[:, :1, :, :1] + edge[:, :, :1, :1])
    ghost = flip_theta(
        (1.0 - fraction) * window[..., 1 : width + 1] + fraction * window[..., :width]
    )
    return mortar_planes_of(section_state, ghost, edge, partial)


def solution(mesh):
    blocks, slabs, bands = (mesh.shape[name] for name in ("blk", "theta", "radial"))
    rows = 4 if slabs % 4 == 0 else 1
    grid = jax.sharding.Mesh(
        mesh.devices.reshape(blocks, rows, slabs // rows, bands), ("blk", "tx", "tz", "radial")
    )
    in_specs = (P(None, "blk", "radial", ("tx", "tz")), P(None, "blk", "radial", ("tx", "tz")), P())
    out_specs = P(None, "blk", "radial", ("tx", "tz"))
    inner = jax.shard_map(shards, mesh=grid, in_specs=in_specs, out_specs=out_specs, check_vma=False)
    sharded = jax.sharding.NamedSharding(mesh, P(None, "blk", "radial", "theta"))

    def run(base_state, section_state, rotor_step):
        return jax.lax.with_sharding_constraint(
            inner(base_state, section_state, rotor_step), sharded
        )

    return run
```

```python
import jax
import jax.numpy as jnp
from jax import lax
from jax.sharding import PartitionSpec as P
from jax.experimental import pallas as pl
from jax.experimental.pallas import tpu as pltpu

gamma_ratio = 1.4
weno_epsilon = 1e-06
step_ratio = 0.12


def padded_2(cells, sides, width, closed):
    for axis, dim in sides:
        count = lax.axis_size(axis)
        ends = count if closed else count - 1
        head = lax.slice_in_dim(cells, 0, width, axis=dim)
        tail = lax.slice_in_dim(cells, cells.shape[dim] - width, cells.shape[dim], axis=dim)
        cells = jnp.concatenate(
            [
                lax.ppermute(tail, axis, [(i, (i + 1) % count) for i in range(ends)]),
                cells,
                lax.ppermute(head, axis, [((i + 1) % count, i) for i in range(ends)]),
            ],
            axis=dim,
        )
    return cells


def partner(block, axis, distance):
    count = lax.axis_size(axis)
    route = []
    for low in range(count):
        high = low | 1 << distance
        if high != low and high < count:
            route += [(low, high), (high, low)]
    return lax.ppermute(block, axis, route)


def pressure_of(state):
    kinetic = 0.5 * (jnp.square(state[1]) + jnp.square(state[2]) + jnp.square(state[3])) / state[0]
    return (gamma_ratio - 1.0) * (state[4] - kinetic)


def euler_flux(state, normal):
    pressure = pressure_of(state)
    velocity = state[normal] / state[0]
    flux = state * velocity[None]
    flux = flux.at[normal].add(pressure)
    flux = flux.at[4].add(pressure * velocity)
    return flux


def wave_speed(state, normal):
    pressure = pressure_of(state)
    return jnp.abs(state[normal] / state[0]) + jnp.sqrt(gamma_ratio * pressure / state[0])


def weno_side(far_left, left_cell, centre, right_cell, far_right):
    smooth_low = 13.0 / 12.0 * jnp.square(far_left - 2.0 * left_cell + centre) + 0.25 * jnp.square(
        far_left - 4.0 * left_cell + 3.0 * centre
    )
    smooth_mid = 13.0 / 12.0 * jnp.square(
        left_cell - 2.0 * centre + right_cell
    ) + 0.25 * jnp.square(left_cell - right_cell)
    smooth_high = 13.0 / 12.0 * jnp.square(
        centre - 2.0 * right_cell + far_right
    ) + 0.25 * jnp.square(3.0 * centre - 4.0 * right_cell + far_right)
    weight_low = 0.1 / jnp.square(weno_epsilon + smooth_low)
    weight_mid = 0.6 / jnp.square(weno_epsilon + smooth_mid)
    weight_high = 0.3 / jnp.square(weno_epsilon + smooth_high)
    guess_low = (2.0 * far_left - 7.0 * left_cell + 11.0 * centre) / 6.0
    guess_mid = (-left_cell + 5.0 * centre + 2.0 * right_cell) / 6.0
    guess_high = (2.0 * centre + 5.0 * right_cell - far_right) / 6.0
    return (weight_low * guess_low + weight_mid * guess_mid + weight_high * guess_high) / (
        weight_low + weight_mid + weight_high
    )


def face_flux(padded, fluxes, axis, count, normal, first, second):
    states = [
        lax.slice_in_dim(padded, shift_index, shift_index + count + 1, axis=axis)
        for shift_index in range(6)
    ]
    physical = [
        lax.slice_in_dim(fluxes, shift_index, shift_index + count + 1, axis=axis)
        for shift_index in range(6)
    ]
    mean = 0.5 * (states[2] + states[3])
    density = mean[0]
    normal_speed = mean[normal] / density
    speed_first = mean[first] / density
    speed_second = mean[second] / density
    kinetic = 0.5 * (jnp.square(normal_speed) + jnp.square(speed_first) + jnp.square(speed_second))
    pressure = pressure_of(mean)
    sound = jnp.sqrt(gamma_ratio * pressure / density)
    enthalpy = (mean[4] + pressure) / density
    inv_sound = 1.0 / sound
    factor_one = (gamma_ratio - 1.0) * jnp.square(inv_sound)
    factor_two = factor_one * kinetic
    dissipation = jnp.maximum(wave_speed(states[2], normal), wave_speed(states[3], normal))

    def project(vector):
        dens_part = vector[0]
        norm_part = vector[normal]
        first_part = vector[first]
        second_part = vector[second]
        energy_part = vector[4]
        tangent_sum = factor_one * (
            speed_first * first_part + speed_second * second_part - energy_part
        )
        wave_minus = 0.5 * (
            (factor_two + normal_speed * inv_sound) * dens_part
            - (factor_one * normal_speed + inv_sound) * norm_part
            - tangent_sum
        )
        entropy = (
            (1.0 - factor_two) * dens_part + factor_one * normal_speed * norm_part + tangent_sum
        )
        shear_first = first_part - speed_first * dens_part
        shear_second = second_part - speed_second * dens_part
        wave_plus = 0.5 * (
            (factor_two - normal_speed * inv_sound) * dens_part
            - (factor_one * normal_speed - inv_sound) * norm_part
            - tangent_sum
        )
        return (wave_minus, entropy, shear_first, shear_second, wave_plus)

    state_chars = [project(cell_state) for cell_state in states]
    flux_chars = [project(cell_flux) for cell_flux in physical]
    recon = []
    for field_index in range(5):
        plus_vals = [
            0.5 * (flux_chars[cell][field_index] + dissipation * state_chars[cell][field_index])
            for cell in range(6)
        ]
        minus_vals = [
            0.5 * (flux_chars[cell][field_index] - dissipation * state_chars[cell][field_index])
            for cell in range(6)
        ]
        recon.append(
            weno_side(plus_vals[0], plus_vals[1], plus_vals[2], plus_vals[3], plus_vals[4])
            + weno_side(minus_vals[5], minus_vals[4], minus_vals[3], minus_vals[2], minus_vals[1])
        )
    wave_minus, entropy, shear_first, shear_second, wave_plus = recon
    acoustic = wave_minus + entropy + wave_plus
    parts = {}
    parts[0] = acoustic
    parts[normal] = (
        (normal_speed - sound) * wave_minus
        + normal_speed * entropy
        + (normal_speed + sound) * wave_plus
    )
    parts[first] = speed_first * acoustic + shear_first
    parts[second] = speed_second * acoustic + shear_second
    parts[4] = (
        (enthalpy - normal_speed * sound) * wave_minus
        + kinetic * entropy
        + speed_first * shear_first
        + speed_second * shear_second
        + (enthalpy + normal_speed * sound) * wave_plus
    )
    return jnp.stack([parts[index_part] for index_part in range(5)])


def divergence(padded, axis, count, normal, first, second):
    faces = face_flux(padded, euler_flux(padded, normal), axis, count, normal, first, second)
    return lax.slice_in_dim(faces, 1, count + 1, axis=axis) - lax.slice_in_dim(
        faces, 0, count, axis=axis
    )


def flip_radial(cells):
    turned = cells[:, :, ::-1]
    return jnp.concatenate([turned[:3], -turned[3:4], turned[4:]], axis=0)


def flip_theta(cells):
    return jnp.concatenate([cells[:2], -cells[2:3], cells[3:]], axis=0)


def hold(cells, value):
    return jnp.where(jnp.isnan(value.reshape(-1)[0]), jnp.zeros((), cells.dtype), cells)


def after(value, index):
    return index + jnp.isnan(value.reshape(-1)[0]).astype(jnp.int32)


def route_parts(rotor_step, width):
    rows = lax.axis_size("tx")
    columns = lax.axis_size("tz")
    turns = rotor_step[0] // 4 // width
    centre = (turns - 1) % (rows * columns)
    return rows, columns, centre // columns, centre % columns


def pick_column(slab, rotor_step, before):
    rows, columns, centre_row, centre_column = route_parts(rotor_step, slab.shape[3])
    source_column = (centre_column - lax.axis_index("tz")) % columns
    gathered = lax.all_gather(slab, "tz")
    return lax.dynamic_index_in_dim(gathered, after(before, source_column), 0, keepdims=False)[
        ..., ::-1
    ]


def pick_row(slab, rotor_step, before):
    rows, columns, centre_row, centre_column = route_parts(rotor_step, slab.shape[3])
    borrow = (lax.axis_index("tz") > centre_column).astype(jnp.int32)
    source_row = (centre_row - lax.axis_index("tx") - borrow) % rows
    gathered = lax.all_gather(slab, "tx")
    return lax.dynamic_index_in_dim(gathered, after(before, source_row), 0, keepdims=False)


def cross_blocks(slab):
    block_count = lax.axis_size("blk")
    slab_count = lax.axis_size("tx") * lax.axis_size("tz")
    this_route = []
    next_route = []
    for blk_from in range(block_count):
        blk_to = (blk_from + 1) % block_count
        for slab_from in range(slab_count):
            source = blk_from * slab_count + slab_from
            this_route.append((source, blk_to * slab_count + slab_from))
            next_route.append((source, blk_to * slab_count + (slab_from + 1) % slab_count))
    axes = ("blk", "tx", "tz")
    return lax.ppermute(slab, axes, this_route), lax.ppermute(slab, axes, next_route)


def window_of(this_slab, next_slab, rotor_step, before):
    width = this_slab.shape[3]
    remainder = after(before, rotor_step[0] // 4 % width)
    doubled = jnp.concatenate([next_slab, this_slab], axis=3)
    return lax.dynamic_slice_in_dim(doubled, width - 1 - remainder, width + 1, 3)


def axial_kernel(padded_ref, out_ref):
    padded = padded_ref[...]
    count = padded.shape[1] - 6
    pressure = pressure_of(padded)
    velocity = padded[1] / padded[0]
    parts = [padded[index_part] * velocity for index_part in range(5)]
    parts[1] = parts[1] + pressure
    parts[4] = parts[4] + pressure * velocity
    faces = face_flux(padded, jnp.stack(parts), 1, count, 1, 2, 3)
    out_ref[...] = faces


def axial_faces(padded):
    components, planes, bands, width = padded.shape
    lanes = 256
    block = (components, planes, bands, lanes)
    out_block = (components, planes - 5, bands, lanes)
    return pl.pallas_call(
        axial_kernel,
        grid=(width // lanes,),
        in_specs=[pl.BlockSpec(block, lambda i: (0, 0, 0, i))],
        out_specs=pl.BlockSpec(out_block, lambda i: (0, 0, 0, i)),
        out_shape=jax.ShapeDtypeStruct((components, planes - 5, bands, width), padded.dtype),
    )(padded)


def mortar_kernel(flag_ref, section_ref, ghost_ref, edge_ref, partial_ref, out_ref):
    front = flag_ref[0] == 0
    cells = section_ref[...]
    ghost = ghost_ref[...]
    planes = cells.shape[1]
    upper = [cells[:, index] for index in range(1, planes)] + [ghost[:, index] for index in range(3)]
    lower = [ghost[:, index] for index in range(3)] + [cells[:, index] for index in range(planes - 1)]
    padded = jnp.stack([jnp.where(front, a, b) for a, b in zip(upper, lower)], axis=1)
    count = padded.shape[1] - 6
    pressure = pressure_of(padded)
    velocity = padded[1] / padded[0]
    parts = [padded[index_part] * velocity for index_part in range(5)]
    parts[1] = parts[1] + pressure
    parts[4] = parts[4] + pressure * velocity
    faces = face_flux(padded, jnp.stack(parts), 1, count, 1, 2, 3)
    edge = edge_ref[...][:, 0]
    after_front = [faces[:, 0] - edge, faces[:, 1] - faces[:, 0], faces[:, 2] - faces[:, 1]]
    after_aft = [faces[:, 1] - faces[:, 0], faces[:, 2] - faces[:, 1], edge - faces[:, 2]]
    axial = jnp.stack([jnp.where(front, a, b) for a, b in zip(after_front, after_aft)], axis=1)
    out_ref[...] = partial_ref[...] - 0.25 * step_ratio * axial


def mortar_planes_of(section_state, ghost, edge, partial):
    components, planes, bands, width = section_state.shape
    lanes = 256
    flag = lax.axis_index("blk").astype(jnp.int32).reshape(1)
    late = lambda i, flag_ref: (0, 1 - flag_ref[0], 0, i)
    return pl.pallas_call(
        mortar_kernel,
        grid_spec=pltpu.PrefetchScalarGridSpec(
            num_scalar_prefetch=1,
            grid=(width // lanes,),
            in_specs=[
                pl.BlockSpec((components, planes, bands, lanes), lambda i, flag_ref: (0, 0, 0, i)),
                pl.BlockSpec((components, 3, bands, lanes), lambda i, flag_ref: (0, 0, 0, i)),
                pl.BlockSpec((components, 1, bands, lanes), lambda i, flag_ref: (0, 0, 0, i)),
                pl.BlockSpec((components, 3, bands, lanes), late),
            ],
            out_specs=pl.BlockSpec((components, 3, bands, lanes), late),
        ),
        out_shape=jax.ShapeDtypeStruct(partial.shape, partial.dtype),
        input_output_aliases={4: 0},
    )(flag, section_state, ghost, edge, partial)


def shards(base_state, section_state, rotor_step):
    planes = section_state.shape[1]
    bands = section_state.shape[2]
    width = section_state.shape[3]
    fraction = (rotor_step[0] % 4).astype(jnp.float32) / 4.0
    early_front = lax.axis_index("blk") == 0
    early_out = jnp.where(early_front, section_state[:, -3:], section_state[:, :3])
    theta_padded = padded_2(hold(section_state, early_out), ((("tx", "tz"), 3),), 3, True)
    radial_raw = padded_2(section_state, (("radial", 2),), 3, False)
    band_index = lax.axis_index("radial")
    band_count = lax.axis_size("radial")
    lower_wall = jnp.where(
        band_index == 0, flip_radial(section_state[:, :, :3]), radial_raw[:, :, :3]
    )
    upper_wall = jnp.where(
        band_index == band_count - 1, flip_radial(section_state[:, :, -3:]), radial_raw[:, :, -3:]
    )
    radial_padded = jnp.concatenate([lower_wall, section_state, upper_wall], axis=2)
    block_index = lax.axis_index("blk")
    front = block_index == 0
    outgoing = early_out
    radial = divergence(radial_padded, 2, bands, 3, 1, 2)
    chosen = pick_column(outgoing, rotor_step, radial)
    theta_padded = hold(theta_padded, chosen)
    azimuthal = divergence(theta_padded, 3, width, 2, 1, 3)
    chosen = pick_row(chosen, rotor_step, azimuthal)
    this_slab, next_slab = cross_blocks(chosen)
    edge_low = jnp.concatenate(
        [section_state[:, :1], section_state[:, :1], section_state[:, :1]], axis=1
    )
    edge_high = jnp.concatenate(
        [section_state[:, -1:], section_state[:, -1:], section_state[:, -1:]], axis=1
    )
    local_window = jnp.where(
        front,
        jnp.concatenate([edge_low, section_state], axis=1),
        jnp.concatenate([section_state, edge_high], axis=1),
    )
    local_window = hold(local_window, chosen)
    local_faces = axial_faces(local_window)
    settled = 0.75 * base_state + 0.25 * (section_state - step_ratio * (radial + azimuthal))
    half = planes // 2
    early = jnp.where(front, settled[:, :half], settled[:, half:]) - 0.25 * step_ratio * (
        local_faces[:, 1:] - local_faces[:, :-1]
    )
    partial = jnp.where(
        front,
        jnp.concatenate([early, settled[:, half:]], axis=1),
        jnp.concatenate([settled[:, :half], early], axis=1),
    )
    edge = jnp.where(front, local_faces[:, -1:], local_faces[:, :1])
    window = window_of(this_slab, next_slab, rotor_step, partial[:, :1, :, :1] + edge[:, :, :1, :1])
    ghost = flip_theta(
        (1.0 - fraction) * window[..., 1 : width + 1] + fraction * window[..., :width]
    )
    return mortar_planes_of(section_state, ghost, edge, partial)


def solution(mesh):
    blocks, slabs, bands = (mesh.shape[name] for name in ("blk", "theta", "radial"))
    rows = 4 if slabs % 4 == 0 else 1
    grid = jax.sharding.Mesh(
        mesh.devices.reshape(blocks, rows, slabs // rows, bands), ("blk", "tx", "tz", "radial")
    )
    in_specs = (P(None, "blk", "radial", ("tx", "tz")), P(None, "blk", "radial", ("tx", "tz")), P())
    out_specs = P(None, "blk", "radial", ("tx", "tz"))
    inner = jax.shard_map(shards, mesh=grid, in_specs=in_specs, out_specs=out_specs, check_vma=False)
    sharded = jax.sharding.NamedSharding(mesh, P(None, "blk", "radial", "theta"))

    def run(base_state, section_state, rotor_step):
        return jax.lax.with_sharding_constraint(
            inner(base_state, section_state, rotor_step), sharded
        )

    return run
```

```python
import jax
import jax.numpy as jnp
from jax import lax
from jax.sharding import PartitionSpec as P
from jax.experimental import pallas as pl
from jax.experimental.pallas import tpu as pltpu

gamma_ratio = 1.4
weno_epsilon = 1e-06
step_ratio = 0.12


def padded_2(cells, sides, width, closed):
    for axis, dim in sides:
        count = lax.axis_size(axis)
        ends = count if closed else count - 1
        head = lax.slice_in_dim(cells, 0, width, axis=dim)
        tail = lax.slice_in_dim(cells, cells.shape[dim] - width, cells.shape[dim], axis=dim)
        cells = jnp.concatenate(
            [
                lax.ppermute(tail, axis, [(i, (i + 1) % count) for i in range(ends)]),
                cells,
                lax.ppermute(head, axis, [((i + 1) % count, i) for i in range(ends)]),
            ],
            axis=dim,
        )
    return cells


def partner(block, axis, distance):
    count = lax.axis_size(axis)
    route = []
    for low in range(count):
        high = low | 1 << distance
        if high != low and high < count:
            route += [(low, high), (high, low)]
    return lax.ppermute(block, axis, route)


def pressure_of(state):
    kinetic = 0.5 * (jnp.square(state[1]) + jnp.square(state[2]) + jnp.square(state[3])) / state[0]
    return (gamma_ratio - 1.0) * (state[4] - kinetic)


def euler_flux(state, normal):
    pressure = pressure_of(state)
    velocity = state[normal] / state[0]
    flux = state * velocity[None]
    flux = flux.at[normal].add(pressure)
    flux = flux.at[4].add(pressure * velocity)
    return flux


def wave_speed(state, normal):
    pressure = pressure_of(state)
    return jnp.abs(state[normal] / state[0]) + jnp.sqrt(gamma_ratio * pressure / state[0])


def weno_side(far_left, left_cell, centre, right_cell, far_right):
    smooth_low = 13.0 / 12.0 * jnp.square(far_left - 2.0 * left_cell + centre) + 0.25 * jnp.square(
        far_left - 4.0 * left_cell + 3.0 * centre
    )
    smooth_mid = 13.0 / 12.0 * jnp.square(
        left_cell - 2.0 * centre + right_cell
    ) + 0.25 * jnp.square(left_cell - right_cell)
    smooth_high = 13.0 / 12.0 * jnp.square(
        centre - 2.0 * right_cell + far_right
    ) + 0.25 * jnp.square(3.0 * centre - 4.0 * right_cell + far_right)
    weight_low = 0.1 / jnp.square(weno_epsilon + smooth_low)
    weight_mid = 0.6 / jnp.square(weno_epsilon + smooth_mid)
    weight_high = 0.3 / jnp.square(weno_epsilon + smooth_high)
    guess_low = (2.0 * far_left - 7.0 * left_cell + 11.0 * centre) / 6.0
    guess_mid = (-left_cell + 5.0 * centre + 2.0 * right_cell) / 6.0
    guess_high = (2.0 * centre + 5.0 * right_cell - far_right) / 6.0
    return (weight_low * guess_low + weight_mid * guess_mid + weight_high * guess_high) / (
        weight_low + weight_mid + weight_high
    )


def face_flux(padded, fluxes, axis, count, normal, first, second):
    states = [
        lax.slice_in_dim(padded, shift_index, shift_index + count + 1, axis=axis)
        for shift_index in range(6)
    ]
    physical = [
        lax.slice_in_dim(fluxes, shift_index, shift_index + count + 1, axis=axis)
        for shift_index in range(6)
    ]
    mean = 0.5 * (states[2] + states[3])
    density = mean[0]
    normal_speed = mean[normal] / density
    speed_first = mean[first] / density
    speed_second = mean[second] / density
    kinetic = 0.5 * (jnp.square(normal_speed) + jnp.square(speed_first) + jnp.square(speed_second))
    pressure = pressure_of(mean)
    sound = jnp.sqrt(gamma_ratio * pressure / density)
    enthalpy = (mean[4] + pressure) / density
    inv_sound = 1.0 / sound
    factor_one = (gamma_ratio - 1.0) * jnp.square(inv_sound)
    factor_two = factor_one * kinetic
    dissipation = jnp.maximum(wave_speed(states[2], normal), wave_speed(states[3], normal))

    def project(vector):
        dens_part = vector[0]
        norm_part = vector[normal]
        first_part = vector[first]
        second_part = vector[second]
        energy_part = vector[4]
        tangent_sum = factor_one * (
            speed_first * first_part + speed_second * second_part - energy_part
        )
        wave_minus = 0.5 * (
            (factor_two + normal_speed * inv_sound) * dens_part
            - (factor_one * normal_speed + inv_sound) * norm_part
            - tangent_sum
        )
        entropy = (
            (1.0 - factor_two) * dens_part + factor_one * normal_speed * norm_part + tangent_sum
        )
        shear_first = first_part - speed_first * dens_part
        shear_second = second_part - speed_second * dens_part
        wave_plus = 0.5 * (
            (factor_two - normal_speed * inv_sound) * dens_part
            - (factor_one * normal_speed - inv_sound) * norm_part
            - tangent_sum
        )
        return (wave_minus, entropy, shear_first, shear_second, wave_plus)

    state_chars = [project(cell_state) for cell_state in states]
    flux_chars = [project(cell_flux) for cell_flux in physical]
    recon = []
    for field_index in range(5):
        plus_vals = [
            0.5 * (flux_chars[cell][field_index] + dissipation * state_chars[cell][field_index])
            for cell in range(6)
        ]
        minus_vals = [
            0.5 * (flux_chars[cell][field_index] - dissipation * state_chars[cell][field_index])
            for cell in range(6)
        ]
        recon.append(
            weno_side(plus_vals[0], plus_vals[1], plus_vals[2], plus_vals[3], plus_vals[4])
            + weno_side(minus_vals[5], minus_vals[4], minus_vals[3], minus_vals[2], minus_vals[1])
        )
    wave_minus, entropy, shear_first, shear_second, wave_plus = recon
    acoustic = wave_minus + entropy + wave_plus
    parts = {}
    parts[0] = acoustic
    parts[normal] = (
        (normal_speed - sound) * wave_minus
        + normal_speed * entropy
        + (normal_speed + sound) * wave_plus
    )
    parts[first] = speed_first * acoustic + shear_first
    parts[second] = speed_second * acoustic + shear_second
    parts[4] = (
        (enthalpy - normal_speed * sound) * wave_minus
        + kinetic * entropy
        + speed_first * shear_first
        + speed_second * shear_second
        + (enthalpy + normal_speed * sound) * wave_plus
    )
    return jnp.stack([parts[index_part] for index_part in range(5)])


def divergence(padded, axis, count, normal, first, second):
    faces = face_flux(padded, euler_flux(padded, normal), axis, count, normal, first, second)
    return lax.slice_in_dim(faces, 1, count + 1, axis=axis) - lax.slice_in_dim(
        faces, 0, count, axis=axis
    )


def flip_radial(cells):
    turned = cells[:, :, ::-1]
    return jnp.concatenate([turned[:3], -turned[3:4], turned[4:]], axis=0)


def flip_theta(cells):
    return jnp.concatenate([cells[:2], -cells[2:3], cells[3:]], axis=0)


def hold(cells, value):
    return jnp.where(jnp.isnan(value.reshape(-1)[0]), jnp.zeros((), cells.dtype), cells)


def after(value, index):
    return index + jnp.isnan(value.reshape(-1)[0]).astype(jnp.int32)


def route_parts(rotor_step, width):
    rows = lax.axis_size("tx")
    columns = lax.axis_size("tz")
    turns = rotor_step[0] // 4 // width
    centre = (turns - 1) % (rows * columns)
    return rows, columns, centre // columns, centre % columns


def pick_column(slab, rotor_step, before):
    rows, columns, centre_row, centre_column = route_parts(rotor_step, slab.shape[3])
    source_column = (centre_column - lax.axis_index("tz")) % columns
    gathered = lax.all_gather(slab, "tz")
    return lax.dynamic_index_in_dim(gathered, after(before, source_column), 0, keepdims=False)[
        ..., ::-1
    ]


def pick_row(slab, rotor_step, before):
    rows, columns, centre_row, centre_column = route_parts(rotor_step, slab.shape[3])
    borrow = (lax.axis_index("tz") > centre_column).astype(jnp.int32)
    source_row = (centre_row - lax.axis_index("tx") - borrow) % rows
    gathered = lax.all_gather(slab, "tx")
    return lax.dynamic_index_in_dim(gathered, after(before, source_row), 0, keepdims=False)


def cross_blocks(slab):
    block_count = lax.axis_size("blk")
    slab_count = lax.axis_size("tx") * lax.axis_size("tz")
    this_route = []
    next_route = []
    for blk_from in range(block_count):
        blk_to = (blk_from + 1) % block_count
        for slab_from in range(slab_count):
            source = blk_from * slab_count + slab_from
            this_route.append((source, blk_to * slab_count + slab_from))
            next_route.append((source, blk_to * slab_count + (slab_from + 1) % slab_count))
    axes = ("blk", "tx", "tz")
    return lax.ppermute(slab, axes, this_route), lax.ppermute(slab, axes, next_route)


def window_of(this_slab, next_slab, rotor_step, before):
    width = this_slab.shape[3]
    remainder = after(before, rotor_step[0] // 4 % width)
    doubled = jnp.concatenate([next_slab, this_slab], axis=3)
    return lax.dynamic_slice_in_dim(doubled, width - 1 - remainder, width + 1, 3)


def axial_kernel(padded_ref, out_ref):
    padded = padded_ref[...]
    count = padded.shape[1] - 6
    pressure = pressure_of(padded)
    velocity = padded[1] / padded[0]
    parts = [padded[index_part] * velocity for index_part in range(5)]
    parts[1] = parts[1] + pressure
    parts[4] = parts[4] + pressure * velocity
    faces = face_flux(padded, jnp.stack(parts), 1, count, 1, 2, 3)
    out_ref[...] = faces


def axial_faces(padded):
    components, planes, bands, width = padded.shape
    lanes = 256
    block = (components, planes, bands, lanes)
    out_block = (components, planes - 5, bands, lanes)
    return pl.pallas_call(
        axial_kernel,
        grid=(width // lanes,),
        in_specs=[pl.BlockSpec(block, lambda i: (0, 0, 0, i))],
        out_specs=pl.BlockSpec(out_block, lambda i: (0, 0, 0, i)),
        out_shape=jax.ShapeDtypeStruct((components, planes - 5, bands, width), padded.dtype),
    )(padded)


def mortar_kernel(flag_ref, section_ref, ghost_ref, edge_ref, partial_ref, out_ref):
    front = flag_ref[0] == 0
    cells = section_ref[...]
    ghost = ghost_ref[...]
    planes = cells.shape[1]
    upper = [cells[:, index] for index in range(1, planes)] + [ghost[:, index] for index in range(3)]
    lower = [ghost[:, index] for index in range(3)] + [cells[:, index] for index in range(planes - 1)]
    padded = jnp.stack([jnp.where(front, a, b) for a, b in zip(upper, lower)], axis=1)
    count = padded.shape[1] - 6
    pressure = pressure_of(padded)
    velocity = padded[1] / padded[0]
    parts = [padded[index_part] * velocity for index_part in range(5)]
    parts[1] = parts[1] + pressure
    parts[4] = parts[4] + pressure * velocity
    faces = face_flux(padded, jnp.stack(parts), 1, count, 1, 2, 3)
    edge = edge_ref[...][:, 0]
    after_front = [faces[:, 0] - edge, faces[:, 1] - faces[:, 0], faces[:, 2] - faces[:, 1]]
    after_aft = [faces[:, 1] - faces[:, 0], faces[:, 2] - faces[:, 1], edge - faces[:, 2]]
    axial = jnp.stack([jnp.where(front, a, b) for a, b in zip(after_front, after_aft)], axis=1)
    out_ref[...] = partial_ref[...] - 0.25 * step_ratio * axial


def mortar_planes_of(section_state, ghost, edge, partial):
    components, planes, bands, width = section_state.shape
    lanes = 512
    flag = lax.axis_index("blk").astype(jnp.int32).reshape(1)
    late = lambda i, flag_ref: (0, 1 - flag_ref[0], 0, i)
    return pl.pallas_call(
        mortar_kernel,
        grid_spec=pltpu.PrefetchScalarGridSpec(
            num_scalar_prefetch=1,
            grid=(width // lanes,),
            in_specs=[
                pl.BlockSpec((components, planes, bands, lanes), lambda i, flag_ref: (0, 0, 0, i)),
                pl.BlockSpec((components, 3, bands, lanes), lambda i, flag_ref: (0, 0, 0, i)),
                pl.BlockSpec((components, 1, bands, lanes), lambda i, flag_ref: (0, 0, 0, i)),
                pl.BlockSpec((components, 3, bands, lanes), late),
            ],
            out_specs=pl.BlockSpec((components, 3, bands, lanes), late),
        ),
        out_shape=jax.ShapeDtypeStruct(partial.shape, partial.dtype),
        input_output_aliases={4: 0},
    )(flag, section_state, ghost, edge, partial)


def shards(base_state, section_state, rotor_step):
    planes = section_state.shape[1]
    bands = section_state.shape[2]
    width = section_state.shape[3]
    fraction = (rotor_step[0] % 4).astype(jnp.float32) / 4.0
    theta_padded = padded_2(section_state, ((("tx", "tz"), 3),), 3, True)
    radial_raw = padded_2(section_state, (("radial", 2),), 3, False)
    band_index = lax.axis_index("radial")
    band_count = lax.axis_size("radial")
    lower_wall = jnp.where(
        band_index == 0, flip_radial(section_state[:, :, :3]), radial_raw[:, :, :3]
    )
    upper_wall = jnp.where(
        band_index == band_count - 1, flip_radial(section_state[:, :, -3:]), radial_raw[:, :, -3:]
    )
    radial_padded = jnp.concatenate([lower_wall, section_state, upper_wall], axis=2)
    block_index = lax.axis_index("blk")
    front = block_index == 0
    outgoing = jnp.where(front, section_state[:, -3:], section_state[:, :3])
    radial = divergence(radial_padded, 2, bands, 3, 1, 2)
    chosen = pick_column(outgoing, rotor_step, radial)
    theta_padded = hold(theta_padded, chosen)
    azimuthal = divergence(theta_padded, 3, width, 2, 1, 3)
    chosen = pick_row(chosen, rotor_step, azimuthal)
    this_slab, next_slab = cross_blocks(chosen)
    edge_low = jnp.concatenate(
        [section_state[:, :1], section_state[:, :1], section_state[:, :1]], axis=1
    )
    edge_high = jnp.concatenate(
        [section_state[:, -1:], section_state[:, -1:], section_state[:, -1:]], axis=1
    )
    local_window = jnp.where(
        front,
        jnp.concatenate([edge_low, section_state], axis=1),
        jnp.concatenate([section_state, edge_high], axis=1),
    )
    local_window = hold(local_window, chosen)
    local_faces = axial_faces(local_window)
    settled = 0.75 * base_state + 0.25 * (section_state - step_ratio * (radial + azimuthal))
    half = planes // 2
    early = jnp.where(front, settled[:, :half], settled[:, half:]) - 0.25 * step_ratio * (
        local_faces[:, 1:] - local_faces[:, :-1]
    )
    partial = jnp.where(
        front,
        jnp.concatenate([early, settled[:, half:]], axis=1),
        jnp.concatenate([settled[:, :half], early], axis=1),
    )
    edge = jnp.where(front, local_faces[:, -1:], local_faces[:, :1])
    window = window_of(this_slab, next_slab, rotor_step, partial[:, :1, :, :1] + edge[:, :, :1, :1])
    ghost = flip_theta(
        (1.0 - fraction) * window[..., 1 : width + 1] + fraction * window[..., :width]
    )
    return mortar_planes_of(section_state, ghost, edge, partial)


def solution(mesh):
    blocks, slabs, bands = (mesh.shape[name] for name in ("blk", "theta", "radial"))
    rows = 4 if slabs % 4 == 0 else 1
    grid = jax.sharding.Mesh(
        mesh.devices.reshape(blocks, rows, slabs // rows, bands), ("blk", "tx", "tz", "radial")
    )
    in_specs = (P(None, "blk", "radial", ("tx", "tz")), P(None, "blk", "radial", ("tx", "tz")), P())
    out_specs = P(None, "blk", "radial", ("tx", "tz"))
    inner = jax.shard_map(shards, mesh=grid, in_specs=in_specs, out_specs=out_specs, check_vma=False)
    sharded = jax.sharding.NamedSharding(mesh, P(None, "blk", "radial", "theta"))

    def run(base_state, section_state, rotor_step):
        return jax.lax.with_sharding_constraint(
            inner(base_state, section_state, rotor_step), sharded
        )

    return run
```
